256 devices in a mesh: heads: 8 (over x, core), ctx: 32 (over z, y).
Axes of the slice: x: 4, y: 4, z: 8, core: 2. Of those that a mesh axis runs over, the one named last changes fastest.
Arguments:
- tokens: bfloat16 [32, 2048, 1024], P('ctx', 'heads'), may hold values from -3 to 3
- ln_gain: float32 [1024], replicated, may hold values from 0.25 to 1.75
- w_qkv: bfloat16 [1024, 3, 1024], P(None, None, 'heads'), may hold values from -4 to 4
- w_out: bfloat16 [1024, 1024], replicated, may hold values from -0.1875 to 0.1875
- neighbours: int32 [32, 16, 8], P('ctx'), may hold values from 0 to 19, as said below
- counts: int32 [32, 16], P('ctx'), may hold values from 1 to 8, as said below
- latents: bfloat16 [512, 1024], replicated, may hold values from -3 to 3
- lat_gain: float32 [1024], replicated, may hold values from 0.25 to 1.75
- w_lat_q: bfloat16 [1024, 1024], P(None, 'heads'), may hold values from -0.75 to 0.75
- w_lat_o: bfloat16 [1024, 1024], P('heads'), may hold values from -0.1875 to 0.1875
- mlp_gain: float32 [1024], replicated, may hold values from 0.25 to 1.75
- w_up: bfloat16 [1024, 4096], P(None, 'ctx'), may hold values from -0.1875 to 0.1875
- w_down: bfloat16 [4096, 1024], P('ctx'), may hold values from -0.09375 to 0.09375
Outputs:
- tokens_out: bfloat16 [32, 2048, 1024], P('ctx', 'heads')
- latents_out: bfloat16 [512, 1024], P('heads')
The draws below stay inside these ranges and needn't reach their ends.
Inputs may be any that keep to these rules, and one draw needn't show every extreme that they name: `neighbours`: in group g, widened index 2 + j is the group's block j, indices below 2 are the previous group's last 2 blocks, indices of 18 and above the next group's first 2. Each entry lies within 2 blocks of the query block's own, never outside the cloud; entries may repeat; slots at or after the count are padding but hold valid indices. In a group with a previous group, slot 0 of block j < 2 is widened block j; in a group with a next group, slot 0 of block 14 + j is widened block 18 + j. `counts`: some list is full in every draw.
All inputs are finite; a program needn't handle non-finite values.
Results may differ from the reference program's by a relative error of at most 0.014.
The reference program's roundings to bfloat16 on the way count: a program that leaves them out, or rounds other values in their place, can miss the bound.
Values may be sent and summed in bfloat16 or wider, within the bound.
A program may use at most 128 MiB of HBM per device.

```python
import math
import jax
import jax.numpy as jnp
from jax import lax

D = 1024
HEADS = 16
HD = 64
LAT = 512
MLPH = 4096
BLK = 128
MAXNB = 8
HB = 2
GROUPS = 32
GTOK = 2048
GBLK = 16


def pattern_tables(key):
    base = jax.random.fold_in(key, 7)
    key_pick, key_level, key_live, key_full = jax.random.split(base, 4)
    group = jnp.arange(GROUPS, dtype=jnp.int32)[:, None]
    block = jnp.arange(GBLK, dtype=jnp.int32)[None, :]
    lowest = jnp.where(group == 0, HB, 0)
    highest = jnp.where(group == GROUPS - 1, GBLK + HB, GBLK + 2 * HB)
    start = jnp.maximum(block, lowest)
    stop = jnp.minimum(block + 2 * HB + 1, highest)
    raw = jax.random.randint(key_pick, (GROUPS, GBLK, MAXNB), 0, 1 << 20)
    lists = start[..., None] + raw % (stop - start)[..., None]
    first = jnp.where(block < HB, start, jnp.where(block >= GBLK - HB, stop - 1, lists[:, :, 0]))
    lists = jnp.concatenate([first[..., None], lists[:, :, 1:]], axis=2)
    level = jax.random.randint(key_level, (GROUPS, 1), 1, MAXNB + 1)
    live = 1 + jax.random.randint(key_live, (GROUPS, GBLK), 0, 1 << 20) % level
    chosen = jax.random.randint(key_full, (), 0, GROUPS * GBLK)
    flat = jnp.arange(GROUPS * GBLK, dtype=jnp.int32).reshape(GROUPS, GBLK)
    live = jnp.where(flat == chosen, MAXNB, live)
    return (lists.astype(jnp.int32), live.astype(jnp.int32))


def draw_neighbours(key, part):
    return pattern_tables(key)[0]


def draw_counts(key, part):
    return pattern_tables(key)[1]


def draw_w_qkv(key, part):
    key_base = jax.random.fold_in(jax.random.fold_in(key, 11), 0)
    shape = (D, 3, HEADS * HD)
    scale = D ** (-0.5)
    base = jnp.clip(jax.random.normal(key_base, shape, jnp.float32), -6.0, 6.0) * scale
    return base.astype(jnp.bfloat16)


def levels(key, shape, pieces, low, largest):
    def one(dim, blocks):
        steps = jax.random.uniform(jax.random.fold_in(jax.random.fold_in(key, 6), dim), (blocks,), jnp.float32, low / len(pieces), largest / len(pieces))
        return jnp.repeat(jnp.exp(steps), shape[dim] // blocks).reshape((-1,) + (1,) * (len(shape) - dim - 1))

    loudness = one(*pieces[0])
    for cut in pieces[1:]:
        loudness = loudness * one(*cut)
    return loudness


def scatter_about(own_key, extent, scale, most, shards=(), held_as=jnp.bfloat16):
    drawn = jax.random.normal(own_key, extent, jnp.float32) * scale
    if len(shards) > 0:
        drawn = levels(own_key, extent, shards, -0.22, 0.18) * drawn
    return jnp.clip(drawn, min=-most, max=most).astype(held_as)


def setup_inputs(seed: int = 0) -> dict:
    splits = jax.random.split(jax.random.key(seed), 14)
    tokens = scatter_about(splits[0], (GROUPS, GTOK, D), 0.5, 3.0, ((0, 32), (1, 8)))
    ln_gain = jnp.clip(1.0 + 0.15 * jax.random.normal(splits[1], (D,), jnp.float32), 0.25, 1.75)
    w_qkv = draw_w_qkv(jax.random.fold_in(splits[13], 71), 0)
    w_out = scatter_about(splits[3], (HEADS * HD, D), (HEADS * HD) ** -0.5, 0.1875)
    neighbours = draw_neighbours(jax.random.fold_in(splits[13], 71), 0)
    counts = draw_counts(jax.random.fold_in(splits[13], 71), 0)
    latents = scatter_about(splits[6], (LAT, D), 0.5, 3.0)
    lat_gain = jnp.clip(1.0 + 0.15 * jax.random.normal(splits[7], (D,), jnp.float32), 0.25, 1.75)
    w_lat_q = scatter_about(splits[8], (D, HEADS * HD), (D // 16) ** -0.5, 0.75, ((1, 8),))
    w_lat_o = scatter_about(splits[9], (HEADS * HD, D), (HEADS * HD) ** -0.5, 0.1875, ((0, 8),))
    mlp_gain = jnp.clip(1.0 + 0.15 * jax.random.normal(splits[10], (D,), jnp.float32), 0.25, 1.75)
    w_up = scatter_about(splits[11], (D, MLPH), D ** -0.5, 0.1875, ((1, 32),))
    w_down = scatter_about(splits[12], (MLPH, D), MLPH ** -0.5, 0.09375, ((0, 32),))
    return {"tokens": tokens, "ln_gain": ln_gain, "w_qkv": w_qkv, "w_out": w_out, "neighbours": neighbours, "counts": counts, "latents": latents, "lat_gain": lat_gain, "w_lat_q": w_lat_q, "w_lat_o": w_lat_o, "mlp_gain": mlp_gain, "w_up": w_up, "w_down": w_down}


EPSILON = 1e-05

def layer_norm(values, gain):
    floats = values.astype(jnp.float32)
    center = lax.optimization_barrier(jnp.mean(floats, axis=-1, keepdims=True))
    spread = lax.optimization_barrier(jnp.mean(jnp.square(floats - center), axis=-1, keepdims=True))
    return (floats - center) * lax.rsqrt(spread + EPSILON) * gain.astype(jnp.float32)

def block_attention(queries, extended, lists, live):
    nblocks = queries.shape[0] // BLK
    heads = queries.shape[1]
    step = math.gcd(nblocks, max(1, 512 // BLK))
    query_blocks = queries.reshape(nblocks // step, step, BLK, heads, HD)
    key_blocks = extended.reshape(-1, BLK, 2, heads, HD)

    def one_step(args):
        block_q, index, count = args
        picked = jnp.take(key_blocks, index, axis=0)
        keys_f = picked[:, :, :, 0].astype(jnp.float32)
        vals_f = picked[:, :, :, 1].astype(jnp.float32)
        scores = jnp.einsum('bqhd,bskhd->bhqsk', block_q.astype(jnp.float32), keys_f) * HD ** (-0.5)
        valid = (jnp.arange(index.shape[1], dtype=jnp.int32)[None, :] < count[:, None])[:, None, None, :, None]
        scores = jnp.where(valid, scores, -jnp.inf)
        top = lax.optimization_barrier(jnp.max(scores, axis=(3, 4), keepdims=True))
        weights = jnp.exp(scores - top)
        total = lax.optimization_barrier(jnp.sum(weights, axis=(3, 4)))
        rounded = lax.optimization_barrier(weights.astype(jnp.bfloat16)).astype(jnp.float32)
        mixed = jnp.einsum('bhqsk,bskhd->bqhd', rounded, vals_f)
        mixed = mixed / jnp.transpose(total, (0, 2, 1))[..., None]
        return mixed.astype(jnp.bfloat16)
    result = lax.map(one_step, (query_blocks, lists.reshape(nblocks // step, step, -1), live.reshape(nblocks // step, step)))
    return result.reshape(nblocks * BLK, heads * HD)

def reference(tokens, ln_gain, w_qkv, w_out, neighbours, counts, latents, lat_gain, w_lat_q, w_lat_o, mlp_gain, w_up, w_down):
    group_tok = tokens.shape[1]
    rim = HB * BLK
    w_flat = w_qkv.reshape(D, 3 * HEADS * HD)

    def project(rows):
        normed = layer_norm(rows, ln_gain).astype(jnp.bfloat16)
        made = jnp.dot(normed, w_flat, preferred_element_type=jnp.float32).astype(jnp.bfloat16)
        return made.reshape(group_tok, 3, HEADS, HD)
    qkv = lax.map(project, tokens)
    pairs = qkv[:, :, 1:]
    blank = jnp.zeros((1, rim) + pairs.shape[2:], jnp.bfloat16)
    before = jnp.concatenate([blank, pairs[:-1, group_tok - rim:]], axis=0)
    after = jnp.concatenate([pairs[1:, :rim], blank], axis=0)
    extended = jnp.concatenate([before, pairs, after], axis=1)

    def attend(args):
        queries, widened, lists, live = args
        return block_attention(queries, widened, lists, live)
    attended = lax.map(attend, (qkv[:, :, 0], extended, neighbours, counts))

    def finish(args):
        rows, mixed = args
        return (rows.astype(jnp.float32) + jnp.dot(mixed, w_out, preferred_element_type=jnp.float32)).astype(jnp.bfloat16)
    tokens_out = lax.map(finish, (tokens, attended))
    lat_norm = layer_norm(latents, lat_gain).astype(jnp.bfloat16)
    lat_q = jnp.dot(lat_norm, w_lat_q, preferred_element_type=jnp.float32).astype(jnp.bfloat16)
    all_keys = qkv[:, :, 1].reshape(-1, HEADS, HD).transpose(1, 0, 2)
    all_vals = qkv[:, :, 2].reshape(-1, HEADS, HD).transpose(1, 0, 2)

    def head_attend(args):
        query, key, value = args
        scores = jnp.dot(query.astype(jnp.float32), key.astype(jnp.float32).T, precision=lax.Precision.HIGHEST) * HD ** (-0.5)
        top = lax.optimization_barrier(jnp.max(scores, axis=-1, keepdims=True))
        weights = jnp.exp(scores - top)
        total = lax.optimization_barrier(jnp.sum(weights, axis=-1, keepdims=True))
        rounded = lax.optimization_barrier(weights.astype(jnp.bfloat16)).astype(jnp.float32)
        return jnp.dot(rounded, value.astype(jnp.float32), precision=lax.Precision.HIGHEST) / total
    per_head = lax.map(head_attend, (lat_q.reshape(LAT, HEADS, HD).transpose(1, 0, 2), all_keys, all_vals))
    lat_att = per_head.transpose(1, 0, 2).reshape(LAT, HEADS * HD).astype(jnp.bfloat16)
    hidden_lat = latents.astype(jnp.float32) + jnp.dot(lat_att, w_lat_o, preferred_element_type=jnp.float32)
    mlp_in = layer_norm(hidden_lat, mlp_gain).astype(jnp.bfloat16)
    inner = jax.nn.gelu(jnp.dot(mlp_in, w_up, preferred_element_type=jnp.float32), approximate=True).astype(jnp.bfloat16)
    latents_out = (hidden_lat + jnp.dot(inner, w_down, preferred_element_type=jnp.float32)).astype(jnp.bfloat16)
    return (tokens_out, latents_out)
```

```python
import functools

import jax
import jax.numpy as jnp
from jax import lax
from jax.experimental import pallas as pl
from jax.experimental.pallas import tpu as pltpu
from jax.sharding import PartitionSpec as P

HD = 64
BLK = 128
WIN = 5
RIM = 256
EPSILON = 1e-05
SCALE2 = HD ** (-0.5) * 1.4426950408889634
MESH = pl.DeviceIdType.MESH
BF = jnp.bfloat16
F32 = jnp.float32


def aligned(start, by):
    return pl.multiple_of(start, by)


def normalise(rows, gain):
    center = jnp.mean(rows, axis=-1, keepdims=True)
    spread = jnp.mean(jnp.square(rows - center), axis=-1, keepdims=True)
    return (rows - center) * lax.rsqrt(spread + EPSILON) * gain


def kernel(
    nh,
    nc,
    tok_hbm,
    lng_ref,
    wqkv_hbm,
    wout_hbm,
    nb_ref,
    cnt_ref,
    lat_hbm,
    latg_ref,
    wlq_hbm,
    wlo_hbm,
    mg_ref,
    wup_hbm,
    wdn_hbm,
    tout_ref,
    lout_ref,
    tok,
    wqkv,
    wout,
    lat,
    wlq,
    wlo,
    wup,
    wdn,
    G,
    latn,
    Q,
    KV,
    kst,
    vst,
    fA,
    fB,
    f2,
    qlat,
    om,
    mm,
    hl,
    multr,
    biasr,
    r1s,
    r1t,
    r1r,
    r1u,
    r2s,
    r2r,
    r3s,
    r3r,
    r4s,
    r4r,
    r5s,
    r5r,
    A,
    R,
    in_sem,
    gs,
    gr,
    xs,
    xr,
):
    h = lax.axis_index("heads")
    c = lax.axis_index("ctx")
    x = h // 2
    k = h % 2
    nrow = tok.shape[0]
    half = nrow // 2
    nlat = lat.shape[0]
    dw = tok.shape[1]
    nk = dw // 128
    gtok = nh * nrow
    nblk = gtok // BLK
    per = nlat // nc

    loads = [
        pltpu.make_async_copy(tok_hbm, tok, in_sem.at[0]),
        pltpu.make_async_copy(lat_hbm, lat, in_sem.at[1]),
        pltpu.make_async_copy(wlq_hbm, wlq, in_sem.at[2]),
        pltpu.make_async_copy(wqkv_hbm.at[0], wqkv.at[:, pl.ds(0, 128)], in_sem.at[3]),
        pltpu.make_async_copy(wqkv_hbm.at[1], wqkv.at[:, pl.ds(128, 128)], in_sem.at[4]),
        pltpu.make_async_copy(wqkv_hbm.at[2], wqkv.at[:, pl.ds(256, 128)], in_sem.at[5]),
        pltpu.make_async_copy(wlo_hbm, wlo, in_sem.at[6]),
        pltpu.make_async_copy(wup_hbm, wup, in_sem.at[7]),
        pltpu.make_async_copy(wdn_hbm, wdn, in_sem.at[8]),
        pltpu.make_async_copy(wout_hbm, wout, in_sem.at[9]),
    ]
    for load in loads:
        load.start()

    barrier = pltpu.get_barrier_semaphore()

    def hello_h(d, carry):
        pl.semaphore_signal(
            barrier, inc=1, device_id={"heads": lax.rem(h + d, nh)}, device_id_type=MESH
        )
        return carry

    def hello_c(d, carry):
        pl.semaphore_signal(
            barrier, inc=1, device_id={"ctx": lax.rem(c + d, nc)}, device_id_type=MESH
        )
        return carry

    lax.fori_loop(1, nh, hello_h, 0)
    lax.fori_loop(1, nc, hello_c, 0)

    loads[0].wait()
    mine = aligned(h * nrow, 256)
    step = 32

    def norm_tokens(i, carry):
        at = pl.ds(aligned(i * step, step), step)
        G[pl.ds(aligned(mine + i * step, step), step), :] = normalise(
            tok[at, :].astype(F32), lng_ref[...]
        ).astype(BF)
        return carry

    lax.fori_loop(0, nrow // step, norm_tokens, 0)
    pl.semaphore_wait(barrier, nh + nc - 2)

    sib = x * 2 + (1 - k)
    right = lax.rem(x + 1, nh // 2) * 2 + k
    left = lax.rem(x + nh // 2 - 1, nh // 2) * 2 + k
    far = lax.rem(x + 2, nh // 2) * 2 + k
    right_s = lax.rem(x + 1, nh // 2) * 2 + (1 - k)
    left_s = lax.rem(x + nh // 2 - 1, nh // 2) * 2 + (1 - k)
    far_s = lax.rem(x + 2, nh // 2) * 2 + (1 - k)

    def piece(block, part):
        return aligned(block * nrow + part * half, 128)

    def move(at, size, sem, to):
        rows = pl.ds(at, size)
        return pltpu.make_async_remote_copy(
            src_ref=G.at[rows, :],
            dst_ref=G.at[rows, :],
            send_sem=gs.at[sem],
            recv_sem=gr.at[sem],
            device_id={"heads": to},
            device_id_type=MESH,
        )

    sends = [
        move(piece(h, 0), half, 1, right),
        move(piece(h, 1), half, 3, left),
        move(mine, nrow, 0, sib),
        move(piece(h, 1), half, 2, right),
        move(piece(h, 0), half, 4, left),
    ]
    for send in sends:
        send.start()

    loads[1].wait()

    def norm_latents(i, carry):
        at = pl.ds(aligned(i * step, step), step)
        latn[at, :] = normalise(lat[at, :].astype(F32), latg_ref[...]).astype(BF)
        return carry

    lax.fori_loop(0, nlat // step, norm_latents, 0)
    loads[2].wait()
    fA[...] = jnp.dot(latn[...], wlq[...], preferred_element_type=F32)
    share = nlat // nh
    two = share // nc
    for hh in range(nh):
        for i in range(two):
            fB[pl.ds(hh * two + i, nc, stride=per), :] = fA[
                pl.ds(hh * share + i, nc, stride=two), :
            ]
    lane = lax.broadcasted_iota(jnp.int32, (nlat, 128), 1)
    lq = fB[...]
    qlat[pl.ds(0, nlat), :] = jnp.where(lane < HD, lq, 0.0).astype(BF)
    qlat[pl.ds(nlat, nlat), :] = jnp.where(lane < HD, 0.0, lq).astype(BF)
    om[...] = jnp.zeros_like(om)
    mm[...] = jnp.full_like(mm, -jnp.inf)

    own64 = lat[pl.ds(aligned(h * share, share), share), :].astype(F32)
    for j in range(nk):
        fA[pl.ds(j, share, stride=nk), :] = own64[:, j * 128 : (j + 1) * 128]
    hl[...] = fA[pl.ds(aligned(c * two * nk, two * nk), two * nk), :]

    slot = lax.broadcasted_iota(jnp.int32, nb_ref.shape, 0)
    column = lax.broadcasted_iota(jnp.int32, nb_ref.shape, 1)
    live = slot < cnt_ref[...]
    eye = lax.broadcasted_iota(jnp.int32, (nblk, nblk), 0) == lax.broadcasted_iota(
        jnp.int32, (nblk, nblk), 1
    )
    for j in range(WIN):
        hits = jnp.where(live & (nb_ref[...] == column + j), 1.0, 0.0)
        times = jnp.sum(hits, axis=0, keepdims=True)
        times = jnp.sum(jnp.where(eye, times, 0.0), axis=1, keepdims=True)
        times = jnp.broadcast_to(times, (nblk, 128))
        multr[j] = times
        biasr[j] = jnp.where(times > 0.0, 0.0, -jnp.inf)

    keys = kst.shape[0]
    tile = 256

    def project(starts):
        rows = jnp.concatenate([G[pl.ds(s, half), :] for s in starts], axis=0)
        made = jnp.dot(rows, wqkv[...], preferred_element_type=F32)
        first = lax.broadcasted_iota(jnp.int32, (half, 128), 1) < HD
        for i, s in enumerate(starts):
            part = slice(i * half, (i + 1) * half)
            q = made[part, 0:128]
            key = made[part, 128:256].astype(BF)
            v = made[part, 256:384]
            v0 = jnp.where(first, v, 1.0).astype(BF)
            v1 = jnp.where(first, 1.0, v).astype(BF)
            Q[0, pl.ds(s, half), :] = jnp.where(first, q, 0.0).astype(BF)
            Q[1, pl.ds(s, half), :] = jnp.where(first, 0.0, q).astype(BF)
            wide = pl.ds(aligned(s + RIM, 128), half)
            KV[0, wide, :] = key
            KV[1, wide, :] = v0
            KV[2, wide, :] = v1
            kst[part, :] = key
            vst[0, part, :] = v0
            vst[1, part, :] = v1

    def cross(t, carry):
        at = pl.ds(aligned(t * tile, tile), tile)
        s = lax.dot_general(
            qlat[at, :], kst[...], (((1,), (1,)), ((), ())), preferred_element_type=F32
        )
        before = mm[at, :]
        top = jnp.maximum(before, jnp.max(s, axis=1, keepdims=True))
        alpha = jnp.exp2((before - top) * SCALE2)
        p = jnp.concatenate(
            [
                jnp.exp2((s[:, j * 128 : (j + 1) * 128] - top) * SCALE2).astype(BF)
                for j in range(keys // 128)
            ],
            axis=1,
        )
        mm[at, :] = top
        om[at, :] = om[at, :] * alpha + jnp.dot(
            p, vst[t * tile // nlat], preferred_element_type=F32
        )
        return carry

    def stage(starts):
        project(starts)
        lax.fori_loop(0, 2 * nlat // tile, cross, 0)

    for i in (3, 4, 5):
        loads[i].wait()
    move(piece(sib, 0), nrow, 0, sib).wait_recv()
    stage([piece(h, 0), piece(h, 1), piece(sib, 0), piece(sib, 1)])

    move(piece(left, 0), half, 1, right).wait_recv()
    passed = [move(piece(left, 0), half, 5, right), move(piece(left, 0), half, 7, sib)]
    move(piece(right, 1), half, 3, left).wait_recv()
    passed += [move(piece(right, 1), half, 6, left), move(piece(right, 1), half, 8, sib)]
    for send in passed:
        send.start()
    sends += passed
    move(piece(left_s, 0), half, 7, sib).wait_recv()
    move(piece(right_s, 1), half, 8, sib).wait_recv()
    stage([piece(left, 0), piece(right, 1), piece(left_s, 0), piece(right_s, 1)])

    move(piece(left, 1), half, 2, right).wait_recv()
    move(piece(right, 0), half, 4, left).wait_recv()
    passed = [move(piece(left, 1), half, 9, sib), move(piece(right, 0), half, 10, sib)]
    for send in passed:
        send.start()
    sends += passed
    move(piece(left_s, 1), half, 9, sib).wait_recv()
    move(piece(right_s, 0), half, 10, sib).wait_recv()
    stage([piece(left, 1), piece(right, 0), piece(left_s, 1), piece(right_s, 0)])

    move(piece(far, 0), half, 5, right).wait_recv()
    move(piece(far, 1), half, 6, left).wait_recv()
    passed = [move(piece(far, 0), half, 11, sib), move(piece(far, 1), half, 12, sib)]
    for send in passed:
        send.start()
    sends += passed
    move(piece(far_s, 0), half, 11, sib).wait_recv()
    move(piece(far_s, 1), half, 12, sib).wait_recv()
    stage([piece(far, 0), piece(far, 1), piece(far_s, 0), piece(far_s, 1)])

    tile1 = 128
    lane1 = lax.broadcasted_iota(jnp.int32, (tile1, 128), 1)
    row1 = lax.broadcasted_iota(jnp.int32, (tile1, 128), 0)
    first1 = lane1 < HD
    pick1 = lax.rem(lane1, HD) == lax.rem(row1, per)
    for t in range(nlat // tile1):
        at0 = pl.ds(t * tile1, tile1)
        at1 = pl.ds(nlat + t * tile1, tile1)
        o0, o1 = om[at0, :], om[at1, :]
        total = pltpu.roll(jnp.where(first1, o1, o0), HD, 1)
        r1s[at0, :] = (jnp.where(first1, o0, o1) / total).astype(BF)
        lse = jnp.where(first1, mm[at0, :], mm[at1, :]) * SCALE2 + jnp.log2(total)
        lse = jnp.where(pick1, lse, 0.0)
        for g in range(tile1 // per):
            r1t[t * (tile1 // per) + g] = jnp.sum(
                lse[g * per : (g + 1) * per, :], axis=0, keepdims=True
            )

    own_c = pl.ds(aligned(c * per, 16), per)

    def to_ctx(src, dst, s, r):
        def body(d, carry):
            to = lax.rem(c + d, nc)
            pltpu.make_async_remote_copy(
                src_ref=src(to),
                dst_ref=dst,
                send_sem=xs.at[s],
                recv_sem=xr.at[r],
                device_id={"ctx": to},
                device_id_type=MESH,
            ).start()
            return carry

        lax.fori_loop(1, nc, body, 0)

    def spread(i, src, dst):
        to_ctx(lambda to: src.at[pl.ds(aligned(to * per, 16), per), :], dst.at[own_c, :], i, i)

    def await_bytes(ref, sem):
        pltpu.make_async_copy(ref, ref, sem).wait()

    rest = pl.ds(0, (nc - 1) * per)
    to_ctx(lambda to: r1t.at[to], r1u.at[c], 1, 1)
    spread(0, r1s, r1r)
    r1r[own_c, :] = r1s[own_c, :]
    r1u[c] = r1t[c]

    def rim(src, dst, sem, to):
        return pltpu.make_async_remote_copy(
            src_ref=KV.at[:, pl.ds(src, RIM), :],
            dst_ref=KV.at[:, pl.ds(dst, RIM), :],
            send_sem=xs.at[sem],
            recv_sem=xr.at[sem],
            device_id={"ctx": to},
            device_id_type=MESH,
        )

    rims = [
        rim(RIM, RIM + gtok, 2, lax.rem(c + nc - 1, nc)),
        rim(gtok, 0, 3, lax.rem(c + 1, nc)),
    ]
    for r in rims:
        r.start()

    firstb = lax.broadcasted_iota(jnp.int32, (BLK, 128), 1) < HD

    def attend(b, carry):
        at = pl.ds(aligned(b * BLK, BLK), BLK)
        win = pl.ds(aligned(b * BLK, BLK), WIN * BLK)
        q = jnp.concatenate([Q[0, at, :], Q[1, at, :]], axis=0)
        s = lax.dot_general(
            q, KV[0, win, :], (((1,), (1,)), ((), ())), preferred_element_type=F32
        )
        parts = [
            s[:, j * BLK : (j + 1) * BLK] + biasr[j, pl.ds(b, 1), :] for j in range(WIN)
        ]
        top = parts[0]
        for part in parts[1:]:
            top = jnp.maximum(top, part)
        top = jnp.max(top, axis=1, keepdims=True)
        p = jnp.concatenate(
            [
                (jnp.exp2((part - top) * SCALE2) * multr[j, pl.ds(b, 1), :]).astype(BF)
                for j, part in enumerate(parts)
            ],
            axis=1,
        )
        o0 = jnp.dot(p[:BLK], KV[1, win, :], preferred_element_type=F32)
        o1 = jnp.dot(p[BLK:], KV[2, win, :], preferred_element_type=F32)
        total = pltpu.roll(jnp.where(firstb, o1, o0), HD, 1)
        A[at, :] = (jnp.where(firstb, o0, o1) / total).astype(BF)
        return carry

    lax.fori_loop(2, nblk - 2, attend, 0)

    await_bytes(r1r.at[rest, :], xr.at[0])
    await_bytes(r1u.at[pl.ds(0, nc - 1)], xr.at[1])
    lanes = lax.broadcasted_iota(jnp.int32, (per, 128), 1)
    pick = lax.rem(lanes, HD) == lax.broadcasted_iota(jnp.int32, (per, 128), 0)
    for i in range(nc):
        fA[pl.ds(i * per, per), :] = jnp.where(pick, r1u[i], 0.0)
    same = (
        lax.broadcasted_iota(jnp.int32, (128, 128), 0) // HD
        == lax.broadcasted_iota(jnp.int32, (128, 128), 1) // HD
    )
    fB[...] = jnp.dot(
        fA[...],
        jnp.where(same, 1.0, 0.0),
        preferred_element_type=F32,
        precision=lax.Precision.HIGHEST,
    )
    peak = fB[pl.ds(0, per), :]
    for i in range(1, nc):
        peak = jnp.maximum(peak, fB[pl.ds(i * per, per), :])
    weight = jnp.zeros((per, 128), F32)
    value = jnp.zeros((per, 128), F32)
    for i in range(nc):
        w = jnp.exp2(fB[pl.ds(i * per, per), :] - peak)
        weight += w
        value += w * r1r[pl.ds(i * per, per), :].astype(F32)
    lat_att = (value / weight).astype(BF)

    loads[6].wait()
    made = jnp.dot(lat_att, wlo[...], preferred_element_type=F32)
    for j in range(nk):
        r2s[pl.ds(j, per, stride=nk), :] = made[:, j * 128 : (j + 1) * 128]
    own_h = pl.ds(aligned(h * two * nk, 16), two * nk)

    def send2(d, carry):
        to = lax.rem(h + d, nh)
        pltpu.make_async_remote_copy(
            src_ref=r2s.at[pl.ds(aligned(to * two * nk, 16), two * nk), :],
            dst_ref=r2r.at[own_h, :],
            send_sem=xs.at[4],
            recv_sem=xr.at[4],
            device_id={"heads": to},
            device_id_type=MESH,
        ).start()
        return carry

    lax.fori_loop(1, nh, send2, 0)
    r2r[own_h, :] = r2s[own_h, :]

    for r in rims:
        r.wait_recv()
    lax.fori_loop(0, 2, attend, 0)
    lax.fori_loop(nblk - 2, nblk, attend, 0)

    rest2 = pl.ds(0, (nh - 1) * two * nk)
    await_bytes(r2r.at[rest2, :], xr.at[4])
    hidden = hl[...]
    for i in range(nh):
        hidden += r2r[pl.ds(i * two * nk, two * nk), :]
    hl[...] = hidden
    for i in range(two):
        row = hidden[i * nk : (i + 1) * nk, :]
        center = jnp.sum(jnp.sum(row, axis=0, keepdims=True), axis=1, keepdims=True) / dw
        off = row - center
        spread2 = (
            jnp.sum(jnp.sum(jnp.square(off), axis=0, keepdims=True), axis=1, keepdims=True) / dw
        )
        f2[pl.ds(i * nk, nk), :] = off * lax.rsqrt(spread2 + EPSILON) * mg_ref[...]
    r3s[...] = f2[...].astype(BF)
    to_ctx(lambda to: r3s, r3r.at[own_c, :], 5, 5)
    r3r[own_c, :] = r3s[...]

    head_cols = pl.ds(aligned(h * 128, 128), 128)

    def send_back(d, carry):
        to = lax.rem(h + d, nh)
        pltpu.make_async_remote_copy(
            src_ref=A.at[pl.ds(aligned(to * nrow, 128), nrow), :],
            dst_ref=R.at[:, head_cols],
            send_sem=xs.at[6],
            recv_sem=xr.at[6],
            device_id={"heads": to},
            device_id_type=MESH,
        ).start()
        return carry

    lax.fori_loop(1, nh, send_back, 0)
    R[:, head_cols] = A[pl.ds(mine, nrow), :]

    loads[7].wait()
    loads[8].wait()
    await_bytes(r3r.at[rest, :], xr.at[5])
    fA[...] = r3r[...].astype(F32)
    rows = jnp.concatenate(
        [fA[pl.ds(j, share, stride=nk), :].astype(BF) for j in range(nk)], axis=1
    )
    inner = jax.nn.gelu(
        jnp.dot(rows, wup[...], preferred_element_type=F32), approximate=True
    ).astype(BF)
    made = jnp.dot(inner, wdn[...], preferred_element_type=F32)
    for j in range(nk):
        fB[pl.ds(j, share, stride=nk), :] = made[:, j * 128 : (j + 1) * 128]
    r4s[...] = fB[...].astype(BF)
    spread(7, r4s, r4r)
    r4r[own_c, :] = r4s[own_c, :]

    loads[9].wait()
    await_bytes(A.at[pl.ds(0, (nh - 1) * nrow), :], xr.at[6])

    def project_out(n, carry):
        cols = pl.ds(aligned(n * 256, 256), 256)
        tout_ref[:, cols] = (
            tok[:, cols].astype(F32)
            + jnp.dot(R[...], wout[:, cols], preferred_element_type=F32)
        ).astype(BF)
        return carry

    lax.fori_loop(0, dw // 256, project_out, 0)

    await_bytes(r4r.at[rest, :], xr.at[7])
    total = hl[...]
    for i in range(nc):
        total += r4r[pl.ds(i * per, per), :].astype(F32)
    r5s[...] = total.astype(BF)
    to_ctx(lambda to: r5s, r5r.at[own_c, :], 8, 8)
    r5r[own_c, :] = r5s[...]
    await_bytes(r5r.at[rest, :], xr.at[8])
    fA[...] = r5r[...].astype(F32)
    for j in range(nk):
        lout_ref[:, j * 128 : (j + 1) * 128] = fA[pl.ds(j, share, stride=nk), :].astype(BF)

    for send in sends:
        send.wait_send()
    for r in rims:
        r.wait_send()
    await_bytes(r1r.at[rest, :], xs.at[0])
    await_bytes(r1u.at[pl.ds(0, nc - 1)], xs.at[1])
    await_bytes(r2r.at[rest2, :], xs.at[4])
    await_bytes(r3r.at[rest, :], xs.at[5])
    await_bytes(A.at[pl.ds(0, (nh - 1) * nrow), :], xs.at[6])
    await_bytes(r4r.at[rest, :], xs.at[7])
    await_bytes(r5r.at[rest, :], xs.at[8])


def per_device(
    nh,
    nc,
    tokens,
    ln_gain,
    w_qkv,
    w_out,
    neighbours,
    counts,
    latents,
    lat_gain,
    w_lat_q,
    w_lat_o,
    mlp_gain,
    w_up,
    w_down,
):
    nrow, dw = tokens.shape[1:]
    nlat = latents.shape[0]
    gtok = nrow * nh
    per = nlat // nc
    share = nlat // nh
    nblk = gtok // BLK
    two = share // nc * (dw // 128)
    hbm = pl.BlockSpec(memory_space=pl.ANY)
    vmem = pl.BlockSpec(memory_space=pltpu.VMEM)
    stage = gtok // 4
    scratch = [
        pltpu.VMEM((nrow, dw), BF),
        pltpu.VMEM((dw, 384), BF),
        pltpu.VMEM((dw, dw), BF),
        pltpu.VMEM((nlat, dw), BF),
        pltpu.VMEM((dw, 128), BF),
        pltpu.VMEM((128, dw), BF),
        pltpu.VMEM(w_up.shape, BF),
        pltpu.VMEM(w_down.shape, BF),
        pltpu.VMEM((gtok, dw), BF),
        pltpu.VMEM((nlat, dw), BF),
        pltpu.VMEM((2, gtok, 128), BF),
        pltpu.VMEM((3, gtok + 2 * RIM, 128), BF),
        pltpu.VMEM((stage, 128), BF),
        pltpu.VMEM((2, stage, 128), BF),
        pltpu.VMEM((nlat, 128), F32),
        pltpu.VMEM((nlat, 128), F32),
        pltpu.VMEM((two, 128), F32),
        pltpu.VMEM((2 * nlat, 128), BF),
        pltpu.VMEM((2 * nlat, 128), F32),
        pltpu.VMEM((2 * nlat, 128), F32),
        pltpu.VMEM((two, 128), F32),
        pltpu.VMEM((WIN, nblk, 128), F32),
        pltpu.VMEM((WIN, nblk, 128), F32),
        pltpu.VMEM((nlat, 128), BF),
        pltpu.VMEM((nc, 1, 128), F32),
        pltpu.VMEM((nlat, 128), BF),
        pltpu.VMEM((nc, 1, 128), F32),
        pltpu.VMEM((nh * two, 128), F32),
        pltpu.VMEM((nh * two, 128), F32),
        pltpu.VMEM((two, 128), BF),
        pltpu.VMEM((nlat, 128), BF),
        pltpu.VMEM((nlat, 128), BF),
        pltpu.VMEM((nlat, 128), BF),
        pltpu.VMEM((two, 128), BF),
        pltpu.VMEM((nlat, 128), BF),
        pltpu.VMEM((gtok, 128), BF),
        pltpu.VMEM((nrow, dw), BF),
        pltpu.SemaphoreType.DMA((10,)),
        pltpu.SemaphoreType.DMA((13,)),
        pltpu.SemaphoreType.DMA((13,)),
        pltpu.SemaphoreType.DMA((9,)),
        pltpu.SemaphoreType.DMA((9,)),
    ]
    tokens_out, latents_out = pl.pallas_call(
        functools.partial(kernel, nh, nc),
        out_shape=(
            jax.ShapeDtypeStruct((nrow, dw), BF),
            jax.ShapeDtypeStruct((share, dw), BF),
        ),
        in_specs=[hbm, vmem, hbm, hbm, vmem, vmem, hbm, vmem, hbm, hbm, vmem, hbm, hbm],
        out_specs=(vmem, vmem),
        scratch_shapes=scratch,
        compiler_params=pltpu.CompilerParams(
            collective_id=0, has_side_effects=True, vmem_limit_bytes=48 * 1024 * 1024
        ),
        name="encoder_block",
    )(
        tokens[0],
        ln_gain.reshape(1, dw),
        jnp.transpose(w_qkv, (1, 0, 2)),
        w_out,
        neighbours[0].T,
        counts,
        latents,
        lat_gain.reshape(1, dw),
        w_lat_q,
        w_lat_o,
        mlp_gain.reshape(dw // 128, 128),
        w_up,
        w_down,
    )
    return (tokens_out[None], latents_out)


def solution(mesh):
    in_specs = (
        P("ctx", "heads", None),
        P(),
        P(None, None, "heads"),
        P(),
        P("ctx", None, None),
        P("ctx", None),
        P(),
        P(),
        P(None, "heads"),
        P("heads", None),
        P(),
        P(None, "ctx"),
        P("ctx", None),
    )
    out_specs = (P("ctx", "heads", None), P("heads", None))
    return jax.shard_map(
        functools.partial(per_device, mesh.shape["heads"], mesh.shape["ctx"]),
        mesh=mesh,
        in_specs=in_specs,
        out_specs=out_specs,
        check_vma=False,
    )
```

```python
import functools

import jax
import jax.numpy as jnp
from jax import lax
from jax.experimental import pallas as pl
from jax.experimental.pallas import tpu as pltpu
from jax.sharding import PartitionSpec as P

HD = 64
BLK = 128
WIN = 5
RIM = 256
EPSILON = 1e-05
SCALE2 = HD ** (-0.5) * 1.4426950408889634
MESH = pl.DeviceIdType.MESH
BF = jnp.bfloat16
F32 = jnp.float32


def aligned(start, by):
    return pl.multiple_of(start, by)


def normalise(rows, gain):
    center = jnp.mean(rows, axis=-1, keepdims=True)
    spread = jnp.mean(jnp.square(rows - center), axis=-1, keepdims=True)
    return (rows - center) * lax.rsqrt(spread + EPSILON) * gain


def kernel(
    nh,
    nc,
    tok_hbm,
    lng_hbm,
    wqkv_hbm,
    wout_hbm,
    nb_hbm,
    cnt_hbm,
    lat_hbm,
    latg_hbm,
    wlq_hbm,
    wlo_hbm,
    mg_hbm,
    wup_hbm,
    wdn_hbm,
    tout_ref,
    lout_ref,
    lng_ref,
    nb_ref,
    cnt_ref,
    latg_ref,
    mg_ref,
    tok,
    wqkv,
    wout,
    lat,
    wlq,
    wlo,
    wup,
    wdn,
    G,
    latn,
    Q,
    KV,
    kst,
    vst,
    fA,
    fB,
    f2,
    qlat,
    om,
    mm,
    hl,
    multr,
    biasr,
    r1s,
    r1t,
    r1r,
    r1u,
    r2s,
    r2r,
    r3s,
    r3r,
    r4s,
    r4r,
    r5s,
    r5r,
    A,
    R,
    in_sem,
    gs,
    gr,
    xs,
    xr,
):
    h = lax.axis_index("heads")
    c = lax.axis_index("ctx")
    x = h // 2
    k = h % 2
    nrow = tok.shape[0]
    half = nrow // 2
    nlat = lat.shape[0]
    dw = tok.shape[1]
    nk = dw // 128
    gtok = nh * nrow
    nblk = gtok // BLK
    per = nlat // nc

    loads = [
        pltpu.make_async_copy(tok_hbm, tok, in_sem.at[0]),
        pltpu.make_async_copy(lat_hbm, lat, in_sem.at[1]),
        pltpu.make_async_copy(wlq_hbm, wlq, in_sem.at[2]),
        pltpu.make_async_copy(wqkv_hbm.at[0], wqkv.at[:, pl.ds(0, 128)], in_sem.at[3]),
        pltpu.make_async_copy(wqkv_hbm.at[1], wqkv.at[:, pl.ds(128, 128)], in_sem.at[4]),
        pltpu.make_async_copy(wqkv_hbm.at[2], wqkv.at[:, pl.ds(256, 128)], in_sem.at[5]),
        pltpu.make_async_copy(wlo_hbm, wlo, in_sem.at[6]),
        pltpu.make_async_copy(wup_hbm, wup, in_sem.at[7]),
        pltpu.make_async_copy(wdn_hbm, wdn, in_sem.at[8]),
        pltpu.make_async_copy(wout_hbm, wout, in_sem.at[9]),
    ]
    small = [
        pltpu.make_async_copy(lng_hbm, lng_ref, in_sem.at[10]),
        pltpu.make_async_copy(latg_hbm, latg_ref, in_sem.at[11]),
        pltpu.make_async_copy(nb_hbm, nb_ref, in_sem.at[12]),
        pltpu.make_async_copy(cnt_hbm, cnt_ref, in_sem.at[13]),
        pltpu.make_async_copy(mg_hbm, mg_ref, in_sem.at[14]),
    ]
    small[0].start()
    for load in loads[:3] + small[1:] + loads[3:]:
        load.start()

    barrier = pltpu.get_barrier_semaphore()

    def hello_h(d, carry):
        pl.semaphore_signal(
            barrier, inc=1, device_id={"heads": lax.rem(h + d, nh)}, device_id_type=MESH
        )
        return carry

    def hello_c(d, carry):
        pl.semaphore_signal(
            barrier, inc=1, device_id={"ctx": lax.rem(c + d, nc)}, device_id_type=MESH
        )
        return carry

    lax.fori_loop(1, nh, hello_h, 0)
    lax.fori_loop(1, nc, hello_c, 0)

    loads[0].wait()
    small[0].wait()
    mine = aligned(h * nrow, 256)
    step = 32

    def norm_tokens(i, carry):
        at = pl.ds(aligned(i * step, step), step)
        G[pl.ds(aligned(mine + i * step, step), step), :] = normalise(
            tok[at, :].astype(F32), lng_ref[...]
        ).astype(BF)
        return carry

    lax.fori_loop(0, nrow // step, norm_tokens, 0)
    pl.semaphore_wait(barrier, nh + nc - 2)

    sib = x * 2 + (1 - k)
    right = lax.rem(x + 1, nh // 2) * 2 + k
    left = lax.rem(x + nh // 2 - 1, nh // 2) * 2 + k
    far = lax.rem(x + 2, nh // 2) * 2 + k
    right_s = lax.rem(x + 1, nh // 2) * 2 + (1 - k)
    left_s = lax.rem(x + nh // 2 - 1, nh // 2) * 2 + (1 - k)
    far_s = lax.rem(x + 2, nh // 2) * 2 + (1 - k)

    def piece(block, part):
        return aligned(block * nrow + part * half, 128)

    def move(at, size, sem, to):
        rows = pl.ds(at, size)
        return pltpu.make_async_remote_copy(
            src_ref=G.at[rows, :],
            dst_ref=G.at[rows, :],
            send_sem=gs.at[sem],
            recv_sem=gr.at[sem],
            device_id={"heads": to},
            device_id_type=MESH,
        )

    pending = []
    sends = [
        move(piece(h, 0), half, 1, right),
        move(piece(h, 1), half, 3, left),
        move(mine, nrow, 0, sib),
        move(piece(h, 1), half, 2, right),
        move(piece(h, 0), half, 4, left),
    ]
    for send in sends:
        send.start()
    pending += [send.wait_send for send in sends]

    loads[1].wait()
    for load in small[1:]:
        load.wait()

    def norm_latents(i, carry):
        at = pl.ds(aligned(i * step, step), step)
        latn[at, :] = normalise(lat[at, :].astype(F32), latg_ref[...]).astype(BF)
        return carry

    lax.fori_loop(0, nlat // step, norm_latents, 0)
    loads[2].wait()
    fA[...] = jnp.dot(latn[...], wlq[...], preferred_element_type=F32)
    share = nlat // nh
    two = share // nc
    for hh in range(nh):
        for i in range(two):
            fB[pl.ds(hh * two + i, nc, stride=per), :] = fA[
                pl.ds(hh * share + i, nc, stride=two), :
            ]
    lane = lax.broadcasted_iota(jnp.int32, (nlat, 128), 1)
    lq = fB[...]
    qlat[pl.ds(0, nlat), :] = jnp.where(lane < HD, lq, 0.0).astype(BF)
    qlat[pl.ds(nlat, nlat), :] = jnp.where(lane < HD, 0.0, lq).astype(BF)
    om[...] = jnp.zeros_like(om)
    mm[...] = jnp.full_like(mm, -jnp.inf)

    own64 = lat[pl.ds(aligned(h * share, share), share), :].astype(F32)
    for j in range(nk):
        fA[pl.ds(j, share, stride=nk), :] = own64[:, j * 128 : (j + 1) * 128]
    hl[...] = fA[pl.ds(aligned(c * two * nk, two * nk), two * nk), :]

    slot = lax.broadcasted_iota(jnp.int32, nb_ref.shape, 0)
    column = lax.broadcasted_iota(jnp.int32, nb_ref.shape, 1)
    live = slot < cnt_ref[...]
    eye = lax.broadcasted_iota(jnp.int32, (nblk, nblk), 0) == lax.broadcasted_iota(
        jnp.int32, (nblk, nblk), 1
    )
    for j in range(WIN):
        hits = jnp.where(live & (nb_ref[...] == column + j), 1.0, 0.0)
        times = jnp.sum(hits, axis=0, keepdims=True)
        times = jnp.sum(jnp.where(eye, times, 0.0), axis=1, keepdims=True)
        times = jnp.broadcast_to(times, (nblk, 128))
        multr[j] = times
        biasr[j] = jnp.where(times > 0.0, 0.0, -jnp.inf)

    keys = kst.shape[0]
    tile = 256

    def project(starts):
        rows = jnp.concatenate([G[pl.ds(s, half), :] for s in starts], axis=0)
        made = jnp.dot(rows, wqkv[...], preferred_element_type=F32)
        first = lax.broadcasted_iota(jnp.int32, (half, 128), 1) < HD
        for i, s in enumerate(starts):
            part = slice(i * half, (i + 1) * half)
            q = made[part, 0:128]
            key = made[part, 128:256].astype(BF)
            v = made[part, 256:384]
            v0 = jnp.where(first, v, 1.0).astype(BF)
            v1 = jnp.where(first, 1.0, v).astype(BF)
            Q[0, pl.ds(s, half), :] = jnp.where(first, q, 0.0).astype(BF)
            Q[1, pl.ds(s, half), :] = jnp.where(first, 0.0, q).astype(BF)
            wide = pl.ds(aligned(s + RIM, 128), half)
            KV[0, wide, :] = key
            KV[1, wide, :] = v0
            KV[2, wide, :] = v1
            kst[part, :] = key
            vst[0, part, :] = v0
            vst[1, part, :] = v1

    def cross(t, carry):
        at = pl.ds(aligned(t * tile, tile), tile)
        s = lax.dot_general(
            qlat[at, :], kst[...], (((1,), (1,)), ((), ())), preferred_element_type=F32
        )
        before = mm[at, :]
        top = jnp.maximum(before, jnp.max(s, axis=1, keepdims=True))
        alpha = jnp.exp2((before - top) * SCALE2)
        p = jnp.concatenate(
            [
                jnp.exp2((s[:, j * 128 : (j + 1) * 128] - top) * SCALE2).astype(BF)
                for j in range(keys // 128)
            ],
            axis=1,
        )
        mm[at, :] = top
        om[at, :] = om[at, :] * alpha + jnp.dot(
            p, vst[t * tile // nlat], preferred_element_type=F32
        )
        return carry

    def stage(starts):
        project(starts)
        lax.fori_loop(0, 2 * nlat // tile, cross, 0)

    for i in (3, 4, 5):
        loads[i].wait()
    move(piece(sib, 0), nrow, 0, sib).wait_recv()
    stage([piece(h, 0), piece(h, 1), piece(sib, 0), piece(sib, 1)])

    move(piece(left, 0), half, 1, right).wait_recv()
    passed = [move(piece(left, 0), half, 5, right), move(piece(left, 0), half, 7, sib)]
    move(piece(right, 1), half, 3, left).wait_recv()
    passed += [move(piece(right, 1), half, 6, left), move(piece(right, 1), half, 8, sib)]
    for send in passed:
        send.start()
    pending += [send.wait_send for send in passed]
    move(piece(left_s, 0), half, 7, sib).wait_recv()
    move(piece(right_s, 1), half, 8, sib).wait_recv()
    stage([piece(left, 0), piece(right, 1), piece(left_s, 0), piece(right_s, 1)])

    move(piece(left, 1), half, 2, right).wait_recv()
    move(piece(right, 0), half, 4, left).wait_recv()
    passed = [move(piece(left, 1), half, 9, sib), move(piece(right, 0), half, 10, sib)]
    for send in passed:
        send.start()
    pending += [send.wait_send for send in passed]
    move(piece(left_s, 1), half, 9, sib).wait_recv()
    move(piece(right_s, 0), half, 10, sib).wait_recv()
    stage([piece(left, 1), piece(right, 0), piece(left_s, 1), piece(right_s, 0)])

    move(piece(far, 0), half, 5, right).wait_recv()
    move(piece(far, 1), half, 6, left).wait_recv()
    passed = [move(piece(far, 0), half, 11, sib), move(piece(far, 1), half, 12, sib)]
    for send in passed:
        send.start()
    pending += [send.wait_send for send in passed]
    move(piece(far_s, 0), half, 11, sib).wait_recv()
    move(piece(far_s, 1), half, 12, sib).wait_recv()
    stage([piece(far, 0), piece(far, 1), piece(far_s, 0), piece(far_s, 1)])

    tile1 = 128
    lane1 = lax.broadcasted_iota(jnp.int32, (tile1, 128), 1)
    row1 = lax.broadcasted_iota(jnp.int32, (tile1, 128), 0)
    first1 = lane1 < HD
    pick1 = lax.rem(lane1, HD) == lax.rem(row1, per)
    for t in range(nlat // tile1):
        at0 = pl.ds(t * tile1, tile1)
        at1 = pl.ds(nlat + t * tile1, tile1)
        o0, o1 = om[at0, :], om[at1, :]
        total = pltpu.roll(jnp.where(first1, o1, o0), HD, 1)
        r1s[at0, :] = (jnp.where(first1, o0, o1) / total).astype(BF)
        lse = jnp.where(first1, mm[at0, :], mm[at1, :]) * SCALE2 + jnp.log2(total)
        lse = jnp.where(pick1, lse, 0.0)
        for g in range(tile1 // per):
            r1t[t * (tile1 // per) + g] = jnp.sum(
                lse[g * per : (g + 1) * per, :], axis=0, keepdims=True
            )

    own_c = pl.ds(aligned(c * per, 16), per)

    def to_ctx(src, dst, s, r):
        def body(d, carry):
            to = lax.rem(c + d, nc)
            pltpu.make_async_remote_copy(
                src_ref=src(to),
                dst_ref=dst,
                send_sem=xs.at[s],
                recv_sem=xr.at[r],
                device_id={"ctx": to},
                device_id_type=MESH,
            ).start()
            return carry

        lax.fori_loop(1, nc, body, 0)

    def spread(i, src, dst):
        to_ctx(lambda to: src.at[pl.ds(aligned(to * per, 16), per), :], dst.at[own_c, :], i, i)

    def await_bytes(ref, sem):
        pltpu.make_async_copy(ref, ref, sem).wait()

    rest = pl.ds(0, (nc - 1) * per)
    to_ctx(lambda to: r1t.at[to], r1u.at[c], 1, 1)
    spread(0, r1s, r1r)
    r1r[own_c, :] = r1s[own_c, :]
    r1u[c] = r1t[c]

    def rim(src, dst, sem, to):
        return pltpu.make_async_remote_copy(
            src_ref=KV.at[:, pl.ds(src, RIM), :],
            dst_ref=KV.at[:, pl.ds(dst, RIM), :],
            send_sem=xs.at[sem],
            recv_sem=xr.at[sem],
            device_id={"ctx": to},
            device_id_type=MESH,
        )

    rims = [
        rim(RIM, RIM + gtok, 2, lax.rem(c + nc - 1, nc)),
        rim(gtok, 0, 3, lax.rem(c + 1, nc)),
    ]
    for r in rims:
        r.start()
    pending += [r.wait_send for r in rims]
    pending += [lambda: await_bytes(r1r.at[rest, :], xs.at[0])]
    pending += [lambda: await_bytes(r1u.at[pl.ds(0, nc - 1)], xs.at[1])]

    firstb = lax.broadcasted_iota(jnp.int32, (BLK, 128), 1) < HD

    def attend(b, carry):
        at = pl.ds(aligned(b * BLK, BLK), BLK)
        win = pl.ds(aligned(b * BLK, BLK), WIN * BLK)
        q = jnp.concatenate([Q[0, at, :], Q[1, at, :]], axis=0)
        s = lax.dot_general(
            q, KV[0, win, :], (((1,), (1,)), ((), ())), preferred_element_type=F32
        )
        parts = [
            s[:, j * BLK : (j + 1) * BLK] + biasr[j, pl.ds(b, 1), :] for j in range(WIN)
        ]
        top = parts[0]
        for part in parts[1:]:
            top = jnp.maximum(top, part)
        top = jnp.max(top, axis=1, keepdims=True)
        p = jnp.concatenate(
            [
                (jnp.exp2((part - top) * SCALE2) * multr[j, pl.ds(b, 1), :]).astype(BF)
                for j, part in enumerate(parts)
            ],
            axis=1,
        )
        o0 = jnp.dot(p[:BLK], KV[1, win, :], preferred_element_type=F32)
        o1 = jnp.dot(p[BLK:], KV[2, win, :], preferred_element_type=F32)
        total = pltpu.roll(jnp.where(firstb, o1, o0), HD, 1)
        A[at, :] = (jnp.where(firstb, o0, o1) / total).astype(BF)
        return carry

    lax.fori_loop(2, nblk - 2, attend, 0)

    await_bytes(r1r.at[rest, :], xr.at[0])
    await_bytes(r1u.at[pl.ds(0, nc - 1)], xr.at[1])
    lanes = lax.broadcasted_iota(jnp.int32, (per, 128), 1)
    pick = lax.rem(lanes, HD) == lax.broadcasted_iota(jnp.int32, (per, 128), 0)
    for i in range(nc):
        fA[pl.ds(i * per, per), :] = jnp.where(pick, r1u[i], 0.0)
    same = (
        lax.broadcasted_iota(jnp.int32, (128, 128), 0) // HD
        == lax.broadcasted_iota(jnp.int32, (128, 128), 1) // HD
    )
    fB[...] = jnp.dot(
        fA[...],
        jnp.where(same, 1.0, 0.0),
        preferred_element_type=F32,
        precision=lax.Precision.HIGHEST,
    )
    peak = fB[pl.ds(0, per), :]
    for i in range(1, nc):
        peak = jnp.maximum(peak, fB[pl.ds(i * per, per), :])
    weight = jnp.zeros((per, 128), F32)
    value = jnp.zeros((per, 128), F32)
    for i in range(nc):
        w = jnp.exp2(fB[pl.ds(i * per, per), :] - peak)
        weight += w
        value += w * r1r[pl.ds(i * per, per), :].astype(F32)
    lat_att = (value / weight).astype(BF)

    loads[6].wait()
    made = jnp.dot(lat_att, wlo[...], preferred_element_type=F32)
    for j in range(nk):
        r2s[pl.ds(j, per, stride=nk), :] = made[:, j * 128 : (j + 1) * 128]
    rest2 = pl.ds(0, (nh - 1) * two * nk)
    own_h = pl.ds(aligned(h * two * nk, 16), two * nk)

    def send2(d, carry):
        to = lax.rem(h + d, nh)
        pltpu.make_async_remote_copy(
            src_ref=r2s.at[pl.ds(aligned(to * two * nk, 16), two * nk), :],
            dst_ref=r2r.at[own_h, :],
            send_sem=xs.at[4],
            recv_sem=xr.at[4],
            device_id={"heads": to},
            device_id_type=MESH,
        ).start()
        return carry

    lax.fori_loop(1, nh, send2, 0)
    r2r[own_h, :] = r2s[own_h, :]
    pending += [lambda: await_bytes(r2r.at[rest2, :], xs.at[4])]

    for r in rims:
        r.wait_recv()
    lax.fori_loop(0, 2, attend, 0)
    lax.fori_loop(nblk - 2, nblk, attend, 0)

    await_bytes(r2r.at[rest2, :], xr.at[4])
    hidden = hl[...]
    for i in range(nh):
        hidden += r2r[pl.ds(i * two * nk, two * nk), :]
    hl[...] = hidden
    for i in range(two):
        row = hidden[i * nk : (i + 1) * nk, :]
        center = jnp.sum(jnp.sum(row, axis=0, keepdims=True), axis=1, keepdims=True) / dw
        off = row - center
        spread2 = (
            jnp.sum(jnp.sum(jnp.square(off), axis=0, keepdims=True), axis=1, keepdims=True) / dw
        )
        f2[pl.ds(i * nk, nk), :] = off * lax.rsqrt(spread2 + EPSILON) * mg_ref[...]
    r3s[...] = f2[...].astype(BF)
    to_ctx(lambda to: r3s, r3r.at[own_c, :], 5, 5)
    r3r[own_c, :] = r3s[...]
    pending += [lambda: await_bytes(r3r.at[rest, :], xs.at[5])]

    head_cols = pl.ds(aligned(h * 128, 128), 128)

    def send_back(d, carry):
        to = lax.rem(h + d, nh)
        pltpu.make_async_remote_copy(
            src_ref=A.at[pl.ds(aligned(to * nrow, 128), nrow), :],
            dst_ref=R.at[:, head_cols],
            send_sem=xs.at[6],
            recv_sem=xr.at[6],
            device_id={"heads": to},
            device_id_type=MESH,
        ).start()
        return carry

    lax.fori_loop(1, nh, send_back, 0)
    R[:, head_cols] = A[pl.ds(mine, nrow), :]
    pending += [lambda: await_bytes(A.at[pl.ds(0, (nh - 1) * nrow), :], xs.at[6])]

    loads[7].wait()
    loads[8].wait()
    await_bytes(r3r.at[rest, :], xr.at[5])
    fA[...] = r3r[...].astype(F32)
    rows = jnp.concatenate(
        [fA[pl.ds(j, share, stride=nk), :].astype(BF) for j in range(nk)], axis=1
    )
    inner = jax.nn.gelu(
        jnp.dot(rows, wup[...], preferred_element_type=F32), approximate=True
    ).astype(BF)
    made = jnp.dot(inner, wdn[...], preferred_element_type=F32)
    for j in range(nk):
        fB[pl.ds(j, share, stride=nk), :] = made[:, j * 128 : (j + 1) * 128]
    r4s[...] = fB[...].astype(BF)
    spread(7, r4s, r4r)
    r4r[own_c, :] = r4s[own_c, :]
    pending += [lambda: await_bytes(r4r.at[rest, :], xs.at[7])]

    loads[9].wait()
    await_bytes(A.at[pl.ds(0, (nh - 1) * nrow), :], xr.at[6])

    def project_out(n, carry):
        cols = pl.ds(aligned(n * 256, 256), 256)
        tout_ref[:, cols] = (
            tok[:, cols].astype(F32)
            + jnp.dot(R[...], wout[:, cols], preferred_element_type=F32)
        ).astype(BF)
        return carry

    lax.fori_loop(0, dw // 256, project_out, 0)

    await_bytes(r4r.at[rest, :], xr.at[7])
    total = hl[...]
    for i in range(nc):
        total += r4r[pl.ds(i * per, per), :].astype(F32)
    r5s[...] = total.astype(BF)
    to_ctx(lambda to: r5s, r5r.at[own_c, :], 8, 8)
    r5r[own_c, :] = r5s[...]
    pending += [lambda: await_bytes(r5r.at[rest, :], xs.at[8])]
    await_bytes(r5r.at[rest, :], xr.at[8])
    fA[...] = r5r[...].astype(F32)
    for j in range(nk):
        lout_ref[:, j * 128 : (j + 1) * 128] = fA[pl.ds(j, share, stride=nk), :].astype(BF)

    for done in pending:
        done()


def per_device(
    nh,
    nc,
    tokens,
    ln_gain,
    w_qkv,
    w_out,
    neighbours,
    counts,
    latents,
    lat_gain,
    w_lat_q,
    w_lat_o,
    mlp_gain,
    w_up,
    w_down,
):
    nrow, dw = tokens.shape[1:]
    nlat = latents.shape[0]
    gtok = nrow * nh
    per = nlat // nc
    share = nlat // nh
    nblk = gtok // BLK
    two = share // nc * (dw // 128)
    hbm = pl.BlockSpec(memory_space=pltpu.HBM)
    vmem = pl.BlockSpec(memory_space=pltpu.VMEM)
    stage = gtok // 4
    scratch = [
        pltpu.VMEM((1, dw), F32),
        pltpu.VMEM((neighbours.shape[2], nblk), jnp.int32),
        pltpu.VMEM((1, nblk), jnp.int32),
        pltpu.VMEM((1, dw), F32),
        pltpu.VMEM((dw // 128, 128), F32),
        pltpu.VMEM((nrow, dw), BF),
        pltpu.VMEM((dw, 384), BF),
        pltpu.VMEM((dw, dw), BF),
        pltpu.VMEM((nlat, dw), BF),
        pltpu.VMEM((dw, 128), BF),
        pltpu.VMEM((128, dw), BF),
        pltpu.VMEM(w_up.shape, BF),
        pltpu.VMEM(w_down.shape, BF),
        pltpu.VMEM((gtok, dw), BF),
        pltpu.VMEM((nlat, dw), BF),
        pltpu.VMEM((2, gtok, 128), BF),
        pltpu.VMEM((3, gtok + 2 * RIM, 128), BF),
        pltpu.VMEM((stage, 128), BF),
        pltpu.VMEM((2, stage, 128), BF),
        pltpu.VMEM((nlat, 128), F32),
        pltpu.VMEM((nlat, 128), F32),
        pltpu.VMEM((two, 128), F32),
        pltpu.VMEM((2 * nlat, 128), BF),
        pltpu.VMEM((2 * nlat, 128), F32),
        pltpu.VMEM((2 * nlat, 128), F32),
        pltpu.VMEM((two, 128), F32),
        pltpu.VMEM((WIN, nblk, 128), F32),
        pltpu.VMEM((WIN, nblk, 128), F32),
        pltpu.VMEM((nlat, 128), BF),
        pltpu.VMEM((nc, 1, 128), F32),
        pltpu.VMEM((nlat, 128), BF),
        pltpu.VMEM((nc, 1, 128), F32),
        pltpu.VMEM((nh * two, 128), F32),
        pltpu.VMEM((nh * two, 128), F32),
        pltpu.VMEM((two, 128), BF),
        pltpu.VMEM((nlat, 128), BF),
        pltpu.VMEM((nlat, 128), BF),
        pltpu.VMEM((nlat, 128), BF),
        pltpu.VMEM((two, 128), BF),
        pltpu.VMEM((nlat, 128), BF),
        pltpu.VMEM((gtok, 128), BF),
        pltpu.VMEM((nrow, dw), BF),
        pltpu.SemaphoreType.DMA((15,)),
        pltpu.SemaphoreType.DMA((13,)),
        pltpu.SemaphoreType.DMA((13,)),
        pltpu.SemaphoreType.DMA((9,)),
        pltpu.SemaphoreType.DMA((9,)),
    ]
    tokens_out, latents_out = pl.pallas_call(
        functools.partial(kernel, nh, nc),
        out_shape=(
            jax.ShapeDtypeStruct((nrow, dw), BF),
            jax.ShapeDtypeStruct((share, dw), BF),
        ),
        in_specs=[hbm] * 13,
        out_specs=(vmem, vmem),
        scratch_shapes=scratch,
        compiler_params=pltpu.CompilerParams(
            collective_id=0, has_side_effects=True, vmem_limit_bytes=60 * 1024 * 1024
        ),
        name="encoder_block",
    )(
        tokens[0],
        ln_gain.reshape(1, dw),
        jnp.transpose(w_qkv, (1, 0, 2)),
        w_out,
        neighbours[0].T,
        counts,
        latents,
        lat_gain.reshape(1, dw),
        w_lat_q,
        w_lat_o,
        mlp_gain.reshape(dw // 128, 128),
        w_up,
        w_down,
    )
    return (tokens_out[None], latents_out)


def solution(mesh):
    in_specs = (
        P("ctx", "heads", None),
        P(),
        P(None, None, "heads"),
        P(),
        P("ctx", None, None),
        P("ctx", None),
        P(),
        P(),
        P(None, "heads"),
        P("heads", None),
        P(),
        P(None, "ctx"),
        P("ctx", None),
    )
    out_specs = (P("ctx", "heads", None), P("heads", None))
    return jax.shard_map(
        functools.partial(per_device, mesh.shape["heads"], mesh.shape["ctx"]),
        mesh=mesh,
        in_specs=in_specs,
        out_specs=out_specs,
        check_vma=False,
    )
```

```python
import functools

import jax
import jax.numpy as jnp
from jax import lax
from jax.experimental import pallas as pl
from jax.experimental.pallas import tpu as pltpu
from jax.sharding import PartitionSpec as P

HD = 64
BLK = 128
WIN = 5
RIM = 256
EPSILON = 1e-05
SCALE2 = HD ** (-0.5) * 1.4426950408889634
MESH = pl.DeviceIdType.MESH
BF = jnp.bfloat16
F32 = jnp.float32


def aligned(start, by):
    return pl.multiple_of(start, by)


def normalise(rows, gain):
    center = jnp.mean(rows, axis=-1, keepdims=True)
    spread = jnp.mean(jnp.square(rows - center), axis=-1, keepdims=True)
    return (rows - center) * lax.rsqrt(spread + EPSILON) * gain


def kernel(
    nh,
    nc,
    tok_hbm,
    lng_hbm,
    wqkv_hbm,
    wout_hbm,
    nb_hbm,
    cnt_hbm,
    lat_hbm,
    latg_hbm,
    wlq_hbm,
    wlo_hbm,
    mg_hbm,
    wup_hbm,
    wdn_hbm,
    tout_ref,
    lout_ref,
    lng_ref,
    nb_ref,
    cnt_ref,
    latg_ref,
    mg_ref,
    tok,
    wqkv,
    wout,
    lat,
    wlq,
    wlo,
    wup,
    wdn,
    G,
    latn,
    Q,
    KV,
    kst,
    vst,
    fA,
    fB,
    f2,
    qlat,
    om,
    mm,
    hl,
    multr,
    biasr,
    r1s,
    r1t,
    r1r,
    r1u,
    r2s,
    r2r,
    r3s,
    r3r,
    r4s,
    r4r,
    r5s,
    r5r,
    A,
    R,
    in_sem,
    gs,
    gr,
    xs,
    xr,
):
    h = lax.axis_index("heads")
    c = lax.axis_index("ctx")
    x = h // 2
    k = h % 2
    nrow = tok.shape[0]
    nlat = lat.shape[0]
    dw = tok.shape[1]
    nk = dw // 128
    gtok = nh * nrow
    nblk = gtok // BLK
    per = nlat // nc

    loads = [
        pltpu.make_async_copy(tok_hbm, tok, in_sem.at[0]),
        pltpu.make_async_copy(lat_hbm, lat, in_sem.at[1]),
        pltpu.make_async_copy(wlq_hbm, wlq, in_sem.at[2]),
        pltpu.make_async_copy(wqkv_hbm.at[0], wqkv.at[:, pl.ds(0, 128)], in_sem.at[3]),
        pltpu.make_async_copy(wqkv_hbm.at[1], wqkv.at[:, pl.ds(128, 128)], in_sem.at[4]),
        pltpu.make_async_copy(wqkv_hbm.at[2], wqkv.at[:, pl.ds(256, 128)], in_sem.at[5]),
        pltpu.make_async_copy(wlo_hbm, wlo, in_sem.at[6]),
        pltpu.make_async_copy(wup_hbm, wup, in_sem.at[7]),
        pltpu.make_async_copy(wdn_hbm, wdn, in_sem.at[8]),
        pltpu.make_async_copy(wout_hbm, wout, in_sem.at[9]),
    ]
    small = [
        pltpu.make_async_copy(lng_hbm, lng_ref, in_sem.at[10]),
        pltpu.make_async_copy(latg_hbm, latg_ref, in_sem.at[11]),
        pltpu.make_async_copy(nb_hbm, nb_ref, in_sem.at[12]),
        pltpu.make_async_copy(cnt_hbm, cnt_ref, in_sem.at[13]),
        pltpu.make_async_copy(mg_hbm, mg_ref, in_sem.at[14]),
    ]
    small[0].start()
    for load in loads[:3] + small[1:] + loads[3:]:
        load.start()

    barrier = pltpu.get_barrier_semaphore()

    def hello_h(d, carry):
        pl.semaphore_signal(
            barrier, inc=1, device_id={"heads": lax.rem(h + d, nh)}, device_id_type=MESH
        )
        return carry

    def hello_c(d, carry):
        pl.semaphore_signal(
            barrier, inc=1, device_id={"ctx": lax.rem(c + d, nc)}, device_id_type=MESH
        )
        return carry

    lax.fori_loop(1, nh, hello_h, 0)
    lax.fori_loop(1, nc, hello_c, 0)

    loads[0].wait()
    small[0].wait()
    mine = aligned(h * nrow, 256)
    step = 32

    def norm_tokens(i, carry):
        at = pl.ds(aligned(i * step, step), step)
        G[pl.ds(aligned(mine + i * step, step), step), :] = normalise(
            tok[at, :].astype(F32), lng_ref[...]
        ).astype(BF)
        return carry

    lax.fori_loop(0, nrow // step, norm_tokens, 0)
    pl.semaphore_wait(barrier, nh + nc - 2)

    sib = x * 2 + (1 - k)
    right = lax.rem(x + 1, nh // 2) * 2 + k
    left = lax.rem(x + nh // 2 - 1, nh // 2) * 2 + k
    far = lax.rem(x + 2, nh // 2) * 2 + k
    right_s = lax.rem(x + 1, nh // 2) * 2 + (1 - k)
    left_s = lax.rem(x + nh // 2 - 1, nh // 2) * 2 + (1 - k)
    far_s = lax.rem(x + 2, nh // 2) * 2 + (1 - k)

    quarter = nrow // 4

    def move(block, part, parts, sem, to):
        rows = pl.ds(aligned(block * nrow + part * quarter, quarter), parts * quarter)
        return pltpu.make_async_remote_copy(
            src_ref=G.at[rows, :],
            dst_ref=G.at[rows, :],
            send_sem=gs.at[sem],
            recv_sem=gr.at[sem],
            device_id={"heads": to},
            device_id_type=MESH,
        )

    pending = []
    sends = []
    for i in range(4):
        sends += [move(h, i, 1, 1 + i, right), move(h, 3 - i, 1, 8 - i, left)]
        if i == 1:
            sends += [move(h, 0, 4, 0, sib)]
    for send in sends:
        send.start()
    pending += [send.wait_send for send in sends]

    loads[1].wait()
    for load in small[1:]:
        load.wait()

    def norm_latents(i, carry):
        at = pl.ds(aligned(i * step, step), step)
        latn[at, :] = normalise(lat[at, :].astype(F32), latg_ref[...]).astype(BF)
        return carry

    lax.fori_loop(0, nlat // step, norm_latents, 0)
    loads[2].wait()
    fA[...] = jnp.dot(latn[...], wlq[...], preferred_element_type=F32)
    share = nlat // nh
    two = share // nc
    for hh in range(nh):
        for i in range(two):
            fB[pl.ds(hh * two + i, nc, stride=per), :] = fA[
                pl.ds(hh * share + i, nc, stride=two), :
            ]
    lane = lax.broadcasted_iota(jnp.int32, (nlat, 128), 1)
    lq = fB[...]
    qlat[pl.ds(0, nlat), :] = jnp.where(lane < HD, lq, 0.0).astype(BF)
    qlat[pl.ds(nlat, nlat), :] = jnp.where(lane < HD, 0.0, lq).astype(BF)
    om[...] = jnp.zeros_like(om)
    mm[...] = jnp.full_like(mm, -jnp.inf)

    own64 = lat[pl.ds(aligned(h * share, share), share), :].astype(F32)
    for j in range(nk):
        fA[pl.ds(j, share, stride=nk), :] = own64[:, j * 128 : (j + 1) * 128]
    hl[...] = fA[pl.ds(aligned(c * two * nk, two * nk), two * nk), :]

    slot = lax.broadcasted_iota(jnp.int32, nb_ref.shape, 0)
    column = lax.broadcasted_iota(jnp.int32, nb_ref.shape, 1)
    live = slot < cnt_ref[...]
    eye = lax.broadcasted_iota(jnp.int32, (nblk, nblk), 0) == lax.broadcasted_iota(
        jnp.int32, (nblk, nblk), 1
    )
    for j in range(WIN):
        hits = jnp.where(live & (nb_ref[...] == column + j), 1.0, 0.0)
        times = jnp.sum(hits, axis=0, keepdims=True)
        times = jnp.sum(jnp.where(eye, times, 0.0), axis=1, keepdims=True)
        times = jnp.broadcast_to(times, (nblk, 128))
        multr[j] = times
        biasr[j] = jnp.where(times > 0.0, 0.0, -jnp.inf)

    def project(pieces):
        spans = [
            (aligned(block * nrow + part * quarter, quarter), parts * quarter)
            for block, part, parts in pieces
        ]
        rows = jnp.concatenate([G[pl.ds(s, size), :] for s, size in spans], axis=0)
        made = jnp.dot(rows, wqkv[...], preferred_element_type=F32)
        at = 0
        for s, size in spans:
            part = slice(at, at + size)
            at += size
            first = lax.broadcasted_iota(jnp.int32, (size, 128), 1) < HD
            q = made[part, 0:128]
            key = made[part, 128:256].astype(BF)
            v = made[part, 256:384]
            v0 = jnp.where(first, v, 1.0).astype(BF)
            v1 = jnp.where(first, 1.0, v).astype(BF)
            Q[0, pl.ds(s, size), :] = jnp.where(first, q, 0.0).astype(BF)
            Q[1, pl.ds(s, size), :] = jnp.where(first, 0.0, q).astype(BF)
            wide = pl.ds(aligned(s + RIM, quarter), size)
            KV[0, wide, :] = key
            KV[1, wide, :] = v0
            KV[2, wide, :] = v1
            kst[part, :] = key
            vst[0, part, :] = v0
            vst[1, part, :] = v1
        return at

    def cross(keys, t):
        at = pl.ds(t * nlat, nlat)
        s = lax.dot_general(
            qlat[at, :],
            kst[pl.ds(0, keys), :],
            (((1,), (1,)), ((), ())),
            preferred_element_type=F32,
        )
        before = mm[at, :]
        top = jnp.maximum(before, jnp.max(s, axis=1, keepdims=True))
        alpha = jnp.exp2((before - top) * SCALE2)
        p = jnp.concatenate(
            [
                jnp.exp2((s[:, j * 128 : (j + 1) * 128] - top) * SCALE2).astype(BF)
                for j in range(keys // 128)
            ],
            axis=1,
        )
        mm[at, :] = top
        om[at, :] = om[at, :] * alpha + jnp.dot(
            p, vst[t, pl.ds(0, keys), :], preferred_element_type=F32
        )

    def stage(pieces):
        keys = project(pieces)
        for t in range(2):
            cross(keys, t)

    def start(copies):
        for copy in copies:
            copy.start()
        pending.extend([copy.wait_send for copy in copies])

    move(left, 0, 1, 1, right).wait_recv()
    move(right, 3, 1, 8, left).wait_recv()
    start([move(left, 0, 1, 9, right), move(right, 3, 1, 12, left)])
    for i in (3, 4, 5):
        loads[i].wait()
    move(sib, 0, 4, 0, sib).wait_recv()
    stage([(h, 0, 4), (sib, 0, 4)])

    move(left, 1, 1, 2, right).wait_recv()
    move(right, 2, 1, 7, left).wait_recv()
    start([move(left, 1, 1, 10, right), move(right, 2, 1, 11, left)])
    start([move(left, 0, 2, 13, sib), move(right, 2, 2, 14, sib)])
    move(left_s, 0, 2, 13, sib).wait_recv()
    move(right_s, 2, 2, 14, sib).wait_recv()
    stage([(left, 0, 2), (right, 2, 2), (left_s, 0, 2), (right_s, 2, 2)])

    for i in (2, 3):
        move(left, i, 1, 1 + i, right).wait_recv()
        move(right, 3 - i, 1, 8 - i, left).wait_recv()
    start([move(left, 2, 2, 15, sib), move(right, 0, 2, 16, sib)])
    move(left_s, 2, 2, 15, sib).wait_recv()
    move(right_s, 0, 2, 16, sib).wait_recv()
    stage([(left, 2, 2), (right, 0, 2), (left_s, 2, 2), (right_s, 0, 2)])

    move(far, 0, 1, 9, right).wait_recv()
    move(far, 3, 1, 12, left).wait_recv()
    start([move(far, 0, 1, 17, sib), move(far, 3, 1, 18, sib)])
    move(far_s, 0, 1, 17, sib).wait_recv()
    move(far_s, 3, 1, 18, sib).wait_recv()
    stage([(far, 0, 1), (far, 3, 1), (far_s, 0, 1), (far_s, 3, 1)])

    move(far, 1, 1, 10, right).wait_recv()
    move(far, 2, 1, 11, left).wait_recv()
    start([move(far, 1, 2, 19, sib)])
    move(far_s, 1, 2, 19, sib).wait_recv()
    stage([(far, 1, 2), (far_s, 1, 2)])

    tile1 = 128
    lane1 = lax.broadcasted_iota(jnp.int32, (tile1, 128), 1)
    row1 = lax.broadcasted_iota(jnp.int32, (tile1, 128), 0)
    first1 = lane1 < HD
    pick1 = lax.rem(lane1, HD) == lax.rem(row1, per)
    for t in range(nlat // tile1):
        at0 = pl.ds(t * tile1, tile1)
        at1 = pl.ds(nlat + t * tile1, tile1)
        o0, o1 = om[at0, :], om[at1, :]
        total = pltpu.roll(jnp.where(first1, o1, o0), HD, 1)
        r1s[at0, :] = (jnp.where(first1, o0, o1) / total).astype(BF)
        lse = jnp.where(first1, mm[at0, :], mm[at1, :]) * SCALE2 + jnp.log2(total)
        lse = jnp.where(pick1, lse, 0.0)
        for g in range(tile1 // per):
            r1t[t * (tile1 // per) + g] = jnp.sum(
                lse[g * per : (g + 1) * per, :], axis=0, keepdims=True
            )

    own_c = pl.ds(aligned(c * per, 16), per)
    ny = 4
    nz = nc // ny
    zs = [lax.rem(c // ny + d, nz) * ny for d in range(nz)]
    ys = [lax.rem(lax.rem(c, ny) + d, ny) for d in range(ny)]
    steps = sorted(
        ((dz, dy) for dz in range(nz) for dy in range(ny) if dz or dy),
        key=lambda d: -(min(d[0], nz - d[0]) + min(d[1], ny - d[1])),
    )
    others = [zs[dz] + ys[dy] for dz, dy in steps]

    def to_ctx(src, dst, s, r):
        for to in others:
            pltpu.make_async_remote_copy(
                src_ref=src(to),
                dst_ref=dst,
                send_sem=xs.at[s],
                recv_sem=xr.at[r],
                device_id={"ctx": to},
                device_id_type=MESH,
            ).start()

    def spread(i, src, dst):
        to_ctx(lambda to: src.at[pl.ds(aligned(to * per, 16), per), :], dst.at[own_c, :], i, i)

    def await_bytes(ref, sem):
        pltpu.make_async_copy(ref, ref, sem).wait()

    rest = pl.ds(0, (nc - 1) * per)
    to_ctx(lambda to: r1t.at[to], r1u.at[c], 1, 1)
    spread(0, r1s, r1r)
    r1r[own_c, :] = r1s[own_c, :]
    r1u[c] = r1t[c]

    def rim(src, dst, sem, to):
        return pltpu.make_async_remote_copy(
            src_ref=KV.at[:, pl.ds(src, RIM), :],
            dst_ref=KV.at[:, pl.ds(dst, RIM), :],
            send_sem=xs.at[sem],
            recv_sem=xr.at[sem],
            device_id={"ctx": to},
            device_id_type=MESH,
        )

    rims = [
        rim(RIM, RIM + gtok, 2, lax.rem(c + nc - 1, nc)),
        rim(gtok, 0, 3, lax.rem(c + 1, nc)),
    ]
    for r in rims:
        r.start()
    pending += [r.wait_send for r in rims]
    pending += [lambda: await_bytes(r1r.at[rest, :], xs.at[0])]
    pending += [lambda: await_bytes(r1u.at[pl.ds(0, nc - 1)], xs.at[1])]

    firstb = lax.broadcasted_iota(jnp.int32, (BLK, 128), 1) < HD

    def attend(b):
        at = pl.ds(aligned(b * BLK, BLK), BLK)
        win = pl.ds(aligned(b * BLK, BLK), WIN * BLK)
        q = jnp.concatenate([Q[0, at, :], Q[1, at, :]], axis=0)
        s = lax.dot_general(
            q, KV[0, win, :], (((1,), (1,)), ((), ())), preferred_element_type=F32
        )
        parts = [
            s[:, j * BLK : (j + 1) * BLK] + biasr[j, pl.ds(b, 1), :] for j in range(WIN)
        ]
        top = parts[0]
        for part in parts[1:]:
            top = jnp.maximum(top, part)
        top = jnp.max(top, axis=1, keepdims=True)
        p = jnp.concatenate(
            [
                (jnp.exp2((part - top) * SCALE2) * multr[j, pl.ds(b, 1), :]).astype(BF)
                for j, part in enumerate(parts)
            ],
            axis=1,
        )
        o0 = jnp.dot(p[:BLK], KV[1, win, :], preferred_element_type=F32)
        o1 = jnp.dot(p[BLK:], KV[2, win, :], preferred_element_type=F32)
        total = pltpu.roll(jnp.where(firstb, o1, o0), HD, 1)
        A[at, :] = (jnp.where(firstb, o0, o1) / total).astype(BF)

    def attend_four(i, carry):
        for j in range(4):
            attend(2 + 4 * i + j)
        return carry

    lax.fori_loop(0, (nblk - 4) // 4, attend_four, 0)

    await_bytes(r1r.at[rest, :], xr.at[0])
    await_bytes(r1u.at[pl.ds(0, nc - 1)], xr.at[1])
    lanes = lax.broadcasted_iota(jnp.int32, (per, 128), 1)
    pick = lax.rem(lanes, HD) == lax.broadcasted_iota(jnp.int32, (per, 128), 0)
    for i in range(nc):
        fA[pl.ds(i * per, per), :] = jnp.where(pick, r1u[i], 0.0)
    same = (
        lax.broadcasted_iota(jnp.int32, (128, 128), 0) // HD
        == lax.broadcasted_iota(jnp.int32, (128, 128), 1) // HD
    )
    fB[...] = jnp.dot(
        fA[...],
        jnp.where(same, 1.0, 0.0),
        preferred_element_type=F32,
        precision=lax.Precision.HIGHEST,
    )
    peak = fB[pl.ds(0, per), :]
    for i in range(1, nc):
        peak = jnp.maximum(peak, fB[pl.ds(i * per, per), :])
    weight = jnp.zeros((per, 128), F32)
    value = jnp.zeros((per, 128), F32)
    for i in range(nc):
        w = jnp.exp2(fB[pl.ds(i * per, per), :] - peak)
        weight += w
        value += w * r1r[pl.ds(i * per, per), :].astype(F32)
    lat_att = (value / weight).astype(BF)

    loads[6].wait()
    made = jnp.dot(lat_att, wlo[...], preferred_element_type=F32)
    for j in range(nk):
        r2s[pl.ds(j, per, stride=nk), :] = made[:, j * 128 : (j + 1) * 128]
    rest2 = pl.ds(0, (nh - 1) * two * nk)
    own_h = pl.ds(aligned(h * two * nk, 16), two * nk)

    def send2(d, carry):
        to = lax.rem(h + d, nh)
        pltpu.make_async_remote_copy(
            src_ref=r2s.at[pl.ds(aligned(to * two * nk, 16), two * nk), :],
            dst_ref=r2r.at[own_h, :],
            send_sem=xs.at[4],
            recv_sem=xr.at[4],
            device_id={"heads": to},
            device_id_type=MESH,
        ).start()
        return carry

    lax.fori_loop(1, nh, send2, 0)
    r2r[own_h, :] = r2s[own_h, :]
    pending += [lambda: await_bytes(r2r.at[rest2, :], xs.at[4])]

    for r in rims:
        r.wait_recv()
    for b in (0, 1, nblk - 2, nblk - 1):
        attend(b)

    await_bytes(r2r.at[rest2, :], xr.at[4])
    hidden = hl[...]
    for i in range(nh):
        hidden += r2r[pl.ds(i * two * nk, two * nk), :]
    hl[...] = hidden
    for i in range(two):
        row = hidden[i * nk : (i + 1) * nk, :]
        center = jnp.sum(jnp.sum(row, axis=0, keepdims=True), axis=1, keepdims=True) / dw
        off = row - center
        spread2 = (
            jnp.sum(jnp.sum(jnp.square(off), axis=0, keepdims=True), axis=1, keepdims=True) / dw
        )
        f2[pl.ds(i * nk, nk), :] = off * lax.rsqrt(spread2 + EPSILON) * mg_ref[...]
    r3s[...] = f2[...].astype(BF)
    to_ctx(lambda to: r3s, r3r.at[own_c, :], 5, 5)
    r3r[own_c, :] = r3s[...]
    pending += [lambda: await_bytes(r3r.at[rest, :], xs.at[5])]

    head_cols = pl.ds(aligned(h * 128, 128), 128)

    def send_back(d, carry):
        to = lax.rem(h + d, nh)
        pltpu.make_async_remote_copy(
            src_ref=A.at[pl.ds(aligned(to * nrow, 128), nrow), :],
            dst_ref=R.at[:, head_cols],
            send_sem=xs.at[6],
            recv_sem=xr.at[6],
            device_id={"heads": to},
            device_id_type=MESH,
        ).start()
        return carry

    lax.fori_loop(1, nh, send_back, 0)
    R[:, head_cols] = A[pl.ds(mine, nrow), :]
    pending += [lambda: await_bytes(A.at[pl.ds(0, (nh - 1) * nrow), :], xs.at[6])]

    loads[7].wait()
    loads[8].wait()
    await_bytes(r3r.at[rest, :], xr.at[5])
    fA[...] = r3r[...].astype(F32)
    rows = jnp.concatenate(
        [fA[pl.ds(j, share, stride=nk), :].astype(BF) for j in range(nk)], axis=1
    )
    inner = jax.nn.gelu(
        jnp.dot(rows, wup[...], preferred_element_type=F32), approximate=True
    ).astype(BF)
    made = jnp.dot(inner, wdn[...], preferred_element_type=F32)
    for j in range(nk):
        fB[pl.ds(j, share, stride=nk), :] = made[:, j * 128 : (j + 1) * 128]
    r4s[...] = fB[...].astype(BF)
    spread(7, r4s, r4r)
    r4r[own_c, :] = r4s[own_c, :]
    pending += [lambda: await_bytes(r4r.at[rest, :], xs.at[7])]

    loads[9].wait()
    await_bytes(A.at[pl.ds(0, (nh - 1) * nrow), :], xr.at[6])

    def project_out(n, carry):
        cols = pl.ds(aligned(n * 256, 256), 256)
        tout_ref[:, cols] = (
            tok[:, cols].astype(F32)
            + jnp.dot(R[...], wout[:, cols], preferred_element_type=F32)
        ).astype(BF)
        return carry

    lax.fori_loop(0, dw // 256, project_out, 0)

    await_bytes(r4r.at[rest, :], xr.at[7])
    total = hl[...]
    for i in range(nc):
        total += r4r[pl.ds(i * per, per), :].astype(F32)
    r5s[...] = total.astype(BF)
    to_ctx(lambda to: r5s, r5r.at[own_c, :], 8, 8)
    r5r[own_c, :] = r5s[...]
    pending += [lambda: await_bytes(r5r.at[rest, :], xs.at[8])]
    await_bytes(r5r.at[rest, :], xr.at[8])
    fA[...] = r5r[...].astype(F32)
    for j in range(nk):
        lout_ref[:, j * 128 : (j + 1) * 128] = fA[pl.ds(j, share, stride=nk), :].astype(BF)

    for done in pending:
        done()


def per_device(
    nh,
    nc,
    tokens,
    ln_gain,
    w_qkv,
    w_out,
    neighbours,
    counts,
    latents,
    lat_gain,
    w_lat_q,
    w_lat_o,
    mlp_gain,
    w_up,
    w_down,
):
    nrow, dw = tokens.shape[1:]
    nlat = latents.shape[0]
    gtok = nrow * nh
    per = nlat // nc
    share = nlat // nh
    nblk = gtok // BLK
    two = share // nc * (dw // 128)
    hbm = pl.BlockSpec(memory_space=pltpu.HBM)
    vmem = pl.BlockSpec(memory_space=pltpu.VMEM)
    stage = gtok // 4
    scratch = [
        pltpu.VMEM((1, dw), F32),
        pltpu.VMEM((neighbours.shape[2], nblk), jnp.int32),
        pltpu.VMEM((1, nblk), jnp.int32),
        pltpu.VMEM((1, dw), F32),
        pltpu.VMEM((dw // 128, 128), F32),
        pltpu.VMEM((nrow, dw), BF),
        pltpu.VMEM((dw, 384), BF),
        pltpu.VMEM((dw, dw), BF),
        pltpu.VMEM((nlat, dw), BF),
        pltpu.VMEM((dw, 128), BF),
        pltpu.VMEM((128, dw), BF),
        pltpu.VMEM(w_up.shape, BF),
        pltpu.VMEM(w_down.shape, BF),
        pltpu.VMEM((gtok, dw), BF),
        pltpu.VMEM((nlat, dw), BF),
        pltpu.VMEM((2, gtok, 128), BF),
        pltpu.VMEM((3, gtok + 2 * RIM, 128), BF),
        pltpu.VMEM((stage, 128), BF),
        pltpu.VMEM((2, stage, 128), BF),
        pltpu.VMEM((nlat, 128), F32),
        pltpu.VMEM((nlat, 128), F32),
        pltpu.VMEM((two, 128), F32),
        pltpu.VMEM((2 * nlat, 128), BF),
        pltpu.VMEM((2 * nlat, 128), F32),
        pltpu.VMEM((2 * nlat, 128), F32),
        pltpu.VMEM((two, 128), F32),
        pltpu.VMEM((WIN, nblk, 128), F32),
        pltpu.VMEM((WIN, nblk, 128), F32),
        pltpu.VMEM((nlat, 128), BF),
        pltpu.VMEM((nc, 1, 128), F32),
        pltpu.VMEM((nlat, 128), BF),
        pltpu.VMEM((nc, 1, 128), F32),
        pltpu.VMEM((nh * two, 128), F32),
        pltpu.VMEM((nh * two, 128), F32),
        pltpu.VMEM((two, 128), BF),
        pltpu.VMEM((nlat, 128), BF),
        pltpu.VMEM((nlat, 128), BF),
        pltpu.VMEM((nlat, 128), BF),
        pltpu.VMEM((two, 128), BF),
        pltpu.VMEM((nlat, 128), BF),
        pltpu.VMEM((gtok, 128), BF),
        pltpu.VMEM((nrow, dw), BF),
        pltpu.SemaphoreType.DMA((15,)),
        pltpu.SemaphoreType.DMA((20,)),
        pltpu.SemaphoreType.DMA((20,)),
        pltpu.SemaphoreType.DMA((9,)),
        pltpu.SemaphoreType.DMA((9,)),
    ]
    tokens_out, latents_out = pl.pallas_call(
        functools.partial(kernel, nh, nc),
        out_shape=(
            jax.ShapeDtypeStruct((nrow, dw), BF),
            jax.ShapeDtypeStruct((share, dw), BF),
        ),
        in_specs=[hbm] * 13,
        out_specs=(vmem, vmem),
        scratch_shapes=scratch,
        compiler_params=pltpu.CompilerParams(
            collective_id=0, has_side_effects=True, vmem_limit_bytes=60 * 1024 * 1024
        ),
        name="encoder_block",
    )(
        tokens[0],
        ln_gain.reshape(1, dw),
        jnp.transpose(w_qkv, (1, 0, 2)),
        w_out,
        neighbours[0].T,
        counts,
        latents,
        lat_gain.reshape(1, dw),
        w_lat_q,
        w_lat_o,
        mlp_gain.reshape(dw // 128, 128),
        w_up,
        w_down,
    )
    return (tokens_out[None], latents_out)


def solution(mesh):
    in_specs = (
        P("ctx", "heads", None),
        P(),
        P(None, None, "heads"),
        P(),
        P("ctx", None, None),
        P("ctx", None),
        P(),
        P(),
        P(None, "heads"),
        P("heads", None),
        P(),
        P(None, "ctx"),
        P("ctx", None),
    )
    out_specs = (P("ctx", "heads", None), P("heads", None))
    return jax.shard_map(
        functools.partial(per_device, mesh.shape["heads"], mesh.shape["ctx"]),
        mesh=mesh,
        in_specs=in_specs,
        out_specs=out_specs,
        check_vma=False,
    )
```

```python
import functools

import jax
import jax.numpy as jnp
from jax import lax
from jax.experimental import pallas as pl
from jax.experimental.pallas import tpu as pltpu
from jax.sharding import PartitionSpec as P

HD = 64
BLK = 128
WIN = 5
RIM = 256
EPSILON = 1e-05
SCALE2 = HD ** (-0.5) * 1.4426950408889634
MESH = pl.DeviceIdType.MESH
BF = jnp.bfloat16
F32 = jnp.float32


def aligned(start, by):
    return pl.multiple_of(start, by)


def normalise(rows, gain):
    center = jnp.mean(rows, axis=-1, keepdims=True)
    spread = jnp.mean(jnp.square(rows - center), axis=-1, keepdims=True)
    return (rows - center) * lax.rsqrt(spread + EPSILON) * gain


def kernel(
    nh,
    nc,
    tok_hbm,
    lng_hbm,
    wqkv_hbm,
    wout_hbm,
    nb_hbm,
    cnt_hbm,
    lat_hbm,
    latg_hbm,
    wlq_hbm,
    wlo_hbm,
    mg_hbm,
    wup_hbm,
    wdn_hbm,
    tout_ref,
    lout_ref,
    lng_ref,
    nb_ref,
    cnt_ref,
    latg_ref,
    mg_ref,
    tok,
    wqkv,
    wout,
    lat,
    wlq,
    wlo,
    wup,
    wdn,
    G,
    latn,
    Q,
    KV,
    kst,
    vst,
    fA,
    fB,
    f2,
    qlat,
    om,
    mm,
    hl,
    multr,
    biasr,
    r1s,
    r1t,
    r1r,
    r1u,
    r2s,
    r2r,
    r3s,
    r3r,
    r4s,
    r4r,
    r5s,
    r5r,
    A,
    R,
    in_sem,
    gs,
    gr,
    xs,
    xr,
    row_sem,
    go_sem,
):
    h = lax.axis_index("heads")
    c = lax.axis_index("ctx")
    x = h // 2
    k = h % 2
    nrow = tok.shape[0]
    nlat = lat.shape[0]
    dw = tok.shape[1]
    nk = dw // 128
    gtok = nh * nrow
    nblk = gtok // BLK
    per = nlat // nc

    loads = [
        pltpu.make_async_copy(tok_hbm, tok, in_sem.at[0]),
        pltpu.make_async_copy(lat_hbm, lat, in_sem.at[1]),
        pltpu.make_async_copy(wlq_hbm, wlq, in_sem.at[2]),
        pltpu.make_async_copy(wqkv_hbm.at[0], wqkv.at[:, pl.ds(0, 128)], in_sem.at[3]),
        pltpu.make_async_copy(wqkv_hbm.at[1], wqkv.at[:, pl.ds(128, 128)], in_sem.at[4]),
        pltpu.make_async_copy(wqkv_hbm.at[2], wqkv.at[:, pl.ds(256, 128)], in_sem.at[5]),
        pltpu.make_async_copy(wlo_hbm, wlo, in_sem.at[6]),
        pltpu.make_async_copy(wup_hbm, wup, in_sem.at[7]),
        pltpu.make_async_copy(wdn_hbm, wdn, in_sem.at[8]),
        pltpu.make_async_copy(wout_hbm, wout, in_sem.at[9]),
    ]
    small = [
        pltpu.make_async_copy(lng_hbm, lng_ref, in_sem.at[10]),
        pltpu.make_async_copy(latg_hbm, latg_ref, in_sem.at[11]),
        pltpu.make_async_copy(nb_hbm, nb_ref, in_sem.at[12]),
        pltpu.make_async_copy(cnt_hbm, cnt_ref, in_sem.at[13]),
        pltpu.make_async_copy(mg_hbm, mg_ref, in_sem.at[14]),
    ]
    small[0].start()
    for load in loads[:3] + small[1:] + loads[3:]:
        load.start()

    barrier = pltpu.get_barrier_semaphore()

    def signal(sem, **to):
        pl.semaphore_signal(sem, inc=1, device_id=to, device_id_type=MESH)

    for d in range(1, nh):
        @pl.when(h != d)
        def _(d=d):
            signal(barrier, heads=d)

    loads[0].wait()
    small[0].wait()
    mine = aligned(h * nrow, 256)
    step = 32

    def norm_tokens(i, carry):
        at = pl.ds(aligned(i * step, step), step)
        G[pl.ds(aligned(mine + i * step, step), step), :] = normalise(
            tok[at, :].astype(F32), lng_ref[...]
        ).astype(BF)
        return carry

    lax.fori_loop(0, nrow // step, norm_tokens, 0)

    @pl.when(h != 0)
    def _():
        pl.semaphore_wait(barrier, nh - 1)

    @pl.when(h == 1)
    def _():
        signal(row_sem, heads=0)

    @pl.when(h == 0)
    def _():
        pl.semaphore_wait(row_sem, 1)


    sib = x * 2 + (1 - k)
    right = lax.rem(x + 1, nh // 2) * 2 + k
    left = lax.rem(x + nh // 2 - 1, nh // 2) * 2 + k
    far = lax.rem(x + 2, nh // 2) * 2 + k
    right_s = lax.rem(x + 1, nh // 2) * 2 + (1 - k)
    left_s = lax.rem(x + nh // 2 - 1, nh // 2) * 2 + (1 - k)
    far_s = lax.rem(x + 2, nh // 2) * 2 + (1 - k)

    quarter = nrow // 4

    def move(block, part, parts, sem, to):
        rows = pl.ds(aligned(block * nrow + part * quarter, quarter), parts * quarter)
        return pltpu.make_async_remote_copy(
            src_ref=G.at[rows, :],
            dst_ref=G.at[rows, :],
            send_sem=gs.at[sem],
            recv_sem=gr.at[sem],
            device_id={"heads": to},
            device_id_type=MESH,
        )

    pending = []
    sends = []
    for i in range(4):
        sends += [move(h, i, 1, 1 + i, right), move(h, 3 - i, 1, 8 - i, left)]
        if i == 1:
            sends += [move(h, 0, 4, 0, sib)]
    for send in sends:
        send.start()
    pending += [send.wait_send for send in sends]

    ny = 4
    nz = nc // ny
    zs = [lax.rem(c // ny + d, nz) * ny for d in range(nz)]
    ys = [lax.rem(lax.rem(c, ny) + d, ny) for d in range(ny)]
    steps = sorted(
        ((dz, dy) for dz in range(nz) for dy in range(ny) if dz or dy),
        key=lambda d: -(min(d[0], nz - d[0]) + min(d[1], ny - d[1])),
    )
    others = [zs[dz] + ys[dy] for dz, dy in steps]

    @pl.when(h == 0)
    def _():
        for to in others:
            signal(barrier, ctx=to)


    loads[1].wait()
    for load in small[1:]:
        load.wait()

    def norm_latents(i, carry):
        at = pl.ds(aligned(i * step, step), step)
        latn[at, :] = normalise(lat[at, :].astype(F32), latg_ref[...]).astype(BF)
        return carry

    lax.fori_loop(0, nlat // step, norm_latents, 0)
    loads[2].wait()
    fA[...] = jnp.dot(latn[...], wlq[...], preferred_element_type=F32)
    share = nlat // nh
    two = share // nc
    for hh in range(nh):
        for i in range(two):
            fB[pl.ds(hh * two + i, nc, stride=per), :] = fA[
                pl.ds(hh * share + i, nc, stride=two), :
            ]
    lane = lax.broadcasted_iota(jnp.int32, (nlat, 128), 1)
    lq = fB[...]
    qlat[pl.ds(0, nlat), :] = jnp.where(lane < HD, lq, 0.0).astype(BF)
    qlat[pl.ds(nlat, nlat), :] = jnp.where(lane < HD, 0.0, lq).astype(BF)
    om[...] = jnp.zeros_like(om)
    mm[...] = jnp.full_like(mm, -jnp.inf)

    own64 = lat[pl.ds(aligned(h * share, share), share), :].astype(F32)
    for j in range(nk):
        fA[pl.ds(j, share, stride=nk), :] = own64[:, j * 128 : (j + 1) * 128]
    hl[...] = fA[pl.ds(aligned(c * two * nk, two * nk), two * nk), :]

    slot = lax.broadcasted_iota(jnp.int32, nb_ref.shape, 0)
    column = lax.broadcasted_iota(jnp.int32, nb_ref.shape, 1)
    live = slot < cnt_ref[...]
    eye = lax.broadcasted_iota(jnp.int32, (nblk, nblk), 0) == lax.broadcasted_iota(
        jnp.int32, (nblk, nblk), 1
    )
    for j in range(WIN):
        hits = jnp.where(live & (nb_ref[...] == column + j), 1.0, 0.0)
        times = jnp.sum(hits, axis=0, keepdims=True)
        times = jnp.sum(jnp.where(eye, times, 0.0), axis=1, keepdims=True)
        times = jnp.broadcast_to(times, (nblk, 128))
        multr[j] = times
        biasr[j] = jnp.where(times > 0.0, 0.0, -jnp.inf)

    def project(pieces):
        spans = [
            (aligned(block * nrow + part * quarter, quarter), parts * quarter)
            for block, part, parts in pieces
        ]
        rows = jnp.concatenate([G[pl.ds(s, size), :] for s, size in spans], axis=0)
        made = jnp.dot(rows, wqkv[...], preferred_element_type=F32)
        at = 0
        for s, size in spans:
            part = slice(at, at + size)
            at += size
            first = lax.broadcasted_iota(jnp.int32, (size, 128), 1) < HD
            q = made[part, 0:128]
            key = made[part, 128:256].astype(BF)
            v = made[part, 256:384]
            v0 = jnp.where(first, v, 1.0).astype(BF)
            v1 = jnp.where(first, 1.0, v).astype(BF)
            Q[0, pl.ds(s, size), :] = jnp.where(first, q, 0.0).astype(BF)
            Q[1, pl.ds(s, size), :] = jnp.where(first, 0.0, q).astype(BF)
            wide = pl.ds(aligned(s + RIM, quarter), size)
            KV[0, wide, :] = key
            KV[1, wide, :] = v0
            KV[2, wide, :] = v1
            kst[part, :] = key
            vst[0, part, :] = v0
            vst[1, part, :] = v1
        return at

    def cross(keys, t):
        at = pl.ds(t * nlat, nlat)
        s = lax.dot_general(
            qlat[at, :],
            kst[pl.ds(0, keys), :],
            (((1,), (1,)), ((), ())),
            preferred_element_type=F32,
        )
        before = mm[at, :]
        top = jnp.maximum(before, jnp.max(s, axis=1, keepdims=True))
        alpha = jnp.exp2((before - top) * SCALE2)
        p = jnp.concatenate(
            [
                jnp.exp2((s[:, j * 128 : (j + 1) * 128] - top) * SCALE2).astype(BF)
                for j in range(keys // 128)
            ],
            axis=1,
        )
        mm[at, :] = top
        om[at, :] = om[at, :] * alpha + jnp.dot(
            p, vst[t, pl.ds(0, keys), :], preferred_element_type=F32
        )

    def stage(pieces):
        keys = project(pieces)
        for t in range(2):
            cross(keys, t)

    def start(copies):
        for copy in copies:
            copy.start()
        pending.extend([copy.wait_send for copy in copies])

    move(left, 0, 1, 1, right).wait_recv()
    move(right, 3, 1, 8, left).wait_recv()
    start([move(left, 0, 1, 9, right), move(right, 3, 1, 12, left)])
    for i in (3, 4, 5):
        loads[i].wait()
    move(sib, 0, 4, 0, sib).wait_recv()
    stage([(h, 0, 4), (sib, 0, 4)])

    move(left, 1, 1, 2, right).wait_recv()
    move(right, 2, 1, 7, left).wait_recv()
    start([move(left, 1, 1, 10, right), move(right, 2, 1, 11, left)])
    start([move(left, 0, 2, 13, sib), move(right, 2, 2, 14, sib)])
    move(left_s, 0, 2, 13, sib).wait_recv()
    move(right_s, 2, 2, 14, sib).wait_recv()
    stage([(left, 0, 2), (right, 2, 2), (left_s, 0, 2), (right_s, 2, 2)])

    for i in (2, 3):
        move(left, i, 1, 1 + i, right).wait_recv()
        move(right, 3 - i, 1, 8 - i, left).wait_recv()
    start([move(left, 2, 2, 15, sib), move(right, 0, 2, 16, sib)])
    move(left_s, 2, 2, 15, sib).wait_recv()
    move(right_s, 0, 2, 16, sib).wait_recv()
    stage([(left, 2, 2), (right, 0, 2), (left_s, 2, 2), (right_s, 0, 2)])

    @pl.when(h == 0)
    def _():
        pl.semaphore_wait(barrier, nc - 1)
        for d in range(1, nh):
            signal(go_sem, heads=d)


    move(far, 0, 1, 9, right).wait_recv()
    move(far, 3, 1, 12, left).wait_recv()
    start([move(far, 0, 1, 17, sib), move(far, 3, 1, 18, sib)])
    move(far_s, 0, 1, 17, sib).wait_recv()
    move(far_s, 3, 1, 18, sib).wait_recv()
    stage([(far, 0, 1), (far, 3, 1), (far_s, 0, 1), (far_s, 3, 1)])

    move(far, 1, 1, 10, right).wait_recv()
    move(far, 2, 1, 11, left).wait_recv()
    start([move(far, 1, 2, 19, sib)])
    move(far_s, 1, 2, 19, sib).wait_recv()
    stage([(far, 1, 2), (far_s, 1, 2)])

    @pl.when(h != 0)
    def _():
        pl.semaphore_wait(go_sem, 1)


    tile1 = 128
    lane1 = lax.broadcasted_iota(jnp.int32, (tile1, 128), 1)
    row1 = lax.broadcasted_iota(jnp.int32, (tile1, 128), 0)
    first1 = lane1 < HD
    pick1 = lax.rem(lane1, HD) == lax.rem(row1, per)
    for t in range(nlat // tile1):
        at0 = pl.ds(t * tile1, tile1)
        at1 = pl.ds(nlat + t * tile1, tile1)
        o0, o1 = om[at0, :], om[at1, :]
        total = pltpu.roll(jnp.where(first1, o1, o0), HD, 1)
        r1s[at0, :] = (jnp.where(first1, o0, o1) / total).astype(BF)
        lse = jnp.where(first1, mm[at0, :], mm[at1, :]) * SCALE2 + jnp.log2(total)
        lse = jnp.where(pick1, lse, 0.0)
        for g in range(tile1 // per):
            r1t[t * (tile1 // per) + g] = jnp.sum(
                lse[g * per : (g + 1) * per, :], axis=0, keepdims=True
            )

    own_c = pl.ds(aligned(c * per, 16), per)
    def to_ctx(src, dst, s, r):
        for to in others:
            pltpu.make_async_remote_copy(
                src_ref=src(to),
                dst_ref=dst,
                send_sem=xs.at[s],
                recv_sem=xr.at[r],
                device_id={"ctx": to},
                device_id_type=MESH,
            ).start()

    def spread(i, src, dst):
        to_ctx(lambda to: src.at[pl.ds(aligned(to * per, 16), per), :], dst.at[own_c, :], i, i)

    def await_bytes(ref, sem):
        pltpu.make_async_copy(ref, ref, sem).wait()

    rest = pl.ds(0, (nc - 1) * per)
    to_ctx(lambda to: r1t.at[to], r1u.at[c], 1, 1)
    spread(0, r1s, r1r)
    r1r[own_c, :] = r1s[own_c, :]
    r1u[c] = r1t[c]

    def rim(src, dst, sem, to):
        return pltpu.make_async_remote_copy(
            src_ref=KV.at[:, pl.ds(src, RIM), :],
            dst_ref=KV.at[:, pl.ds(dst, RIM), :],
            send_sem=xs.at[sem],
            recv_sem=xr.at[sem],
            device_id={"ctx": to},
            device_id_type=MESH,
        )

    rims = [
        rim(RIM, RIM + gtok, 2, lax.rem(c + nc - 1, nc)),
        rim(gtok, 0, 3, lax.rem(c + 1, nc)),
    ]
    for r in rims:
        r.start()
    pending += [r.wait_send for r in rims]
    pending += [lambda: await_bytes(r1r.at[rest, :], xs.at[0])]
    pending += [lambda: await_bytes(r1u.at[pl.ds(0, nc - 1)], xs.at[1])]

    firstb = lax.broadcasted_iota(jnp.int32, (BLK, 128), 1) < HD

    def attend(b):
        at = pl.ds(aligned(b * BLK, BLK), BLK)
        win = pl.ds(aligned(b * BLK, BLK), WIN * BLK)
        q = jnp.concatenate([Q[0, at, :], Q[1, at, :]], axis=0)
        s = lax.dot_general(
            q, KV[0, win, :], (((1,), (1,)), ((), ())), preferred_element_type=F32
        )
        parts = [
            s[:, j * BLK : (j + 1) * BLK] + biasr[j, pl.ds(b, 1), :] for j in range(WIN)
        ]
        top = parts[0]
        for part in parts[1:]:
            top = jnp.maximum(top, part)
        top = jnp.max(top, axis=1, keepdims=True)
        p = jnp.concatenate(
            [
                (jnp.exp2((part - top) * SCALE2) * multr[j, pl.ds(b, 1), :]).astype(BF)
                for j, part in enumerate(parts)
            ],
            axis=1,
        )
        o0 = jnp.dot(p[:BLK], KV[1, win, :], preferred_element_type=F32)
        o1 = jnp.dot(p[BLK:], KV[2, win, :], preferred_element_type=F32)
        total = pltpu.roll(jnp.where(firstb, o1, o0), HD, 1)
        A[at, :] = (jnp.where(firstb, o0, o1) / total).astype(BF)

    def attend_four(i, carry):
        for j in range(4):
            attend(2 + 4 * i + j)
        return carry

    lax.fori_loop(0, (nblk - 4) // 4, attend_four, 0)

    await_bytes(r1r.at[rest, :], xr.at[0])
    await_bytes(r1u.at[pl.ds(0, nc - 1)], xr.at[1])
    lanes = lax.broadcasted_iota(jnp.int32, (per, 128), 1)
    pick = lax.rem(lanes, HD) == lax.broadcasted_iota(jnp.int32, (per, 128), 0)
    for i in range(nc):
        fA[pl.ds(i * per, per), :] = jnp.where(pick, r1u[i], 0.0)
    same = (
        lax.broadcasted_iota(jnp.int32, (128, 128), 0) // HD
        == lax.broadcasted_iota(jnp.int32, (128, 128), 1) // HD
    )
    fB[...] = jnp.dot(
        fA[...],
        jnp.where(same, 1.0, 0.0),
        preferred_element_type=F32,
        precision=lax.Precision.HIGHEST,
    )
    peak = fB[pl.ds(0, per), :]
    for i in range(1, nc):
        peak = jnp.maximum(peak, fB[pl.ds(i * per, per), :])
    weight = jnp.zeros((per, 128), F32)
    value = jnp.zeros((per, 128), F32)
    for i in range(nc):
        w = jnp.exp2(fB[pl.ds(i * per, per), :] - peak)
        weight += w
        value += w * r1r[pl.ds(i * per, per), :].astype(F32)
    lat_att = (value / weight).astype(BF)

    loads[6].wait()
    made = jnp.dot(lat_att, wlo[...], preferred_element_type=F32)
    for j in range(nk):
        r2s[pl.ds(j, per, stride=nk), :] = made[:, j * 128 : (j + 1) * 128]
    rest2 = pl.ds(0, (nh - 1) * two * nk)
    own_h = pl.ds(aligned(h * two * nk, 16), two * nk)

    def send2(d, carry):
        to = lax.rem(h + d, nh)
        pltpu.make_async_remote_copy(
            src_ref=r2s.at[pl.ds(aligned(to * two * nk, 16), two * nk), :],
            dst_ref=r2r.at[own_h, :],
            send_sem=xs.at[4],
            recv_sem=xr.at[4],
            device_id={"heads": to},
            device_id_type=MESH,
        ).start()
        return carry

    lax.fori_loop(1, nh, send2, 0)
    r2r[own_h, :] = r2s[own_h, :]
    pending += [lambda: await_bytes(r2r.at[rest2, :], xs.at[4])]

    for r in rims:
        r.wait_recv()
    for b in (0, 1, nblk - 2, nblk - 1):
        attend(b)

    await_bytes(r2r.at[rest2, :], xr.at[4])
    hidden = hl[...]
    for i in range(nh):
        hidden += r2r[pl.ds(i * two * nk, two * nk), :]
    hl[...] = hidden
    for i in range(two):
        row = hidden[i * nk : (i + 1) * nk, :]
        center = jnp.sum(jnp.sum(row, axis=0, keepdims=True), axis=1, keepdims=True) / dw
        off = row - center
        spread2 = (
            jnp.sum(jnp.sum(jnp.square(off), axis=0, keepdims=True), axis=1, keepdims=True) / dw
        )
        f2[pl.ds(i * nk, nk), :] = off * lax.rsqrt(spread2 + EPSILON) * mg_ref[...]
    r3s[...] = f2[...].astype(BF)
    to_ctx(lambda to: r3s, r3r.at[own_c, :], 5, 5)
    r3r[own_c, :] = r3s[...]
    pending += [lambda: await_bytes(r3r.at[rest, :], xs.at[5])]

    head_cols = pl.ds(aligned(h * 128, 128), 128)

    def send_back(d, carry):
        to = lax.rem(h + d, nh)
        pltpu.make_async_remote_copy(
            src_ref=A.at[pl.ds(aligned(to * nrow, 128), nrow), :],
            dst_ref=R.at[:, head_cols],
            send_sem=xs.at[6],
            recv_sem=xr.at[6],
            device_id={"heads": to},
            device_id_type=MESH,
        ).start()
        return carry

    lax.fori_loop(1, nh, send_back, 0)
    R[:, head_cols] = A[pl.ds(mine, nrow), :]
    pending += [lambda: await_bytes(A.at[pl.ds(0, (nh - 1) * nrow), :], xs.at[6])]

    loads[7].wait()
    loads[8].wait()
    await_bytes(r3r.at[rest, :], xr.at[5])
    fA[...] = r3r[...].astype(F32)
    rows = jnp.concatenate(
        [fA[pl.ds(j, share, stride=nk), :].astype(BF) for j in range(nk)], axis=1
    )
    inner = jax.nn.gelu(
        jnp.dot(rows, wup[...], preferred_element_type=F32), approximate=True
    ).astype(BF)
    made = jnp.dot(inner, wdn[...], preferred_element_type=F32)
    for j in range(nk):
        fB[pl.ds(j, share, stride=nk), :] = made[:, j * 128 : (j + 1) * 128]
    r4s[...] = fB[...].astype(BF)
    spread(7, r4s, r4r)
    r4r[own_c, :] = r4s[own_c, :]
    pending += [lambda: await_bytes(r4r.at[rest, :], xs.at[7])]

    loads[9].wait()
    await_bytes(A.at[pl.ds(0, (nh - 1) * nrow), :], xr.at[6])

    def project_out(n, carry):
        cols = pl.ds(aligned(n * 256, 256), 256)
        tout_ref[:, cols] = (
            tok[:, cols].astype(F32)
            + jnp.dot(R[...], wout[:, cols], preferred_element_type=F32)
        ).astype(BF)
        return carry

    lax.fori_loop(0, dw // 256, project_out, 0)

    await_bytes(r4r.at[rest, :], xr.at[7])
    total = hl[...]
    for i in range(nc):
        total += r4r[pl.ds(i * per, per), :].astype(F32)
    r5s[...] = total.astype(BF)
    to_ctx(lambda to: r5s, r5r.at[own_c, :], 8, 8)
    r5r[own_c, :] = r5s[...]
    pending += [lambda: await_bytes(r5r.at[rest, :], xs.at[8])]
    await_bytes(r5r.at[rest, :], xr.at[8])
    fA[...] = r5r[...].astype(F32)
    for j in range(nk):
        lout_ref[:, j * 128 : (j + 1) * 128] = fA[pl.ds(j, share, stride=nk), :].astype(BF)

    for done in pending:
        done()


def per_device(
    nh,
    nc,
    tokens,
    ln_gain,
    w_qkv,
    w_out,
    neighbours,
    counts,
    latents,
    lat_gain,
    w_lat_q,
    w_lat_o,
    mlp_gain,
    w_up,
    w_down,
):
    nrow, dw = tokens.shape[1:]
    nlat = latents.shape[0]
    gtok = nrow * nh
    per = nlat // nc
    share = nlat // nh
    nblk = gtok // BLK
    two = share // nc * (dw // 128)
    hbm = pl.BlockSpec(memory_space=pltpu.HBM)
    vmem = pl.BlockSpec(memory_space=pltpu.VMEM)
    stage = gtok // 4
    scratch = [
        pltpu.VMEM((1, dw), F32),
        pltpu.VMEM((neighbours.shape[2], nblk), jnp.int32),
        pltpu.VMEM((1, nblk), jnp.int32),
        pltpu.VMEM((1, dw), F32),
        pltpu.VMEM((dw // 128, 128), F32),
        pltpu.VMEM((nrow, dw), BF),
        pltpu.VMEM((dw, 384), BF),
        pltpu.VMEM((dw, dw), BF),
        pltpu.VMEM((nlat, dw), BF),
        pltpu.VMEM((dw, 128), BF),
        pltpu.VMEM((128, dw), BF),
        pltpu.VMEM(w_up.shape, BF),
        pltpu.VMEM(w_down.shape, BF),
        pltpu.VMEM((gtok, dw), BF),
        pltpu.VMEM((nlat, dw), BF),
        pltpu.VMEM((2, gtok, 128), BF),
        pltpu.VMEM((3, gtok + 2 * RIM, 128), BF),
        pltpu.VMEM((stage, 128), BF),
        pltpu.VMEM((2, stage, 128), BF),
        pltpu.VMEM((nlat, 128), F32),
        pltpu.VMEM((nlat, 128), F32),
        pltpu.VMEM((two, 128), F32),
        pltpu.VMEM((2 * nlat, 128), BF),
        pltpu.VMEM((2 * nlat, 128), F32),
        pltpu.VMEM((2 * nlat, 128), F32),
        pltpu.VMEM((two, 128), F32),
        pltpu.VMEM((WIN, nblk, 128), F32),
        pltpu.VMEM((WIN, nblk, 128), F32),
        pltpu.VMEM((nlat, 128), BF),
        pltpu.VMEM((nc, 1, 128), F32),
        pltpu.VMEM((nlat, 128), BF),
        pltpu.VMEM((nc, 1, 128), F32),
        pltpu.VMEM((nh * two, 128), F32),
        pltpu.VMEM((nh * two, 128), F32),
        pltpu.VMEM((two, 128), BF),
        pltpu.VMEM((nlat, 128), BF),
        pltpu.VMEM((nlat, 128), BF),
        pltpu.VMEM((nlat, 128), BF),
        pltpu.VMEM((two, 128), BF),
        pltpu.VMEM((nlat, 128), BF),
        pltpu.VMEM((gtok, 128), BF),
        pltpu.VMEM((nrow, dw), BF),
        pltpu.SemaphoreType.DMA((15,)),
        pltpu.SemaphoreType.DMA((20,)),
        pltpu.SemaphoreType.DMA((20,)),
        pltpu.SemaphoreType.DMA((9,)),
        pltpu.SemaphoreType.DMA((9,)),
        pltpu.SemaphoreType.REGULAR,
        pltpu.SemaphoreType.REGULAR,
    ]
    tokens_out, latents_out = pl.pallas_call(
        functools.partial(kernel, nh, nc),
        out_shape=(
            jax.ShapeDtypeStruct((nrow, dw), BF),
            jax.ShapeDtypeStruct((share, dw), BF),
        ),
        in_specs=[hbm] * 13,
        out_specs=(vmem, vmem),
        scratch_shapes=scratch,
        compiler_params=pltpu.CompilerParams(
            collective_id=0, has_side_effects=True, vmem_limit_bytes=60 * 1024 * 1024
        ),
        name="encoder_block",
    )(
        tokens[0],
        ln_gain.reshape(1, dw),
        jnp.transpose(w_qkv, (1, 0, 2)),
        w_out,
        neighbours[0].T,
        counts,
        latents,
        lat_gain.reshape(1, dw),
        w_lat_q,
        w_lat_o,
        mlp_gain.reshape(dw // 128, 128),
        w_up,
        w_down,
    )
    return (tokens_out[None], latents_out)


def solution(mesh):
    in_specs = (
        P("ctx", "heads", None),
        P(),
        P(None, None, "heads"),
        P(),
        P("ctx", None, None),
        P("ctx", None),
        P(),
        P(),
        P(None, "heads"),
        P("heads", None),
        P(),
        P(None, "ctx"),
        P("ctx", None),
    )
    out_specs = (P("ctx", "heads", None), P("heads", None))
    return jax.shard_map(
        functools.partial(per_device, mesh.shape["heads"], mesh.shape["ctx"]),
        mesh=mesh,
        in_specs=in_specs,
        out_specs=out_specs,
        check_vma=False,
    )
```

```python
import functools

import jax
import jax.numpy as jnp
from jax import lax
from jax.experimental import pallas as pl
from jax.experimental.pallas import tpu as pltpu
from jax.sharding import PartitionSpec as P

HD = 64
BLK = 128
WIN = 5
RIM = 256
EPSILON = 1e-05
SCALE2 = HD ** (-0.5) * 1.4426950408889634
MESH = pl.DeviceIdType.MESH
BF = jnp.bfloat16
F32 = jnp.float32


def aligned(start, by):
    return pl.multiple_of(start, by)


def normalise(rows, gain):
    center = jnp.mean(rows, axis=-1, keepdims=True)
    spread = jnp.mean(jnp.square(rows - center), axis=-1, keepdims=True)
    return (rows - center) * lax.rsqrt(spread + EPSILON) * gain


def kernel(
    nh,
    nc,
    tok_hbm,
    lng_hbm,
    wqkv_hbm,
    wout_hbm,
    nb_hbm,
    cnt_hbm,
    lat_hbm,
    latg_hbm,
    wlq_hbm,
    wlo_hbm,
    mg_hbm,
    wup_hbm,
    wdn_hbm,
    tout_ref,
    lout_ref,
    lng_ref,
    nb_ref,
    cnt_ref,
    latg_ref,
    mg_ref,
    tok,
    wqkv,
    wout,
    lat,
    wlq,
    wlo,
    wup,
    wdn,
    G,
    latn,
    Q,
    KV,
    kst,
    vst,
    fA,
    fB,
    f2,
    qlat,
    om,
    mm,
    hl,
    multr,
    biasr,
    r1s,
    r1t,
    r1r,
    r1u,
    r2s,
    r2r,
    r3s,
    r3r,
    r4s,
    r4r,
    r5s,
    r5r,
    A,
    R,
    in_sem,
    gs,
    gr,
    xs,
    xr,
    row_sem,
    go_sem,
):
    h = lax.axis_index("heads")
    c = lax.axis_index("ctx")
    x = h // 2
    k = h % 2
    nrow = tok.shape[0]
    nlat = lat.shape[0]
    dw = tok.shape[1]
    nk = dw // 128
    gtok = nh * nrow
    nblk = gtok // BLK
    per = nlat // nc

    ny = 4
    nz = nc // ny
    z = c // ny
    y = lax.rem(c, ny)
    zs = [lax.rem(z + d, nz) * ny for d in range(nz)]
    ys = [lax.rem(y + d, ny) for d in range(ny)]
    own_y = pl.ds(aligned(y * 128, 128), 128)

    loads = [
        pltpu.make_async_copy(tok_hbm, tok, in_sem.at[0]),
        pltpu.make_async_copy(lat_hbm, lat, in_sem.at[1]),
        pltpu.make_async_copy(wlq_hbm, wlq, in_sem.at[2]),
        pltpu.make_async_copy(wqkv_hbm.at[0], wqkv.at[:, pl.ds(0, 128)], in_sem.at[3]),
        pltpu.make_async_copy(wqkv_hbm.at[1], wqkv.at[:, pl.ds(128, 128)], in_sem.at[4]),
        pltpu.make_async_copy(wqkv_hbm.at[2], wqkv.at[:, pl.ds(256, 128)], in_sem.at[5]),
        pltpu.make_async_copy(wlo_hbm, wlo, in_sem.at[6]),
        pltpu.make_async_copy(wup_hbm, wup.at[:, own_y], in_sem.at[7]),
        pltpu.make_async_copy(wdn_hbm, wdn.at[own_y, :], in_sem.at[8]),
        pltpu.make_async_copy(wout_hbm, wout, in_sem.at[9]),
    ]
    small = [
        pltpu.make_async_copy(lng_hbm, lng_ref, in_sem.at[10]),
        pltpu.make_async_copy(latg_hbm, latg_ref, in_sem.at[11]),
        pltpu.make_async_copy(nb_hbm, nb_ref, in_sem.at[12]),
        pltpu.make_async_copy(cnt_hbm, cnt_ref, in_sem.at[13]),
        pltpu.make_async_copy(mg_hbm, mg_ref, in_sem.at[14]),
    ]
    small[0].start()
    for load in loads[:3] + small[1:] + loads[3:]:
        load.start()

    barrier = pltpu.get_barrier_semaphore()

    def signal(sem, **to):
        pl.semaphore_signal(sem, inc=1, device_id=to, device_id_type=MESH)

    for d in range(1, nh):
        @pl.when(h != d)
        def _(d=d):
            signal(barrier, heads=d)

    loads[0].wait()
    small[0].wait()
    mine = aligned(h * nrow, 256)
    step = 32

    def norm_tokens(i, carry):
        at = pl.ds(aligned(i * step, step), step)
        G[pl.ds(aligned(mine + i * step, step), step), :] = normalise(
            tok[at, :].astype(F32), lng_ref[...]
        ).astype(BF)
        return carry

    lax.fori_loop(0, nrow // step, norm_tokens, 0)

    @pl.when(h != 0)
    def _():
        pl.semaphore_wait(barrier, nh - 1)

    @pl.when(h == 1)
    def _():
        signal(row_sem, heads=0)

    @pl.when(h == 0)
    def _():
        pl.semaphore_wait(row_sem, 1)


    sib = x * 2 + (1 - k)
    right = lax.rem(x + 1, nh // 2) * 2 + k
    left = lax.rem(x + nh // 2 - 1, nh // 2) * 2 + k
    far = lax.rem(x + 2, nh // 2) * 2 + k
    right_s = lax.rem(x + 1, nh // 2) * 2 + (1 - k)
    left_s = lax.rem(x + nh // 2 - 1, nh // 2) * 2 + (1 - k)
    far_s = lax.rem(x + 2, nh // 2) * 2 + (1 - k)

    quarter = nrow // 4

    def move(block, part, parts, sem, to):
        rows = pl.ds(aligned(block * nrow + part * quarter, quarter), parts * quarter)
        return pltpu.make_async_remote_copy(
            src_ref=G.at[rows, :],
            dst_ref=G.at[rows, :],
            send_sem=gs.at[sem],
            recv_sem=gr.at[sem],
            device_id={"heads": to},
            device_id_type=MESH,
        )

    pending = []
    sends = []
    for i in range(4):
        sends += [move(h, i, 1, 1 + i, right), move(h, 3 - i, 1, 8 - i, left)]
        if i == 1:
            sends += [move(h, 0, 4, 0, sib)]
    for send in sends:
        send.start()
    pending += [send.wait_send for send in sends]

    steps = sorted(
        ((dz, dy) for dz in range(nz) for dy in range(ny) if dz or dy),
        key=lambda d: -(min(d[0], nz - d[0]) + min(d[1], ny - d[1])),
    )
    others = [zs[dz] + ys[dy] for dz, dy in steps]
    z_peers = [zs[dz] + y for dz, dy in steps if dy == 0]
    y_steps = [dy for dz, dy in steps if dz == 0]

    @pl.when(h == 0)
    def _():
        for to in others:
            signal(barrier, ctx=to)


    loads[1].wait()
    for load in small[1:]:
        load.wait()

    def norm_latents(i, carry):
        at = pl.ds(aligned(i * step, step), step)
        latn[at, :] = normalise(lat[at, :].astype(F32), latg_ref[...]).astype(BF)
        return carry

    lax.fori_loop(0, nlat // step, norm_latents, 0)
    loads[2].wait()
    fA[...] = jnp.dot(latn[...], wlq[...], preferred_element_type=F32)
    share = nlat // nh
    two = share // nc
    for hh in range(nh):
        for i in range(two):
            fB[pl.ds(hh * two + i, nc, stride=per), :] = fA[
                pl.ds(hh * share + i, nc, stride=two), :
            ]
    lane = lax.broadcasted_iota(jnp.int32, (nlat, 128), 1)
    lq = fB[...]
    qlat[pl.ds(0, nlat), :] = jnp.where(lane < HD, lq, 0.0).astype(BF)
    qlat[pl.ds(nlat, nlat), :] = jnp.where(lane < HD, 0.0, lq).astype(BF)
    om[...] = jnp.zeros_like(om)
    mm[...] = jnp.full_like(mm, -jnp.inf)

    own64 = lat[pl.ds(aligned(h * share, share), share), :].astype(F32)
    for j in range(nk):
        fA[pl.ds(j, share, stride=nk), :] = own64[:, j * 128 : (j + 1) * 128]
    hl[...] = fA[pl.ds(aligned(c * two * nk, two * nk), two * nk), :]

    slot = lax.broadcasted_iota(jnp.int32, nb_ref.shape, 0)
    column = lax.broadcasted_iota(jnp.int32, nb_ref.shape, 1)
    live = slot < cnt_ref[...]
    eye = lax.broadcasted_iota(jnp.int32, (nblk, nblk), 0) == lax.broadcasted_iota(
        jnp.int32, (nblk, nblk), 1
    )
    for j in range(WIN):
        hits = jnp.where(live & (nb_ref[...] == column + j), 1.0, 0.0)
        times = jnp.sum(hits, axis=0, keepdims=True)
        times = jnp.sum(jnp.where(eye, times, 0.0), axis=1, keepdims=True)
        times = jnp.broadcast_to(times, (nblk, 128))
        multr[j] = times
        biasr[j] = jnp.where(times > 0.0, 0.0, -jnp.inf)

    def project(pieces):
        spans = [
            (aligned(block * nrow + part * quarter, quarter), parts * quarter)
            for block, part, parts in pieces
        ]
        rows = jnp.concatenate([G[pl.ds(s, size), :] for s, size in spans], axis=0)
        made = jnp.dot(rows, wqkv[...], preferred_element_type=F32)
        at = 0
        for s, size in spans:
            part = slice(at, at + size)
            at += size
            first = lax.broadcasted_iota(jnp.int32, (size, 128), 1) < HD
            q = made[part, 0:128]
            key = made[part, 128:256].astype(BF)
            v = made[part, 256:384]
            v0 = jnp.where(first, v, 1.0).astype(BF)
            v1 = jnp.where(first, 1.0, v).astype(BF)
            Q[0, pl.ds(s, size), :] = jnp.where(first, q, 0.0).astype(BF)
            Q[1, pl.ds(s, size), :] = jnp.where(first, 0.0, q).astype(BF)
            wide = pl.ds(aligned(s + RIM, quarter), size)
            KV[0, wide, :] = key
            KV[1, wide, :] = v0
            KV[2, wide, :] = v1
            kst[part, :] = key
            vst[0, part, :] = v0
            vst[1, part, :] = v1
        return at

    def cross(keys, t):
        at = pl.ds(t * nlat, nlat)
        s = lax.dot_general(
            qlat[at, :],
            kst[pl.ds(0, keys), :],
            (((1,), (1,)), ((), ())),
            preferred_element_type=F32,
        )
        before = mm[at, :]
        top = jnp.maximum(before, jnp.max(s, axis=1, keepdims=True))
        alpha = jnp.exp2((before - top) * SCALE2)
        p = jnp.concatenate(
            [
                jnp.exp2((s[:, j * 128 : (j + 1) * 128] - top) * SCALE2).astype(BF)
                for j in range(keys // 128)
            ],
            axis=1,
        )
        mm[at, :] = top
        om[at, :] = om[at, :] * alpha + jnp.dot(
            p, vst[t, pl.ds(0, keys), :], preferred_element_type=F32
        )

    def stage(pieces):
        keys = project(pieces)
        for t in range(2):
            cross(keys, t)

    def start(copies):
        for copy in copies:
            copy.start()
        pending.extend([copy.wait_send for copy in copies])

    move(left, 0, 1, 1, right).wait_recv()
    move(right, 3, 1, 8, left).wait_recv()
    start([move(left, 0, 1, 9, right), move(right, 3, 1, 12, left)])
    for i in (3, 4, 5):
        loads[i].wait()
    move(sib, 0, 4, 0, sib).wait_recv()
    stage([(h, 0, 4), (sib, 0, 4)])

    @pl.when(h == 0)
    def _():
        pl.semaphore_wait(barrier, nc - 1)
        for d in range(1, nh):
            signal(go_sem, heads=d)


    move(left, 1, 1, 2, right).wait_recv()
    move(right, 2, 1, 7, left).wait_recv()
    start([move(left, 1, 1, 10, right), move(right, 2, 1, 11, left)])
    start([move(left, 0, 2, 13, sib), move(right, 2, 2, 14, sib)])
    move(left_s, 0, 2, 13, sib).wait_recv()
    move(right_s, 2, 2, 14, sib).wait_recv()
    stage([(left, 0, 2), (right, 2, 2), (left_s, 0, 2), (right_s, 2, 2)])

    @pl.when(h != 0)
    def _():
        pl.semaphore_wait(go_sem, 1)

    loads[7].wait()
    loads[8].wait()

    def share_weight(ref, sem, **to):
        pltpu.make_async_remote_copy(
            src_ref=ref,
            dst_ref=ref,
            send_sem=xs.at[sem],
            recv_sem=xr.at[sem],
            device_id=to,
            device_id_type=MESH,
        ).start()

    @pl.when(k == 0)
    def _():
        for dy in y_steps:
            share_weight(wup.at[:, own_y], 9, ctx=zs[0] + ys[dy])

    @pl.when(k == 1)
    def _():
        for dy in y_steps:
            share_weight(wdn.at[own_y, :], 9, ctx=zs[0] + ys[dy])

    for i in (2, 3):
        move(left, i, 1, 1 + i, right).wait_recv()
        move(right, 3 - i, 1, 8 - i, left).wait_recv()
    start([move(left, 2, 2, 15, sib), move(right, 0, 2, 16, sib)])

    move(left_s, 2, 2, 15, sib).wait_recv()
    move(right_s, 0, 2, 16, sib).wait_recv()
    stage([(left, 2, 2), (right, 0, 2), (left_s, 2, 2), (right_s, 0, 2)])

    move(far, 0, 1, 9, right).wait_recv()
    move(far, 3, 1, 12, left).wait_recv()
    start([move(far, 0, 1, 17, sib), move(far, 3, 1, 18, sib)])
    move(far_s, 0, 1, 17, sib).wait_recv()
    move(far_s, 3, 1, 18, sib).wait_recv()
    stage([(far, 0, 1), (far, 3, 1), (far_s, 0, 1), (far_s, 3, 1)])

    move(far, 1, 1, 10, right).wait_recv()
    move(far, 2, 1, 11, left).wait_recv()
    start([move(far, 1, 2, 19, sib)])
    move(far_s, 1, 2, 19, sib).wait_recv()
    stage([(far, 1, 2), (far_s, 1, 2)])

    tile1 = 128
    lane1 = lax.broadcasted_iota(jnp.int32, (tile1, 128), 1)
    row1 = lax.broadcasted_iota(jnp.int32, (tile1, 128), 0)
    first1 = lane1 < HD
    pick1 = lax.rem(lane1, HD) == lax.rem(row1, per)
    for t in range(nlat // tile1):
        at0 = pl.ds(t * tile1, tile1)
        at1 = pl.ds(nlat + t * tile1, tile1)
        o0, o1 = om[at0, :], om[at1, :]
        total = pltpu.roll(jnp.where(first1, o1, o0), HD, 1)
        r1s[at0, :] = (jnp.where(first1, o0, o1) / total).astype(BF)
        lse = jnp.where(first1, mm[at0, :], mm[at1, :]) * SCALE2 + jnp.log2(total)
        lse = jnp.where(pick1, lse, 0.0)
        for g in range(tile1 // per):
            r1t[t * (tile1 // per) + g] = jnp.sum(
                lse[g * per : (g + 1) * per, :], axis=0, keepdims=True
            )

    own_c = pl.ds(aligned(c * per, 16), per)
    def to_ctx(src, dst, s, r, peers=others):
        for to in peers:
            pltpu.make_async_remote_copy(
                src_ref=src(to),
                dst_ref=dst,
                send_sem=xs.at[s],
                recv_sem=xr.at[r],
                device_id={"ctx": to},
                device_id_type=MESH,
            ).start()

    def spread(i, src, dst):
        to_ctx(lambda to: src.at[pl.ds(aligned(to * per, 16), per), :], dst.at[own_c, :], i, i)

    def await_bytes(ref, sem):
        pltpu.make_async_copy(ref, ref, sem).wait()

    rest = pl.ds(0, (nc - 1) * per)
    to_ctx(lambda to: r1t.at[to], r1u.at[c], 1, 1)
    spread(0, r1s, r1r)
    r1r[own_c, :] = r1s[own_c, :]
    r1u[c] = r1t[c]

    def rim(src, dst, sem, to):
        return pltpu.make_async_remote_copy(
            src_ref=KV.at[:, pl.ds(src, RIM), :],
            dst_ref=KV.at[:, pl.ds(dst, RIM), :],
            send_sem=xs.at[sem],
            recv_sem=xr.at[sem],
            device_id={"ctx": to},
            device_id_type=MESH,
        )

    rims = [
        rim(RIM, RIM + gtok, 2, lax.rem(c + nc - 1, nc)),
        rim(gtok, 0, 3, lax.rem(c + 1, nc)),
    ]
    for r in rims:
        r.start()
    pending += [r.wait_send for r in rims]
    pending += [lambda: await_bytes(r1r.at[rest, :], xs.at[0])]
    pending += [lambda: await_bytes(r1u.at[pl.ds(0, nc - 1)], xs.at[1])]

    firstb = lax.broadcasted_iota(jnp.int32, (BLK, 128), 1) < HD

    def attend(b):
        at = pl.ds(aligned(b * BLK, BLK), BLK)
        win = pl.ds(aligned(b * BLK, BLK), WIN * BLK)
        q = jnp.concatenate([Q[0, at, :], Q[1, at, :]], axis=0)
        s = lax.dot_general(
            q, KV[0, win, :], (((1,), (1,)), ((), ())), preferred_element_type=F32
        )
        parts = [
            s[:, j * BLK : (j + 1) * BLK] + biasr[j, pl.ds(b, 1), :] for j in range(WIN)
        ]
        top = parts[0]
        for part in parts[1:]:
            top = jnp.maximum(top, part)
        top = jnp.max(top, axis=1, keepdims=True)
        p = jnp.concatenate(
            [
                (jnp.exp2((part - top) * SCALE2) * multr[j, pl.ds(b, 1), :]).astype(BF)
                for j, part in enumerate(parts)
            ],
            axis=1,
        )
        o0 = jnp.dot(p[:BLK], KV[1, win, :], preferred_element_type=F32)
        o1 = jnp.dot(p[BLK:], KV[2, win, :], preferred_element_type=F32)
        total = pltpu.roll(jnp.where(firstb, o1, o0), HD, 1)
        A[at, :] = (jnp.where(firstb, o0, o1) / total).astype(BF)

    def attend_four(i, carry):
        for j in range(4):
            attend(2 + 4 * i + j)
        return carry

    lax.fori_loop(0, (nblk - 4) // 4, attend_four, 0)

    await_bytes(r1r.at[rest, :], xr.at[0])
    await_bytes(r1u.at[pl.ds(0, nc - 1)], xr.at[1])
    lanes = lax.broadcasted_iota(jnp.int32, (per, 128), 1)
    pick = lax.rem(lanes, HD) == lax.broadcasted_iota(jnp.int32, (per, 128), 0)
    for i in range(nc):
        fA[pl.ds(i * per, per), :] = jnp.where(pick, r1u[i], 0.0)
    same = (
        lax.broadcasted_iota(jnp.int32, (128, 128), 0) // HD
        == lax.broadcasted_iota(jnp.int32, (128, 128), 1) // HD
    )
    fB[...] = jnp.dot(
        fA[...],
        jnp.where(same, 1.0, 0.0),
        preferred_element_type=F32,
        precision=lax.Precision.HIGHEST,
    )
    peak = fB[pl.ds(0, per), :]
    for i in range(1, nc):
        peak = jnp.maximum(peak, fB[pl.ds(i * per, per), :])
    weight = jnp.zeros((per, 128), F32)
    value = jnp.zeros((per, 128), F32)
    for i in range(nc):
        w = jnp.exp2(fB[pl.ds(i * per, per), :] - peak)
        weight += w
        value += w * r1r[pl.ds(i * per, per), :].astype(F32)
    lat_att = (value / weight).astype(BF)

    loads[6].wait()
    made = jnp.dot(lat_att, wlo[...], preferred_element_type=F32)
    for j in range(nk):
        r2s[pl.ds(j, per, stride=nk), :] = made[:, j * 128 : (j + 1) * 128]
    rest2 = pl.ds(0, (nh - 1) * two * nk)
    own_h = pl.ds(aligned(h * two * nk, 16), two * nk)

    def send2(d, carry):
        to = lax.rem(h + d, nh)
        pltpu.make_async_remote_copy(
            src_ref=r2s.at[pl.ds(aligned(to * two * nk, 16), two * nk), :],
            dst_ref=r2r.at[own_h, :],
            send_sem=xs.at[4],
            recv_sem=xr.at[4],
            device_id={"heads": to},
            device_id_type=MESH,
        ).start()
        return carry

    lax.fori_loop(1, nh, send2, 0)
    r2r[own_h, :] = r2s[own_h, :]
    pending += [lambda: await_bytes(r2r.at[rest2, :], xs.at[4])]

    foreign = (ny - 1) * 128

    @pl.when(k == 0)
    def _():
        await_bytes(wup.at[:, pl.ds(0, foreign)], xr.at[9])
        for dy in y_steps:
            share_weight(wup.at[:, pl.ds(aligned(ys[dy] * 128, 128), 128)], 10, heads=sib)

    @pl.when(k == 1)
    def _():
        await_bytes(wdn.at[pl.ds(0, foreign), :], xr.at[9])
        for dy in y_steps:
            share_weight(wdn.at[pl.ds(aligned(ys[dy] * 128, 128), 128), :], 10, heads=sib)

    pending += [lambda: await_bytes(wup.at[:, pl.ds(0, foreign)], xs.at[9])]
    pending += [lambda: await_bytes(wup.at[:, pl.ds(0, foreign)], xs.at[10])]

    for r in rims:
        r.wait_recv()
    for b in (0, 1, nblk - 2, nblk - 1):
        attend(b)

    await_bytes(r2r.at[rest2, :], xr.at[4])
    hidden = hl[...]
    for i in range(nh):
        hidden += r2r[pl.ds(i * two * nk, two * nk), :]
    hl[...] = hidden
    for i in range(two):
        row = hidden[i * nk : (i + 1) * nk, :]
        center = jnp.sum(jnp.sum(row, axis=0, keepdims=True), axis=1, keepdims=True) / dw
        off = row - center
        spread2 = (
            jnp.sum(jnp.sum(jnp.square(off), axis=0, keepdims=True), axis=1, keepdims=True) / dw
        )
        f2[pl.ds(i * nk, nk), :] = off * lax.rsqrt(spread2 + EPSILON) * mg_ref[...]
    r3s[...] = f2[...].astype(BF)
    own_z = pl.ds(aligned(z * per, 16), per)
    restz = pl.ds(0, (nz - 1) * per)
    to_ctx(lambda to: r3s, r3r.at[own_z, :], 5, 5, z_peers)
    r3r[own_z, :] = r3s[...]
    pending += [lambda: await_bytes(r3r.at[restz, :], xs.at[5])]

    head_cols = pl.ds(aligned(h * 128, 128), 128)

    def send_back(d, carry):
        to = lax.rem(h + d, nh)
        pltpu.make_async_remote_copy(
            src_ref=A.at[pl.ds(aligned(to * nrow, 128), nrow), :],
            dst_ref=R.at[:, head_cols],
            send_sem=xs.at[6],
            recv_sem=xr.at[6],
            device_id={"heads": to},
            device_id_type=MESH,
        ).start()
        return carry

    lax.fori_loop(1, nh, send_back, 0)
    R[:, head_cols] = A[pl.ds(mine, nrow), :]
    pending += [lambda: await_bytes(A.at[pl.ds(0, (nh - 1) * nrow), :], xs.at[6])]

    await_bytes(r3r.at[restz, :], xr.at[5])
    await_bytes(wup.at[:, pl.ds(0, foreign)], xr.at[10])
    group = nz * two
    fA[pl.ds(0, nz * per), :] = r3r[...].astype(F32)
    rows = jnp.concatenate(
        [fA[pl.ds(j, group, stride=nk), :].astype(BF) for j in range(nk)], axis=1
    )
    inner = jax.nn.gelu(
        jnp.dot(rows, wup[...], preferred_element_type=F32), approximate=True
    ).astype(BF)
    made = jnp.dot(inner, wdn[...], preferred_element_type=F32)
    for j in range(nk):
        r4s[pl.ds(j, group, stride=nk), :] = made[:, j * 128 : (j + 1) * 128]
    to_ctx(
        lambda to: r4s.at[pl.ds(aligned(to // ny * per, 16), per), :],
        r4r.at[own_z, :],
        7,
        7,
        z_peers,
    )
    r4r[own_z, :] = r4s[own_z, :]
    pending += [lambda: await_bytes(r4r.at[restz, :], xs.at[7])]

    await_bytes(r4r.at[restz, :], xr.at[7])
    total = hl[...]
    for i in range(nz):
        total += r4r[pl.ds(i * per, per), :]
    r5s[...] = total.astype(BF)
    to_ctx(lambda to: r5s, r5r.at[own_c, :], 8, 8)
    r5r[own_c, :] = r5s[...]
    pending += [lambda: await_bytes(r5r.at[rest, :], xs.at[8])]
    loads[9].wait()
    await_bytes(A.at[pl.ds(0, (nh - 1) * nrow), :], xr.at[6])

    def project_out(n, carry):
        cols = pl.ds(aligned(n * 256, 256), 256)
        tout_ref[:, cols] = (
            tok[:, cols].astype(F32)
            + jnp.dot(R[...], wout[:, cols], preferred_element_type=F32)
        ).astype(BF)
        return carry

    lax.fori_loop(0, dw // 256, project_out, 0)

    await_bytes(r5r.at[rest, :], xr.at[8])
    fA[...] = r5r[...].astype(F32)
    for j in range(nk):
        lout_ref[:, j * 128 : (j + 1) * 128] = fA[pl.ds(j, share, stride=nk), :].astype(BF)

    for done in pending:
        done()


def per_device(
    nh,
    nc,
    tokens,
    ln_gain,
    w_qkv,
    w_out,
    neighbours,
    counts,
    latents,
    lat_gain,
    w_lat_q,
    w_lat_o,
    mlp_gain,
    w_up,
    w_down,
):
    nrow, dw = tokens.shape[1:]
    nlat = latents.shape[0]
    gtok = nrow * nh
    per = nlat // nc
    share = nlat // nh
    nblk = gtok // BLK
    two = share // nc * (dw // 128)
    hbm = pl.BlockSpec(memory_space=pltpu.HBM)
    vmem = pl.BlockSpec(memory_space=pltpu.VMEM)
    stage = gtok // 4
    scratch = [
        pltpu.VMEM((1, dw), F32),
        pltpu.VMEM((neighbours.shape[2], nblk), jnp.int32),
        pltpu.VMEM((1, nblk), jnp.int32),
        pltpu.VMEM((1, dw), F32),
        pltpu.VMEM((dw // 128, 128), F32),
        pltpu.VMEM((nrow, dw), BF),
        pltpu.VMEM((dw, 384), BF),
        pltpu.VMEM((dw, dw), BF),
        pltpu.VMEM((nlat, dw), BF),
        pltpu.VMEM((dw, 128), BF),
        pltpu.VMEM((128, dw), BF),
        pltpu.VMEM((dw, 4 * w_up.shape[1]), BF),
        pltpu.VMEM((4 * w_down.shape[0], dw), BF),
        pltpu.VMEM((gtok, dw), BF),
        pltpu.VMEM((nlat, dw), BF),
        pltpu.VMEM((2, gtok, 128), BF),
        pltpu.VMEM((3, gtok + 2 * RIM, 128), BF),
        pltpu.VMEM((stage, 128), BF),
        pltpu.VMEM((2, stage, 128), BF),
        pltpu.VMEM((nlat, 128), F32),
        pltpu.VMEM((nlat, 128), F32),
        pltpu.VMEM((two, 128), F32),
        pltpu.VMEM((2 * nlat, 128), BF),
        pltpu.VMEM((2 * nlat, 128), F32),
        pltpu.VMEM((2 * nlat, 128), F32),
        pltpu.VMEM((two, 128), F32),
        pltpu.VMEM((WIN, nblk, 128), F32),
        pltpu.VMEM((WIN, nblk, 128), F32),
        pltpu.VMEM((nlat, 128), BF),
        pltpu.VMEM((nc, 1, 128), F32),
        pltpu.VMEM((nlat, 128), BF),
        pltpu.VMEM((nc, 1, 128), F32),
        pltpu.VMEM((nh * two, 128), F32),
        pltpu.VMEM((nh * two, 128), F32),
        pltpu.VMEM((two, 128), BF),
        pltpu.VMEM((nlat // 4, 128), BF),
        pltpu.VMEM((nlat // 4, 128), F32),
        pltpu.VMEM((nlat // 4, 128), F32),
        pltpu.VMEM((two, 128), BF),
        pltpu.VMEM((nlat, 128), BF),
        pltpu.VMEM((gtok, 128), BF),
        pltpu.VMEM((nrow, dw), BF),
        pltpu.SemaphoreType.DMA((15,)),
        pltpu.SemaphoreType.DMA((20,)),
        pltpu.SemaphoreType.DMA((20,)),
        pltpu.SemaphoreType.DMA((11,)),
        pltpu.SemaphoreType.DMA((11,)),
        pltpu.SemaphoreType.REGULAR,
        pltpu.SemaphoreType.REGULAR,
    ]
    tokens_out, latents_out = pl.pallas_call(
        functools.partial(kernel, nh, nc),
        out_shape=(
            jax.ShapeDtypeStruct((nrow, dw), BF),
            jax.ShapeDtypeStruct((share, dw), BF),
        ),
        in_specs=[hbm] * 13,
        out_specs=(vmem, vmem),
        scratch_shapes=scratch,
        compiler_params=pltpu.CompilerParams(
            collective_id=0, has_side_effects=True, vmem_limit_bytes=60 * 1024 * 1024
        ),
        name="encoder_block",
    )(
        tokens[0],
        ln_gain.reshape(1, dw),
        jnp.transpose(w_qkv, (1, 0, 2)),
        w_out,
        neighbours[0].T,
        counts,
        latents,
        lat_gain.reshape(1, dw),
        w_lat_q,
        w_lat_o,
        mlp_gain.reshape(dw // 128, 128),
        w_up,
        w_down,
    )
    return (tokens_out[None], latents_out)


def solution(mesh):
    in_specs = (
        P("ctx", "heads", None),
        P(),
        P(None, None, "heads"),
        P(),
        P("ctx", None, None),
        P("ctx", None),
        P(),
        P(),
        P(None, "heads"),
        P("heads", None),
        P(),
        P(None, "ctx"),
        P("ctx", None),
    )
    out_specs = (P("ctx", "heads", None), P("heads", None))
    return jax.shard_map(
        functools.partial(per_device, mesh.shape["heads"], mesh.shape["ctx"]),
        mesh=mesh,
        in_specs=in_specs,
        out_specs=out_specs,
        check_vma=False,
    )
```

```python
import functools

import jax
import jax.numpy as jnp
from jax import lax
from jax.experimental import pallas as pl
from jax.experimental.pallas import tpu as pltpu
from jax.sharding import PartitionSpec as P

HD = 64
BLK = 128
WIN = 5
RIM = 256
EPSILON = 1e-05
SCALE2 = HD ** (-0.5) * 1.4426950408889634
MESH = pl.DeviceIdType.MESH
BF = jnp.bfloat16
F32 = jnp.float32


def aligned(start, by):
    return pl.multiple_of(start, by)


def normalise(rows, gain):
    center = jnp.mean(rows, axis=-1, keepdims=True)
    spread = jnp.mean(jnp.square(rows - center), axis=-1, keepdims=True)
    return (rows - center) * lax.rsqrt(spread + EPSILON) * gain


def kernel(
    nh,
    nc,
    tok_hbm,
    lng_hbm,
    wqkv_hbm,
    wout_hbm,
    nb_hbm,
    cnt_hbm,
    lat_hbm,
    latg_hbm,
    wlq_hbm,
    wlo_hbm,
    mg_hbm,
    wup_hbm,
    wdn_hbm,
    tout_hbm,
    lout_ref,
    tout_ref,
    lng_ref,
    nb_ref,
    cnt_ref,
    latg_ref,
    mg_ref,
    tok,
    wqkv,
    wout,
    lat,
    wlq,
    wlo,
    wup,
    wdn,
    G,
    latn,
    Q,
    KV,
    kst,
    vst,
    fA,
    fB,
    f2,
    qlat,
    om,
    mm,
    hl,
    multr,
    biasr,
    r1s,
    r1t,
    r1r,
    r1u,
    r2s,
    r2r,
    r3s,
    r3r,
    r4s,
    r4r,
    r5s,
    r5r,
    A,
    R,
    in_sem,
    gs,
    gr,
    xs,
    xr,
    row_sem,
    go_sem,
):
    h = lax.axis_index("heads")
    c = lax.axis_index("ctx")
    x = h // 2
    k = h % 2
    nrow = tok.shape[0]
    nlat = lat.shape[0]
    dw = tok.shape[1]
    nk = dw // 128
    gtok = nh * nrow
    nblk = gtok // BLK
    per = nlat // nc

    ny = 4
    nz = nc // ny
    z = c // ny
    y = lax.rem(c, ny)
    zs = [lax.rem(z + d, nz) * ny for d in range(nz)]
    ys = [lax.rem(y + d, ny) for d in range(ny)]
    own_y = pl.ds(aligned(y * 128, 128), 128)

    loads = [
        pltpu.make_async_copy(tok_hbm, tok, in_sem.at[0]),
        pltpu.make_async_copy(lat_hbm, lat, in_sem.at[1]),
        pltpu.make_async_copy(wlq_hbm, wlq, in_sem.at[2]),
        pltpu.make_async_copy(wqkv_hbm.at[0], wqkv.at[:, pl.ds(0, 128)], in_sem.at[3]),
        pltpu.make_async_copy(wqkv_hbm.at[1], wqkv.at[:, pl.ds(128, 128)], in_sem.at[4]),
        pltpu.make_async_copy(wqkv_hbm.at[2], wqkv.at[:, pl.ds(256, 128)], in_sem.at[5]),
        pltpu.make_async_copy(wlo_hbm, wlo, in_sem.at[6]),
        pltpu.make_async_copy(wup_hbm, wup.at[:, own_y], in_sem.at[7]),
        pltpu.make_async_copy(wdn_hbm, wdn.at[own_y, :], in_sem.at[8]),
        pltpu.make_async_copy(wout_hbm, wout, in_sem.at[9]),
    ]
    small = [
        pltpu.make_async_copy(lng_hbm, lng_ref, in_sem.at[10]),
        pltpu.make_async_copy(latg_hbm, latg_ref, in_sem.at[11]),
        pltpu.make_async_copy(nb_hbm, nb_ref, in_sem.at[12]),
        pltpu.make_async_copy(cnt_hbm, cnt_ref, in_sem.at[13]),
        pltpu.make_async_copy(mg_hbm, mg_ref, in_sem.at[14]),
    ]
    small[0].start()
    for load in loads[:3] + small[1:] + loads[3:]:
        load.start()

    barrier = pltpu.get_barrier_semaphore()

    def signal(sem, **to):
        pl.semaphore_signal(sem, inc=1, device_id=to, device_id_type=MESH)

    for d in range(1, nh):
        @pl.when(h != d)
        def _(d=d):
            signal(barrier, heads=d)

    loads[0].wait()
    small[0].wait()
    mine = aligned(h * nrow, 256)
    step = 32

    def norm_tokens(i, carry):
        at = pl.ds(aligned(i * step, step), step)
        G[pl.ds(aligned(mine + i * step, step), step), :] = normalise(
            tok[at, :].astype(F32), lng_ref[...]
        ).astype(BF)
        return carry

    lax.fori_loop(0, nrow // step, norm_tokens, 0)

    @pl.when(h != 0)
    def _():
        pl.semaphore_wait(barrier, nh - 1)

    @pl.when(h == 1)
    def _():
        signal(row_sem, heads=0)

    @pl.when(h == 0)
    def _():
        pl.semaphore_wait(row_sem, 1)


    sib = x * 2 + (1 - k)
    right = lax.rem(x + 1, nh // 2) * 2 + k
    left = lax.rem(x + nh // 2 - 1, nh // 2) * 2 + k
    far = lax.rem(x + 2, nh // 2) * 2 + k
    right_s = lax.rem(x + 1, nh // 2) * 2 + (1 - k)
    left_s = lax.rem(x + nh // 2 - 1, nh // 2) * 2 + (1 - k)
    far_s = lax.rem(x + 2, nh // 2) * 2 + (1 - k)

    quarter = nrow // 4

    def move(block, part, parts, sem, to):
        rows = pl.ds(aligned(block * nrow + part * quarter, quarter), parts * quarter)
        return pltpu.make_async_remote_copy(
            src_ref=G.at[rows, :],
            dst_ref=G.at[rows, :],
            send_sem=gs.at[sem],
            recv_sem=gr.at[sem],
            device_id={"heads": to},
            device_id_type=MESH,
        )

    pending = []
    sends = []
    for i in range(4):
        sends += [move(h, i, 1, 1 + i, right), move(h, 3 - i, 1, 8 - i, left)]
        if i == 1:
            sends += [move(h, 0, 4, 0, sib)]
    for send in sends:
        send.start()
    pending += [send.wait_send for send in sends]

    steps = sorted(
        ((dz, dy) for dz in range(nz) for dy in range(ny) if dz or dy),
        key=lambda d: -(min(d[0], nz - d[0]) + min(d[1], ny - d[1])),
    )
    others = [zs[dz] + ys[dy] for dz, dy in steps]
    z_peers = [zs[dz] + y for dz, dy in steps if dy == 0]
    y_steps = [dy for dz, dy in steps if dz == 0]

    @pl.when(h == 0)
    def _():
        for to in others:
            signal(barrier, ctx=to)


    loads[1].wait()
    for load in small[1:]:
        load.wait()

    def norm_latents(i, carry):
        at = pl.ds(aligned(i * step, step), step)
        latn[at, :] = normalise(lat[at, :].astype(F32), latg_ref[...]).astype(BF)
        return carry

    lax.fori_loop(0, nlat // step, norm_latents, 0)
    loads[2].wait()
    fA[...] = jnp.dot(latn[...], wlq[...], preferred_element_type=F32)
    share = nlat // nh
    two = share // nc
    for hh in range(nh):
        for i in range(two):
            fB[pl.ds(hh * two + i, nc, stride=per), :] = fA[
                pl.ds(hh * share + i, nc, stride=two), :
            ]
    lane = lax.broadcasted_iota(jnp.int32, (nlat, 128), 1)
    lq = fB[...]
    qlat[pl.ds(0, nlat), :] = jnp.where(lane < HD, lq, 0.0).astype(BF)
    qlat[pl.ds(nlat, nlat), :] = jnp.where(lane < HD, 0.0, lq).astype(BF)
    om[...] = jnp.zeros_like(om)
    mm[...] = jnp.full_like(mm, -jnp.inf)

    own64 = lat[pl.ds(aligned(h * share, share), share), :].astype(F32)
    for j in range(nk):
        fA[pl.ds(j, share, stride=nk), :] = own64[:, j * 128 : (j + 1) * 128]
    hl[...] = fA[pl.ds(aligned(c * two * nk, two * nk), two * nk), :]

    slot = lax.broadcasted_iota(jnp.int32, nb_ref.shape, 0)
    column = lax.broadcasted_iota(jnp.int32, nb_ref.shape, 1)
    live = slot < cnt_ref[...]
    eye = lax.broadcasted_iota(jnp.int32, (nblk, nblk), 0) == lax.broadcasted_iota(
        jnp.int32, (nblk, nblk), 1
    )
    for j in range(WIN):
        hits = jnp.where(live & (nb_ref[...] == column + j), 1.0, 0.0)
        times = jnp.sum(hits, axis=0, keepdims=True)
        times = jnp.sum(jnp.where(eye, times, 0.0), axis=1, keepdims=True)
        times = jnp.broadcast_to(times, (nblk, 128))
        multr[j] = times
        biasr[j] = jnp.where(times > 0.0, 0.0, -jnp.inf)

    def project(pieces):
        spans = [
            (aligned(block * nrow + part * quarter, quarter), parts * quarter)
            for block, part, parts in pieces
        ]
        rows = jnp.concatenate([G[pl.ds(s, size), :] for s, size in spans], axis=0)
        made = jnp.dot(rows, wqkv[...], preferred_element_type=F32)
        at = 0
        for s, size in spans:
            part = slice(at, at + size)
            at += size
            first = lax.broadcasted_iota(jnp.int32, (size, 128), 1) < HD
            q = made[part, 0:128]
            key = made[part, 128:256].astype(BF)
            v = made[part, 256:384]
            v0 = jnp.where(first, v, 1.0).astype(BF)
            v1 = jnp.where(first, 1.0, v).astype(BF)
            Q[0, pl.ds(s, size), :] = jnp.where(first, q, 0.0).astype(BF)
            Q[1, pl.ds(s, size), :] = jnp.where(first, 0.0, q).astype(BF)
            wide = pl.ds(aligned(s + RIM, quarter), size)
            KV[0, wide, :] = key
            KV[1, wide, :] = v0
            KV[2, wide, :] = v1
            kst[part, :] = key
            vst[0, part, :] = v0
            vst[1, part, :] = v1
        return at

    def cross(keys, t):
        at = pl.ds(t * nlat, nlat)
        s = lax.dot_general(
            qlat[at, :],
            kst[pl.ds(0, keys), :],
            (((1,), (1,)), ((), ())),
            preferred_element_type=F32,
        )
        before = mm[at, :]
        top = jnp.maximum(before, jnp.max(s, axis=1, keepdims=True))
        alpha = jnp.exp2((before - top) * SCALE2)
        p = jnp.concatenate(
            [
                jnp.exp2((s[:, j * 128 : (j + 1) * 128] - top) * SCALE2).astype(BF)
                for j in range(keys // 128)
            ],
            axis=1,
        )
        mm[at, :] = top
        om[at, :] = om[at, :] * alpha + jnp.dot(
            p, vst[t, pl.ds(0, keys), :], preferred_element_type=F32
        )

    def stage(pieces):
        keys = project(pieces)
        for t in range(2):
            cross(keys, t)

    def start(copies):
        for copy in copies:
            copy.start()
        pending.extend([copy.wait_send for copy in copies])

    move(left, 0, 1, 1, right).wait_recv()
    move(right, 3, 1, 8, left).wait_recv()
    start([move(left, 0, 1, 9, right), move(right, 3, 1, 12, left)])
    for i in (3, 4, 5):
        loads[i].wait()
    move(sib, 0, 4, 0, sib).wait_recv()
    stage([(h, 0, 4), (sib, 0, 4)])

    @pl.when(h == 0)
    def _():
        pl.semaphore_wait(barrier, nc - 1)
        for d in range(1, nh):
            signal(go_sem, heads=d)


    move(left, 1, 1, 2, right).wait_recv()
    move(right, 2, 1, 7, left).wait_recv()
    start([move(left, 1, 1, 10, right), move(right, 2, 1, 11, left)])
    start([move(left, 0, 2, 13, sib), move(right, 2, 2, 14, sib)])
    move(left_s, 0, 2, 13, sib).wait_recv()
    move(right_s, 2, 2, 14, sib).wait_recv()
    stage([(left, 0, 2), (right, 2, 2), (left_s, 0, 2), (right_s, 2, 2)])

    @pl.when(h != 0)
    def _():
        pl.semaphore_wait(go_sem, 1)

    loads[7].wait()
    loads[8].wait()

    def share_weight(ref, sem, **to):
        pltpu.make_async_remote_copy(
            src_ref=ref,
            dst_ref=ref,
            send_sem=xs.at[sem],
            recv_sem=xr.at[sem],
            device_id=to,
            device_id_type=MESH,
        ).start()

    @pl.when(k == 0)
    def _():
        for dy in y_steps:
            share_weight(wup.at[:, own_y], 9, ctx=zs[0] + ys[dy])

    @pl.when(k == 1)
    def _():
        for dy in y_steps:
            share_weight(wdn.at[own_y, :], 9, ctx=zs[0] + ys[dy])

    for i in (2, 3):
        move(left, i, 1, 1 + i, right).wait_recv()
        move(right, 3 - i, 1, 8 - i, left).wait_recv()
    start([move(left, 2, 2, 15, sib), move(right, 0, 2, 16, sib)])

    move(left_s, 2, 2, 15, sib).wait_recv()
    move(right_s, 0, 2, 16, sib).wait_recv()
    stage([(left, 2, 2), (right, 0, 2), (left_s, 2, 2), (right_s, 0, 2)])

    move(far, 0, 1, 9, right).wait_recv()
    move(far, 3, 1, 12, left).wait_recv()
    start([move(far, 0, 1, 17, sib), move(far, 3, 1, 18, sib)])
    move(far_s, 0, 1, 17, sib).wait_recv()
    move(far_s, 3, 1, 18, sib).wait_recv()
    stage([(far, 0, 1), (far, 3, 1), (far_s, 0, 1), (far_s, 3, 1)])

    move(far, 1, 1, 10, right).wait_recv()
    move(far, 2, 1, 11, left).wait_recv()
    start([move(far, 1, 2, 19, sib)])
    move(far_s, 1, 2, 19, sib).wait_recv()
    stage([(far, 1, 2), (far_s, 1, 2)])

    tile1 = 128
    lane1 = lax.broadcasted_iota(jnp.int32, (tile1, 128), 1)
    row1 = lax.broadcasted_iota(jnp.int32, (tile1, 128), 0)
    first1 = lane1 < HD
    pick1 = lax.rem(lane1, HD) == lax.rem(row1, per)
    for t in range(nlat // tile1):
        at0 = pl.ds(t * tile1, tile1)
        at1 = pl.ds(nlat + t * tile1, tile1)
        o0, o1 = om[at0, :], om[at1, :]
        total = pltpu.roll(jnp.where(first1, o1, o0), HD, 1)
        r1s[at0, :] = (jnp.where(first1, o0, o1) / total).astype(BF)
        lse = jnp.where(first1, mm[at0, :], mm[at1, :]) * SCALE2 + jnp.log2(total)
        lse = jnp.where(pick1, lse, 0.0)
        for g in range(tile1 // per):
            r1t[t * (tile1 // per) + g] = jnp.sum(
                lse[g * per : (g + 1) * per, :], axis=0, keepdims=True
            )

    own_c = pl.ds(aligned(c * per, 16), per)
    def to_ctx(src, dst, s, r, peers=others):
        for to in peers:
            pltpu.make_async_remote_copy(
                src_ref=src(to),
                dst_ref=dst,
                send_sem=xs.at[s],
                recv_sem=xr.at[r],
                device_id={"ctx": to},
                device_id_type=MESH,
            ).start()

    def spread(i, src, dst):
        to_ctx(lambda to: src.at[pl.ds(aligned(to * per, 16), per), :], dst.at[own_c, :], i, i)

    def await_bytes(ref, sem):
        pltpu.make_async_copy(ref, ref, sem).wait()

    rest = pl.ds(0, (nc - 1) * per)
    to_ctx(lambda to: r1t.at[to], r1u.at[c], 1, 1)
    spread(0, r1s, r1r)
    r1r[own_c, :] = r1s[own_c, :]
    r1u[c] = r1t[c]

    def rim(src, dst, sem, to):
        return pltpu.make_async_remote_copy(
            src_ref=KV.at[:, pl.ds(src, RIM), :],
            dst_ref=KV.at[:, pl.ds(dst, RIM), :],
            send_sem=xs.at[sem],
            recv_sem=xr.at[sem],
            device_id={"ctx": to},
            device_id_type=MESH,
        )

    rims = [
        rim(RIM, RIM + gtok, 2, lax.rem(c + nc - 1, nc)),
        rim(gtok, 0, 3, lax.rem(c + 1, nc)),
    ]
    for r in rims:
        r.start()
    pending += [r.wait_send for r in rims]
    pending += [lambda: await_bytes(r1r.at[rest, :], xs.at[0])]
    pending += [lambda: await_bytes(r1u.at[pl.ds(0, nc - 1)], xs.at[1])]

    firstb = lax.broadcasted_iota(jnp.int32, (BLK, 128), 1) < HD

    def attend(b):
        at = pl.ds(aligned(b * BLK, BLK), BLK)
        win = pl.ds(aligned(b * BLK, BLK), WIN * BLK)
        q = jnp.concatenate([Q[0, at, :], Q[1, at, :]], axis=0)
        s = lax.dot_general(
            q, KV[0, win, :], (((1,), (1,)), ((), ())), preferred_element_type=F32
        )
        parts = [
            s[:, j * BLK : (j + 1) * BLK] + biasr[j, pl.ds(b, 1), :] for j in range(WIN)
        ]
        top = parts[0]
        for part in parts[1:]:
            top = jnp.maximum(top, part)
        top = jnp.max(top, axis=1, keepdims=True)
        p = jnp.concatenate(
            [
                (jnp.exp2((part - top) * SCALE2) * multr[j, pl.ds(b, 1), :]).astype(BF)
                for j, part in enumerate(parts)
            ],
            axis=1,
        )
        o0 = jnp.dot(p[:BLK], KV[1, win, :], preferred_element_type=F32)
        o1 = jnp.dot(p[BLK:], KV[2, win, :], preferred_element_type=F32)
        total = pltpu.roll(jnp.where(firstb, o1, o0), HD, 1)
        A[at, :] = (jnp.where(firstb, o0, o1) / total).astype(BF)

    def attend_four(i, carry):
        for j in range(4):
            attend(2 + 4 * i + j)
        return carry

    lax.fori_loop(0, 2, attend_four, 0)

    await_bytes(r1r.at[rest, :], xr.at[0])
    await_bytes(r1u.at[pl.ds(0, nc - 1)], xr.at[1])
    lanes = lax.broadcasted_iota(jnp.int32, (per, 128), 1)
    pick = lax.rem(lanes, HD) == lax.broadcasted_iota(jnp.int32, (per, 128), 0)
    for i in range(nc):
        fA[pl.ds(i * per, per), :] = jnp.where(pick, r1u[i], 0.0)
    same = (
        lax.broadcasted_iota(jnp.int32, (128, 128), 0) // HD
        == lax.broadcasted_iota(jnp.int32, (128, 128), 1) // HD
    )
    fB[...] = jnp.dot(
        fA[...],
        jnp.where(same, 1.0, 0.0),
        preferred_element_type=F32,
        precision=lax.Precision.HIGHEST,
    )
    peak = fB[pl.ds(0, per), :]
    for i in range(1, nc):
        peak = jnp.maximum(peak, fB[pl.ds(i * per, per), :])
    weight = jnp.zeros((per, 128), F32)
    value = jnp.zeros((per, 128), F32)
    for i in range(nc):
        w = jnp.exp2(fB[pl.ds(i * per, per), :] - peak)
        weight += w
        value += w * r1r[pl.ds(i * per, per), :].astype(F32)
    lat_att = (value / weight).astype(BF)

    loads[6].wait()
    made = jnp.dot(lat_att, wlo[...], preferred_element_type=F32)
    for j in range(nk):
        r2s[pl.ds(j, per, stride=nk), :] = made[:, j * 128 : (j + 1) * 128]
    rest2 = pl.ds(0, (nh - 1) * two * nk)
    own_h = pl.ds(aligned(h * two * nk, 16), two * nk)

    def send2(d, carry):
        to = lax.rem(h + d, nh)
        pltpu.make_async_remote_copy(
            src_ref=r2s.at[pl.ds(aligned(to * two * nk, 16), two * nk), :],
            dst_ref=r2r.at[own_h, :],
            send_sem=xs.at[4],
            recv_sem=xr.at[4],
            device_id={"heads": to},
            device_id_type=MESH,
        ).start()
        return carry

    lax.fori_loop(1, nh, send2, 0)
    r2r[own_h, :] = r2s[own_h, :]
    pending += [lambda: await_bytes(r2r.at[rest2, :], xs.at[4])]

    foreign = (ny - 1) * 128

    @pl.when(k == 0)
    def _():
        await_bytes(wup.at[:, pl.ds(0, foreign)], xr.at[9])
        for dy in y_steps:
            share_weight(wup.at[:, pl.ds(aligned(ys[dy] * 128, 128), 128)], 10, heads=sib)

    @pl.when(k == 1)
    def _():
        await_bytes(wdn.at[pl.ds(0, foreign), :], xr.at[9])
        for dy in y_steps:
            share_weight(wdn.at[pl.ds(aligned(ys[dy] * 128, 128), 128), :], 10, heads=sib)

    pending += [lambda: await_bytes(wup.at[:, pl.ds(0, foreign)], xs.at[9])]
    pending += [lambda: await_bytes(wup.at[:, pl.ds(0, foreign)], xs.at[10])]

    lax.fori_loop(2, (nblk - 4) // 4, attend_four, 0)

    await_bytes(r2r.at[rest2, :], xr.at[4])
    hidden = hl[...]
    for i in range(nh):
        hidden += r2r[pl.ds(i * two * nk, two * nk), :]
    hl[...] = hidden
    for i in range(two):
        row = hidden[i * nk : (i + 1) * nk, :]
        center = jnp.sum(jnp.sum(row, axis=0, keepdims=True), axis=1, keepdims=True) / dw
        off = row - center
        spread2 = (
            jnp.sum(jnp.sum(jnp.square(off), axis=0, keepdims=True), axis=1, keepdims=True) / dw
        )
        f2[pl.ds(i * nk, nk), :] = off * lax.rsqrt(spread2 + EPSILON) * mg_ref[...]
    r3s[...] = f2[...].astype(BF)
    own_z = pl.ds(aligned(z * per, 16), per)
    restz = pl.ds(0, (nz - 1) * per)
    to_ctx(lambda to: r3s, r3r.at[own_z, :], 5, 5, z_peers)
    r3r[own_z, :] = r3s[...]
    pending += [lambda: await_bytes(r3r.at[restz, :], xs.at[5])]

    for r in rims:
        r.wait_recv()
    for b in (0, 1, nblk - 2, nblk - 1):
        attend(b)

    head_cols = pl.ds(aligned(h * 128, 128), 128)

    def send_back(d, carry):
        to = lax.rem(h + d, nh)
        pltpu.make_async_remote_copy(
            src_ref=A.at[pl.ds(aligned(to * nrow, 128), nrow), :],
            dst_ref=R.at[:, head_cols],
            send_sem=xs.at[6],
            recv_sem=xr.at[6],
            device_id={"heads": to},
            device_id_type=MESH,
        ).start()
        return carry

    lax.fori_loop(1, nh, send_back, 0)
    R[:, head_cols] = A[pl.ds(mine, nrow), :]
    pending += [lambda: await_bytes(A.at[pl.ds(0, (nh - 1) * nrow), :], xs.at[6])]

    await_bytes(r3r.at[restz, :], xr.at[5])
    await_bytes(wup.at[:, pl.ds(0, foreign)], xr.at[10])
    group = nz * two
    fA[pl.ds(0, nz * per), :] = r3r[...].astype(F32)
    rows = jnp.concatenate(
        [fA[pl.ds(j, group, stride=nk), :].astype(BF) for j in range(nk)], axis=1
    )
    inner = jax.nn.gelu(
        jnp.dot(rows, wup[...], preferred_element_type=F32), approximate=True
    ).astype(BF)
    made = jnp.dot(inner, wdn[...], preferred_element_type=F32)
    for j in range(nk):
        r4s[pl.ds(j, group, stride=nk), :] = made[:, j * 128 : (j + 1) * 128]
    to_ctx(
        lambda to: r4s.at[pl.ds(aligned(to // ny * per, 16), per), :],
        r4r.at[own_z, :],
        7,
        7,
        z_peers,
    )
    r4r[own_z, :] = r4s[own_z, :]
    pending += [lambda: await_bytes(r4r.at[restz, :], xs.at[7])]

    await_bytes(r4r.at[restz, :], xr.at[7])
    total = hl[...]
    for i in range(nz):
        total += r4r[pl.ds(i * per, per), :]
    r5s[...] = total.astype(BF)
    to_ctx(lambda to: r5s, r5r.at[own_c, :], 8, 8)
    r5r[own_c, :] = r5s[...]
    pending += [lambda: await_bytes(r5r.at[rest, :], xs.at[8])]
    loads[9].wait()
    await_bytes(A.at[pl.ds(0, (nh - 1) * nrow), :], xr.at[6])

    def project_out(n, carry):
        cols = pl.ds(aligned(n * 256, 256), 256)
        tout_ref[:, cols] = (
            tok[:, cols].astype(F32)
            + jnp.dot(R[...], wout[:, cols], preferred_element_type=F32)
        ).astype(BF)
        return carry

    lax.fori_loop(0, dw // 256, project_out, 0)
    leave = pltpu.make_async_copy(tout_ref, tout_hbm, in_sem.at[15])
    leave.start()
    pending += [leave.wait]

    await_bytes(r5r.at[rest, :], xr.at[8])
    fA[...] = r5r[...].astype(F32)
    for j in range(nk):
        lout_ref[:, j * 128 : (j + 1) * 128] = fA[pl.ds(j, share, stride=nk), :].astype(BF)

    for done in pending:
        done()


def hand_over(a_ref, b_ref, a_out, b_out, a, b, came, left):
    rows = a.shape[0] // 4
    parts = [pl.ds(i * rows, rows) for i in range(4)]
    trips = [(a_ref.at[p, :], a.at[p, :], a_out.at[p, :]) for p in parts] + [(b_ref, b, b_out)]
    loads = [pltpu.make_async_copy(t[0], t[1], came.at[i]) for i, t in enumerate(trips)]
    stores = [pltpu.make_async_copy(t[1], t[2], left.at[i]) for i, t in enumerate(trips)]
    for copy in loads:
        copy.start()
    for load, store in zip(loads, stores):
        load.wait()
        store.start()
    for copy in stores:
        copy.wait()


def per_device(
    nh,
    nc,
    tokens,
    ln_gain,
    w_qkv,
    w_out,
    neighbours,
    counts,
    latents,
    lat_gain,
    w_lat_q,
    w_lat_o,
    mlp_gain,
    w_up,
    w_down,
):
    nrow, dw = tokens.shape[1:]
    nlat = latents.shape[0]
    gtok = nrow * nh
    per = nlat // nc
    share = nlat // nh
    nblk = gtok // BLK
    two = share // nc * (dw // 128)
    hbm = pl.BlockSpec(memory_space=pltpu.HBM)
    vmem = pl.BlockSpec(memory_space=pltpu.VMEM)
    stage = gtok // 4
    scratch = [
        pltpu.VMEM((nrow, dw), BF),
        pltpu.VMEM((1, dw), F32),
        pltpu.VMEM((neighbours.shape[2], nblk), jnp.int32),
        pltpu.VMEM((1, nblk), jnp.int32),
        pltpu.VMEM((1, dw), F32),
        pltpu.VMEM((dw // 128, 128), F32),
        pltpu.VMEM((nrow, dw), BF),
        pltpu.VMEM((dw, 384), BF),
        pltpu.VMEM((dw, dw), BF),
        pltpu.VMEM((nlat, dw), BF),
        pltpu.VMEM((dw, 128), BF),
        pltpu.VMEM((128, dw), BF),
        pltpu.VMEM((dw, 4 * w_up.shape[1]), BF),
        pltpu.VMEM((4 * w_down.shape[0], dw), BF),
        pltpu.VMEM((gtok, dw), BF),
        pltpu.VMEM((nlat, dw), BF),
        pltpu.VMEM((2, gtok, 128), BF),
        pltpu.VMEM((3, gtok + 2 * RIM, 128), BF),
        pltpu.VMEM((stage, 128), BF),
        pltpu.VMEM((2, stage, 128), BF),
        pltpu.VMEM((nlat, 128), F32),
        pltpu.VMEM((nlat, 128), F32),
        pltpu.VMEM((two, 128), F32),
        pltpu.VMEM((2 * nlat, 128), BF),
        pltpu.VMEM((2 * nlat, 128), F32),
        pltpu.VMEM((2 * nlat, 128), F32),
        pltpu.VMEM((two, 128), F32),
        pltpu.VMEM((WIN, nblk, 128), F32),
        pltpu.VMEM((WIN, nblk, 128), F32),
        pltpu.VMEM((nlat, 128), BF),
        pltpu.VMEM((nc, 1, 128), F32),
        pltpu.VMEM((nlat, 128), BF),
        pltpu.VMEM((nc, 1, 128), F32),
        pltpu.VMEM((nh * two, 128), F32),
        pltpu.VMEM((nh * two, 128), F32),
        pltpu.VMEM((two, 128), BF),
        pltpu.VMEM((nlat // 4, 128), BF),
        pltpu.VMEM((nlat // 4, 128), F32),
        pltpu.VMEM((nlat // 4, 128), F32),
        pltpu.VMEM((two, 128), BF),
        pltpu.VMEM((nlat, 128), BF),
        pltpu.VMEM((gtok, 128), BF),
        pltpu.VMEM((nrow, dw), BF),
        pltpu.SemaphoreType.DMA((16,)),
        pltpu.SemaphoreType.DMA((20,)),
        pltpu.SemaphoreType.DMA((20,)),
        pltpu.SemaphoreType.DMA((11,)),
        pltpu.SemaphoreType.DMA((11,)),
        pltpu.SemaphoreType.REGULAR,
        pltpu.SemaphoreType.REGULAR,
    ]
    tokens_out, latents_out = pl.pallas_call(
        functools.partial(kernel, nh, nc),
        out_shape=(
            jax.ShapeDtypeStruct((nrow, dw), BF),
            jax.ShapeDtypeStruct((share, dw), BF),
        ),
        in_specs=[hbm] * 13,
        out_specs=(hbm, vmem),
        scratch_shapes=scratch,
        compiler_params=pltpu.CompilerParams(
            collective_id=0, has_side_effects=True, vmem_limit_bytes=60 * 1024 * 1024
        ),
        name="encoder_block",
    )(
        tokens[0],
        ln_gain.reshape(1, dw),
        jnp.transpose(w_qkv, (1, 0, 2)),
        w_out,
        neighbours[0].T,
        counts,
        latents,
        lat_gain.reshape(1, dw),
        w_lat_q,
        w_lat_o,
        mlp_gain.reshape(dw // 128, 128),
        w_up,
        w_down,
    )
    tokens_out, latents_out = pl.pallas_call(
        hand_over,
        out_shape=(
            jax.ShapeDtypeStruct((nrow, dw), BF),
            jax.ShapeDtypeStruct((share, dw), BF),
        ),
        in_specs=[hbm, hbm],
        out_specs=(hbm, hbm),
        scratch_shapes=[
            pltpu.VMEM((nrow, dw), BF),
            pltpu.VMEM((share, dw), BF),
            pltpu.SemaphoreType.DMA((5,)),
            pltpu.SemaphoreType.DMA((5,)),
        ],
        compiler_params=pltpu.CompilerParams(vmem_limit_bytes=60 * 1024 * 1024),
        name="hand_over",
    )(tokens_out, latents_out)
    return (tokens_out[None], latents_out)


def solution(mesh):
    in_specs = (
        P("ctx", "heads", None),
        P(),
        P(None, None, "heads"),
        P(),
        P("ctx", None, None),
        P("ctx", None),
        P(),
        P(),
        P(None, "heads"),
        P("heads", None),
        P(),
        P(None, "ctx"),
        P("ctx", None),
    )
    out_specs = (P("ctx", "heads", None), P("heads", None))
    return jax.shard_map(
        functools.partial(per_device, mesh.shape["heads"], mesh.shape["ctx"]),
        mesh=mesh,
        in_specs=in_specs,
        out_specs=out_specs,
        check_vma=False,
    )
```

```python
import functools

import jax
import jax.numpy as jnp
from jax import lax
from jax.experimental import pallas as pl
from jax.experimental.pallas import tpu as pltpu
from jax.sharding import PartitionSpec as P

HD = 64
BLK = 128
WIN = 5
RIM = 256
EPSILON = 1e-05
SCALE2 = HD ** (-0.5) * 1.4426950408889634
MESH = pl.DeviceIdType.MESH
BF = jnp.bfloat16
F32 = jnp.float32


def aligned(start, by):
    return pl.multiple_of(start, by)


def normalise(rows, gain):
    center = jnp.mean(rows, axis=-1, keepdims=True)
    spread = jnp.mean(jnp.square(rows - center), axis=-1, keepdims=True)
    return (rows - center) * lax.rsqrt(spread + EPSILON) * gain


def kernel(
    nh,
    nc,
    tok_hbm,
    lng_hbm,
    wqkv_hbm,
    wout_hbm,
    nb_hbm,
    cnt_hbm,
    lat_hbm,
    latg_hbm,
    wlq_hbm,
    wlo_hbm,
    mg_hbm,
    wup_hbm,
    wdn_hbm,
    tout_hbm,
    r5r,
    tout_ref,
    lng_ref,
    nb_ref,
    cnt_ref,
    latg_ref,
    mg_ref,
    tok,
    wqkv,
    wout,
    lat,
    wlq,
    wlo,
    wup,
    wdn,
    G,
    latn,
    Q,
    KV,
    kst,
    vst,
    fA,
    fB,
    f2,
    qlat,
    om,
    mm,
    hl,
    multr,
    biasr,
    r1s,
    r1t,
    r1r,
    r1u,
    r2s,
    r2r,
    r3s,
    r3r,
    r4s,
    r4r,
    r5s,
    A,
    R,
    in_sem,
    gs,
    gr,
    xs,
    xr,
    row_sem,
    go_sem,
):
    h = lax.axis_index("heads")
    c = lax.axis_index("ctx")
    x = h // 2
    k = h % 2
    nrow = tok.shape[0]
    nlat = lat.shape[0]
    dw = tok.shape[1]
    nk = dw // 128
    gtok = nh * nrow
    nblk = gtok // BLK
    per = nlat // nc

    ny = 4
    nz = nc // ny
    z = c // ny
    y = lax.rem(c, ny)
    zs = [lax.rem(z + d, nz) * ny for d in range(nz)]
    ys = [lax.rem(y + d, ny) for d in range(ny)]
    own_y = pl.ds(aligned(y * 128, 128), 128)

    loads = [
        pltpu.make_async_copy(tok_hbm, tok, in_sem.at[0]),
        pltpu.make_async_copy(lat_hbm, lat, in_sem.at[1]),
        pltpu.make_async_copy(wlq_hbm, wlq, in_sem.at[2]),
        pltpu.make_async_copy(wqkv_hbm.at[0], wqkv.at[:, pl.ds(0, 128)], in_sem.at[3]),
        pltpu.make_async_copy(wqkv_hbm.at[1], wqkv.at[:, pl.ds(128, 128)], in_sem.at[4]),
        pltpu.make_async_copy(wqkv_hbm.at[2], wqkv.at[:, pl.ds(256, 128)], in_sem.at[5]),
        pltpu.make_async_copy(wlo_hbm, wlo, in_sem.at[6]),
        pltpu.make_async_copy(wup_hbm, wup.at[:, own_y], in_sem.at[7]),
        pltpu.make_async_copy(wdn_hbm, wdn.at[own_y, :], in_sem.at[8]),
        pltpu.make_async_copy(wout_hbm, wout, in_sem.at[9]),
    ]
    small = [
        pltpu.make_async_copy(lng_hbm, lng_ref, in_sem.at[10]),
        pltpu.make_async_copy(latg_hbm, latg_ref, in_sem.at[11]),
        pltpu.make_async_copy(nb_hbm, nb_ref, in_sem.at[12]),
        pltpu.make_async_copy(cnt_hbm, cnt_ref, in_sem.at[13]),
        pltpu.make_async_copy(mg_hbm, mg_ref, in_sem.at[14]),
    ]
    small[0].start()
    for load in loads[:3] + small[1:] + loads[3:]:
        load.start()

    barrier = pltpu.get_barrier_semaphore()

    def signal(sem, **to):
        pl.semaphore_signal(sem, inc=1, device_id=to, device_id_type=MESH)

    for d in range(1, nh):
        @pl.when(h != d)
        def _(d=d):
            signal(barrier, heads=d)

    loads[0].wait()
    small[0].wait()
    mine = aligned(h * nrow, 256)
    step = 32

    def norm_tokens(i, carry):
        at = pl.ds(aligned(i * step, step), step)
        G[pl.ds(aligned(mine + i * step, step), step), :] = normalise(
            tok[at, :].astype(F32), lng_ref[...]
        ).astype(BF)
        return carry

    lax.fori_loop(0, nrow // step, norm_tokens, 0)

    @pl.when(h != 0)
    def _():
        pl.semaphore_wait(barrier, nh - 1)

    @pl.when(h == 1)
    def _():
        signal(row_sem, heads=0)

    @pl.when(h == 0)
    def _():
        pl.semaphore_wait(row_sem, 1)


    sib = x * 2 + (1 - k)
    right = lax.rem(x + 1, nh // 2) * 2 + k
    left = lax.rem(x + nh // 2 - 1, nh // 2) * 2 + k
    far = lax.rem(x + 2, nh // 2) * 2 + k
    right_s = lax.rem(x + 1, nh // 2) * 2 + (1 - k)
    left_s = lax.rem(x + nh // 2 - 1, nh // 2) * 2 + (1 - k)
    far_s = lax.rem(x + 2, nh // 2) * 2 + (1 - k)

    quarter = nrow // 4

    def move(block, part, parts, sem, to):
        rows = pl.ds(aligned(block * nrow + part * quarter, quarter), parts * quarter)
        return pltpu.make_async_remote_copy(
            src_ref=G.at[rows, :],
            dst_ref=G.at[rows, :],
            send_sem=gs.at[sem],
            recv_sem=gr.at[sem],
            device_id={"heads": to},
            device_id_type=MESH,
        )

    pending = []
    sends = []
    for i in range(4):
        sends += [move(h, i, 1, 1 + i, right), move(h, 3 - i, 1, 8 - i, left)]
        if i == 1:
            sends += [move(h, 0, 4, 0, sib)]
    for send in sends:
        send.start()
    pending += [send.wait_send for send in sends]

    steps = sorted(
        ((dz, dy) for dz in range(nz) for dy in range(ny) if dz or dy),
        key=lambda d: -(min(d[0], nz - d[0]) + min(d[1], ny - d[1])),
    )
    others = [zs[dz] + ys[dy] for dz, dy in steps]
    z_peers = [zs[dz] + y for dz, dy in steps if dy == 0]
    y_steps = [dy for dz, dy in steps if dz == 0]

    @pl.when(h == 0)
    def _():
        for to in others:
            signal(barrier, ctx=to)


    loads[1].wait()
    for load in small[1:]:
        load.wait()

    def norm_latents(i, carry):
        at = pl.ds(aligned(i * step, step), step)
        latn[at, :] = normalise(lat[at, :].astype(F32), latg_ref[...]).astype(BF)
        return carry

    lax.fori_loop(0, nlat // step, norm_latents, 0)
    loads[2].wait()
    fA[...] = jnp.dot(latn[...], wlq[...], preferred_element_type=F32)
    share = nlat // nh
    two = share // nc
    for hh in range(nh):
        for i in range(two):
            fB[pl.ds(hh * two + i, nc, stride=per), :] = fA[
                pl.ds(hh * share + i, nc, stride=two), :
            ]
    lane = lax.broadcasted_iota(jnp.int32, (nlat, 128), 1)
    lq = fB[...]
    qlat[pl.ds(0, nlat), :] = jnp.where(lane < HD, lq, 0.0).astype(BF)
    qlat[pl.ds(nlat, nlat), :] = jnp.where(lane < HD, 0.0, lq).astype(BF)
    om[...] = jnp.zeros_like(om)
    mm[...] = jnp.full_like(mm, -jnp.inf)

    own64 = lat[pl.ds(aligned(h * share, share), share), :].astype(F32)
    for j in range(nk):
        fA[pl.ds(j, share, stride=nk), :] = own64[:, j * 128 : (j + 1) * 128]
    hl[...] = fA[pl.ds(aligned(c * two * nk, two * nk), two * nk), :]

    slot = lax.broadcasted_iota(jnp.int32, nb_ref.shape, 0)
    column = lax.broadcasted_iota(jnp.int32, nb_ref.shape, 1)
    live = slot < cnt_ref[...]
    eye = lax.broadcasted_iota(jnp.int32, (nblk, nblk), 0) == lax.broadcasted_iota(
        jnp.int32, (nblk, nblk), 1
    )
    for j in range(WIN):
        hits = jnp.where(live & (nb_ref[...] == column + j), 1.0, 0.0)
        times = jnp.sum(hits, axis=0, keepdims=True)
        times = jnp.sum(jnp.where(eye, times, 0.0), axis=1, keepdims=True)
        times = jnp.broadcast_to(times, (nblk, 128))
        multr[j] = times
        biasr[j] = jnp.where(times > 0.0, 0.0, -jnp.inf)

    def project(pieces):
        spans = [
            (aligned(block * nrow + part * quarter, quarter), parts * quarter)
            for block, part, parts in pieces
        ]
        rows = jnp.concatenate([G[pl.ds(s, size), :] for s, size in spans], axis=0)
        made = jnp.dot(rows, wqkv[...], preferred_element_type=F32)
        at = 0
        for s, size in spans:
            part = slice(at, at + size)
            at += size
            first = lax.broadcasted_iota(jnp.int32, (size, 128), 1) < HD
            q = made[part, 0:128]
            key = made[part, 128:256].astype(BF)
            v = made[part, 256:384]
            v0 = jnp.where(first, v, 1.0).astype(BF)
            v1 = jnp.where(first, 1.0, v).astype(BF)
            Q[0, pl.ds(s, size), :] = jnp.where(first, q, 0.0).astype(BF)
            Q[1, pl.ds(s, size), :] = jnp.where(first, 0.0, q).astype(BF)
            wide = pl.ds(aligned(s + RIM, quarter), size)
            KV[0, wide, :] = key
            KV[1, wide, :] = v0
            KV[2, wide, :] = v1
            kst[part, :] = key
            vst[0, part, :] = v0
            vst[1, part, :] = v1
        return at

    def cross(keys, t):
        at = pl.ds(t * nlat, nlat)
        s = lax.dot_general(
            qlat[at, :],
            kst[pl.ds(0, keys), :],
            (((1,), (1,)), ((), ())),
            preferred_element_type=F32,
        )
        before = mm[at, :]
        top = jnp.maximum(before, jnp.max(s, axis=1, keepdims=True))
        alpha = jnp.exp2((before - top) * SCALE2)
        p = jnp.concatenate(
            [
                jnp.exp2((s[:, j * 128 : (j + 1) * 128] - top) * SCALE2).astype(BF)
                for j in range(keys // 128)
            ],
            axis=1,
        )
        mm[at, :] = top
        om[at, :] = om[at, :] * alpha + jnp.dot(
            p, vst[t, pl.ds(0, keys), :], preferred_element_type=F32
        )

    def stage(pieces):
        keys = project(pieces)
        for t in range(2):
            cross(keys, t)

    def start(copies):
        for copy in copies:
            copy.start()
        pending.extend([copy.wait_send for copy in copies])

    move(left, 0, 1, 1, right).wait_recv()
    move(right, 3, 1, 8, left).wait_recv()
    start([move(left, 0, 1, 9, right), move(right, 3, 1, 12, left)])
    for i in (3, 4, 5):
        loads[i].wait()
    move(sib, 0, 4, 0, sib).wait_recv()
    stage([(h, 0, 4), (sib, 0, 4)])

    @pl.when(h == 0)
    def _():
        pl.semaphore_wait(barrier, nc - 1)
        for d in range(1, nh):
            signal(go_sem, heads=d)


    move(left, 1, 1, 2, right).wait_recv()
    move(right, 2, 1, 7, left).wait_recv()
    start([move(left, 1, 1, 10, right), move(right, 2, 1, 11, left)])
    start([move(left, 0, 2, 13, sib), move(right, 2, 2, 14, sib)])
    move(left_s, 0, 2, 13, sib).wait_recv()
    move(right_s, 2, 2, 14, sib).wait_recv()
    stage([(left, 0, 2), (right, 2, 2), (left_s, 0, 2), (right_s, 2, 2)])

    @pl.when(h != 0)
    def _():
        pl.semaphore_wait(go_sem, 1)

    loads[7].wait()
    loads[8].wait()

    def share_weight(ref, sem, **to):
        pltpu.make_async_remote_copy(
            src_ref=ref,
            dst_ref=ref,
            send_sem=xs.at[sem],
            recv_sem=xr.at[sem],
            device_id=to,
            device_id_type=MESH,
        ).start()

    @pl.when(k == 0)
    def _():
        for dy in y_steps:
            share_weight(wup.at[:, own_y], 9, ctx=zs[0] + ys[dy])

    @pl.when(k == 1)
    def _():
        for dy in y_steps:
            share_weight(wdn.at[own_y, :], 9, ctx=zs[0] + ys[dy])

    for i in (2, 3):
        move(left, i, 1, 1 + i, right).wait_recv()
        move(right, 3 - i, 1, 8 - i, left).wait_recv()
    start([move(left, 2, 2, 15, sib), move(right, 0, 2, 16, sib)])

    move(left_s, 2, 2, 15, sib).wait_recv()
    move(right_s, 0, 2, 16, sib).wait_recv()
    stage([(left, 2, 2), (right, 0, 2), (left_s, 2, 2), (right_s, 0, 2)])

    move(far, 0, 1, 9, right).wait_recv()
    move(far, 3, 1, 12, left).wait_recv()
    start([move(far, 0, 1, 17, sib), move(far, 3, 1, 18, sib)])
    move(far_s, 0, 1, 17, sib).wait_recv()
    move(far_s, 3, 1, 18, sib).wait_recv()
    stage([(far, 0, 1), (far, 3, 1), (far_s, 0, 1), (far_s, 3, 1)])

    move(far, 1, 1, 10, right).wait_recv()
    move(far, 2, 1, 11, left).wait_recv()
    start([move(far, 1, 2, 19, sib)])
    move(far_s, 1, 2, 19, sib).wait_recv()
    stage([(far, 1, 2), (far_s, 1, 2)])

    tile1 = 128
    lane1 = lax.broadcasted_iota(jnp.int32, (tile1, 128), 1)
    row1 = lax.broadcasted_iota(jnp.int32, (tile1, 128), 0)
    first1 = lane1 < HD
    pick1 = lax.rem(lane1, HD) == lax.rem(row1, per)
    for t in range(nlat // tile1):
        at0 = pl.ds(t * tile1, tile1)
        at1 = pl.ds(nlat + t * tile1, tile1)
        o0, o1 = om[at0, :], om[at1, :]
        total = pltpu.roll(jnp.where(first1, o1, o0), HD, 1)
        r1s[at0, :] = (jnp.where(first1, o0, o1) / total).astype(BF)
        lse = jnp.where(first1, mm[at0, :], mm[at1, :]) * SCALE2 + jnp.log2(total)
        lse = jnp.where(pick1, lse, 0.0)
        for g in range(tile1 // per):
            r1t[t * (tile1 // per) + g] = jnp.sum(
                lse[g * per : (g + 1) * per, :], axis=0, keepdims=True
            )

    own_c = pl.ds(aligned(c * per, 16), per)
    def to_ctx(src, dst, s, r, peers=others):
        for to in peers:
            pltpu.make_async_remote_copy(
                src_ref=src(to),
                dst_ref=dst,
                send_sem=xs.at[s],
                recv_sem=xr.at[r],
                device_id={"ctx": to},
                device_id_type=MESH,
            ).start()

    def spread(i, src, dst):
        to_ctx(lambda to: src.at[pl.ds(aligned(to * per, 16), per), :], dst.at[own_c, :], i, i)

    def await_bytes(ref, sem):
        pltpu.make_async_copy(ref, ref, sem).wait()

    rest = pl.ds(0, (nc - 1) * per)
    to_ctx(lambda to: r1t.at[to], r1u.at[c], 1, 1)
    spread(0, r1s, r1r)
    r1r[own_c, :] = r1s[own_c, :]
    r1u[c] = r1t[c]

    def rim(src, dst, sem, to):
        return pltpu.make_async_remote_copy(
            src_ref=KV.at[:, pl.ds(src, RIM), :],
            dst_ref=KV.at[:, pl.ds(dst, RIM), :],
            send_sem=xs.at[sem],
            recv_sem=xr.at[sem],
            device_id={"ctx": to},
            device_id_type=MESH,
        )

    rims = [
        rim(RIM, RIM + gtok, 2, lax.rem(c + nc - 1, nc)),
        rim(gtok, 0, 3, lax.rem(c + 1, nc)),
    ]
    for r in rims:
        r.start()
    pending += [r.wait_send for r in rims]
    pending += [lambda: await_bytes(r1r.at[rest, :], xs.at[0])]
    pending += [lambda: await_bytes(r1u.at[pl.ds(0, nc - 1)], xs.at[1])]

    firstb = lax.broadcasted_iota(jnp.int32, (BLK, 128), 1) < HD

    def attend(b):
        at = pl.ds(aligned(b * BLK, BLK), BLK)
        win = pl.ds(aligned(b * BLK, BLK), WIN * BLK)
        q = jnp.concatenate([Q[0, at, :], Q[1, at, :]], axis=0)
        s = lax.dot_general(
            q, KV[0, win, :], (((1,), (1,)), ((), ())), preferred_element_type=F32
        )
        parts = [
            s[:, j * BLK : (j + 1) * BLK] + biasr[j, pl.ds(b, 1), :] for j in range(WIN)
        ]
        top = parts[0]
        for part in parts[1:]:
            top = jnp.maximum(top, part)
        top = jnp.max(top, axis=1, keepdims=True)
        p = jnp.concatenate(
            [
                (jnp.exp2((part - top) * SCALE2) * multr[j, pl.ds(b, 1), :]).astype(BF)
                for j, part in enumerate(parts)
            ],
            axis=1,
        )
        o0 = jnp.dot(p[:BLK], KV[1, win, :], preferred_element_type=F32)
        o1 = jnp.dot(p[BLK:], KV[2, win, :], preferred_element_type=F32)
        total = pltpu.roll(jnp.where(firstb, o1, o0), HD, 1)
        A[at, :] = (jnp.where(firstb, o0, o1) / total).astype(BF)

    def attend_four(i, carry):
        for j in range(4):
            attend(2 + 4 * i + j)
        return carry

    lax.fori_loop(0, 2, attend_four, 0)

    await_bytes(r1r.at[rest, :], xr.at[0])
    await_bytes(r1u.at[pl.ds(0, nc - 1)], xr.at[1])
    lanes = lax.broadcasted_iota(jnp.int32, (per, 128), 1)
    pick = lax.rem(lanes, HD) == lax.broadcasted_iota(jnp.int32, (per, 128), 0)
    for i in range(nc):
        fA[pl.ds(i * per, per), :] = jnp.where(pick, r1u[i], 0.0)
    same = (
        lax.broadcasted_iota(jnp.int32, (128, 128), 0) // HD
        == lax.broadcasted_iota(jnp.int32, (128, 128), 1) // HD
    )
    fB[...] = jnp.dot(
        fA[...],
        jnp.where(same, 1.0, 0.0),
        preferred_element_type=F32,
        precision=lax.Precision.HIGHEST,
    )
    peak = fB[pl.ds(0, per), :]
    for i in range(1, nc):
        peak = jnp.maximum(peak, fB[pl.ds(i * per, per), :])
    weight = jnp.zeros((per, 128), F32)
    value = jnp.zeros((per, 128), F32)
    for i in range(nc):
        w = jnp.exp2(fB[pl.ds(i * per, per), :] - peak)
        weight += w
        value += w * r1r[pl.ds(i * per, per), :].astype(F32)
    lat_att = (value / weight).astype(BF)

    loads[6].wait()
    made = jnp.dot(lat_att, wlo[...], preferred_element_type=F32)
    for j in range(nk):
        r2s[pl.ds(j, per, stride=nk), :] = made[:, j * 128 : (j + 1) * 128]
    rest2 = pl.ds(0, (nh - 1) * two * nk)
    own_h = pl.ds(aligned(h * two * nk, 16), two * nk)

    def send2(d, carry):
        to = lax.rem(h + d, nh)
        pltpu.make_async_remote_copy(
            src_ref=r2s.at[pl.ds(aligned(to * two * nk, 16), two * nk), :],
            dst_ref=r2r.at[own_h, :],
            send_sem=xs.at[4],
            recv_sem=xr.at[4],
            device_id={"heads": to},
            device_id_type=MESH,
        ).start()
        return carry

    lax.fori_loop(1, nh, send2, 0)
    r2r[own_h, :] = r2s[own_h, :]
    pending += [lambda: await_bytes(r2r.at[rest2, :], xs.at[4])]

    foreign = (ny - 1) * 128

    @pl.when(k == 0)
    def _():
        await_bytes(wup.at[:, pl.ds(0, foreign)], xr.at[9])
        for dy in y_steps:
            share_weight(wup.at[:, pl.ds(aligned(ys[dy] * 128, 128), 128)], 10, heads=sib)

    @pl.when(k == 1)
    def _():
        await_bytes(wdn.at[pl.ds(0, foreign), :], xr.at[9])
        for dy in y_steps:
            share_weight(wdn.at[pl.ds(aligned(ys[dy] * 128, 128), 128), :], 10, heads=sib)

    pending += [lambda: await_bytes(wup.at[:, pl.ds(0, foreign)], xs.at[9])]
    pending += [lambda: await_bytes(wup.at[:, pl.ds(0, foreign)], xs.at[10])]

    lax.fori_loop(2, (nblk - 4) // 4, attend_four, 0)

    await_bytes(r2r.at[rest2, :], xr.at[4])
    hidden = hl[...]
    for i in range(nh):
        hidden += r2r[pl.ds(i * two * nk, two * nk), :]
    hl[...] = hidden
    for i in range(two):
        row = hidden[i * nk : (i + 1) * nk, :]
        center = jnp.sum(jnp.sum(row, axis=0, keepdims=True), axis=1, keepdims=True) / dw
        off = row - center
        spread2 = (
            jnp.sum(jnp.sum(jnp.square(off), axis=0, keepdims=True), axis=1, keepdims=True) / dw
        )
        f2[pl.ds(i * nk, nk), :] = off * lax.rsqrt(spread2 + EPSILON) * mg_ref[...]
    r3s[...] = f2[...].astype(BF)
    own_z = pl.ds(aligned(z * per, 16), per)
    restz = pl.ds(0, (nz - 1) * per)
    to_ctx(lambda to: r3s, r3r.at[own_z, :], 5, 5, z_peers)
    r3r[own_z, :] = r3s[...]
    pending += [lambda: await_bytes(r3r.at[restz, :], xs.at[5])]

    for r in rims:
        r.wait_recv()
    for b in (0, 1, nblk - 2, nblk - 1):
        attend(b)

    head_cols = pl.ds(aligned(h * 128, 128), 128)

    def send_back(d, carry):
        to = lax.rem(h + d, nh)
        pltpu.make_async_remote_copy(
            src_ref=A.at[pl.ds(aligned(to * nrow, 128), nrow), :],
            dst_ref=R.at[:, head_cols],
            send_sem=xs.at[6],
            recv_sem=xr.at[6],
            device_id={"heads": to},
            device_id_type=MESH,
        ).start()
        return carry

    lax.fori_loop(1, nh, send_back, 0)
    R[:, head_cols] = A[pl.ds(mine, nrow), :]
    pending += [lambda: await_bytes(A.at[pl.ds(0, (nh - 1) * nrow), :], xs.at[6])]

    await_bytes(r3r.at[restz, :], xr.at[5])
    await_bytes(wup.at[:, pl.ds(0, foreign)], xr.at[10])
    group = nz * two
    fA[pl.ds(0, nz * per), :] = r3r[...].astype(F32)
    rows = jnp.concatenate(
        [fA[pl.ds(j, group, stride=nk), :].astype(BF) for j in range(nk)], axis=1
    )
    inner = jax.nn.gelu(
        jnp.dot(rows, wup[...], preferred_element_type=F32), approximate=True
    ).astype(BF)
    made = jnp.dot(inner, wdn[...], preferred_element_type=F32)
    for j in range(nk):
        r4s[pl.ds(j, group, stride=nk), :] = made[:, j * 128 : (j + 1) * 128]
    to_ctx(
        lambda to: r4s.at[pl.ds(aligned(to // ny * per, 16), per), :],
        r4r.at[own_z, :],
        7,
        7,
        z_peers,
    )
    r4r[own_z, :] = r4s[own_z, :]
    pending += [lambda: await_bytes(r4r.at[restz, :], xs.at[7])]

    await_bytes(r4r.at[restz, :], xr.at[7])
    total = hl[...]
    for i in range(nz):
        total += r4r[pl.ds(i * per, per), :]
    r5s[...] = total.astype(BF)
    to_ctx(lambda to: r5s, r5r.at[own_c, :], 8, 8)
    own5 = pltpu.make_async_copy(r5s, r5r.at[own_c, :], in_sem.at[16])
    own5.start()
    pending += [own5.wait]
    pending += [lambda: await_bytes(r5r.at[rest, :], xs.at[8])]
    loads[9].wait()
    await_bytes(A.at[pl.ds(0, (nh - 1) * nrow), :], xr.at[6])

    def project_out(n, carry):
        cols = pl.ds(aligned(n * 256, 256), 256)
        tout_ref[:, cols] = (
            tok[:, cols].astype(F32)
            + jnp.dot(R[...], wout[:, cols], preferred_element_type=F32)
        ).astype(BF)
        return carry

    lax.fori_loop(0, dw // 256, project_out, 0)
    leave = pltpu.make_async_copy(tout_ref, tout_hbm, in_sem.at[15])
    leave.start()
    pending += [leave.wait]

    await_bytes(r5r.at[rest, :], xr.at[8])

    for done in pending:
        done()


def hand_over(a_ref, b_ref, a_out, b_out, a, b, f, r, came, left):
    rows = a.shape[0] // 4
    parts = [pl.ds(i * rows, rows) for i in range(4)]
    latents = pltpu.make_async_copy(b_ref, b, came.at[4])
    loads = [pltpu.make_async_copy(a_ref.at[p, :], a.at[p, :], came.at[i]) for i, p in enumerate(parts)]
    stores = [pltpu.make_async_copy(a.at[p, :], a_out.at[p, :], left.at[i]) for i, p in enumerate(parts)]
    stores += [pltpu.make_async_copy(r, b_out, left.at[4])]
    latents.start()
    for copy in loads:
        copy.start()
    latents.wait()
    f[...] = b[...].astype(F32)
    share, dw = r.shape
    nk = dw // 128
    for j in range(nk):
        r[:, j * 128 : (j + 1) * 128] = f[pl.ds(j, share, stride=nk), :].astype(BF)
    stores[4].start()
    for load, store in zip(loads, stores):
        load.wait()
        store.start()
    for copy in stores:
        copy.wait()


def per_device(
    nh,
    nc,
    tokens,
    ln_gain,
    w_qkv,
    w_out,
    neighbours,
    counts,
    latents,
    lat_gain,
    w_lat_q,
    w_lat_o,
    mlp_gain,
    w_up,
    w_down,
):
    nrow, dw = tokens.shape[1:]
    nlat = latents.shape[0]
    gtok = nrow * nh
    per = nlat // nc
    share = nlat // nh
    nblk = gtok // BLK
    two = share // nc * (dw // 128)
    hbm = pl.BlockSpec(memory_space=pltpu.HBM)
    vmem = pl.BlockSpec(memory_space=pltpu.VMEM)
    stage = gtok // 4
    scratch = [
        pltpu.VMEM((nrow, dw), BF),
        pltpu.VMEM((1, dw), F32),
        pltpu.VMEM((neighbours.shape[2], nblk), jnp.int32),
        pltpu.VMEM((1, nblk), jnp.int32),
        pltpu.VMEM((1, dw), F32),
        pltpu.VMEM((dw // 128, 128), F32),
        pltpu.VMEM((nrow, dw), BF),
        pltpu.VMEM((dw, 384), BF),
        pltpu.VMEM((dw, dw), BF),
        pltpu.VMEM((nlat, dw), BF),
        pltpu.VMEM((dw, 128), BF),
        pltpu.VMEM((128, dw), BF),
        pltpu.VMEM((dw, 4 * w_up.shape[1]), BF),
        pltpu.VMEM((4 * w_down.shape[0], dw), BF),
        pltpu.VMEM((gtok, dw), BF),
        pltpu.VMEM((nlat, dw), BF),
        pltpu.VMEM((2, gtok, 128), BF),
        pltpu.VMEM((3, gtok + 2 * RIM, 128), BF),
        pltpu.VMEM((stage, 128), BF),
        pltpu.VMEM((2, stage, 128), BF),
        pltpu.VMEM((nlat, 128), F32),
        pltpu.VMEM((nlat, 128), F32),
        pltpu.VMEM((two, 128), F32),
        pltpu.VMEM((2 * nlat, 128), BF),
        pltpu.VMEM((2 * nlat, 128), F32),
        pltpu.VMEM((2 * nlat, 128), F32),
        pltpu.VMEM((two, 128), F32),
        pltpu.VMEM((WIN, nblk, 128), F32),
        pltpu.VMEM((WIN, nblk, 128), F32),
        pltpu.VMEM((nlat, 128), BF),
        pltpu.VMEM((nc, 1, 128), F32),
        pltpu.VMEM((nlat, 128), BF),
        pltpu.VMEM((nc, 1, 128), F32),
        pltpu.VMEM((nh * two, 128), F32),
        pltpu.VMEM((nh * two, 128), F32),
        pltpu.VMEM((two, 128), BF),
        pltpu.VMEM((nlat // 4, 128), BF),
        pltpu.VMEM((nlat // 4, 128), F32),
        pltpu.VMEM((nlat // 4, 128), F32),
        pltpu.VMEM((two, 128), BF),
        pltpu.VMEM((gtok, 128), BF),
        pltpu.VMEM((nrow, dw), BF),
        pltpu.SemaphoreType.DMA((17,)),
        pltpu.SemaphoreType.DMA((20,)),
        pltpu.SemaphoreType.DMA((20,)),
        pltpu.SemaphoreType.DMA((11,)),
        pltpu.SemaphoreType.DMA((11,)),
        pltpu.SemaphoreType.REGULAR,
        pltpu.SemaphoreType.REGULAR,
    ]
    tokens_out, rows_out = pl.pallas_call(
        functools.partial(kernel, nh, nc),
        out_shape=(
            jax.ShapeDtypeStruct((nrow, dw), BF),
            jax.ShapeDtypeStruct((nlat, 128), BF),
        ),
        in_specs=[hbm] * 13,
        out_specs=(hbm, hbm),
        scratch_shapes=scratch,
        compiler_params=pltpu.CompilerParams(
            collective_id=0, has_side_effects=True, vmem_limit_bytes=60 * 1024 * 1024
        ),
        name="encoder_block",
    )(
        tokens[0],
        ln_gain.reshape(1, dw),
        jnp.transpose(w_qkv, (1, 0, 2)),
        w_out,
        neighbours[0].T,
        counts,
        latents,
        lat_gain.reshape(1, dw),
        w_lat_q,
        w_lat_o,
        mlp_gain.reshape(dw // 128, 128),
        w_up,
        w_down,
    )
    tokens_out, latents_out = pl.pallas_call(
        hand_over,
        out_shape=(
            jax.ShapeDtypeStruct((nrow, dw), BF),
            jax.ShapeDtypeStruct((share, dw), BF),
        ),
        in_specs=[hbm, hbm],
        out_specs=(hbm, hbm),
        scratch_shapes=[
            pltpu.VMEM((nrow, dw), BF),
            pltpu.VMEM((nlat, 128), BF),
            pltpu.VMEM((nlat, 128), F32),
            pltpu.VMEM((share, dw), BF),
            pltpu.SemaphoreType.DMA((5,)),
            pltpu.SemaphoreType.DMA((5,)),
        ],
        compiler_params=pltpu.CompilerParams(vmem_limit_bytes=60 * 1024 * 1024),
        name="hand_over",
    )(tokens_out, rows_out)
    return (tokens_out[None], latents_out)


def solution(mesh):
    in_specs = (
        P("ctx", "heads", None),
        P(),
        P(None, None, "heads"),
        P(),
        P("ctx", None, None),
        P("ctx", None),
        P(),
        P(),
        P(None, "heads"),
        P("heads", None),
        P(),
        P(None, "ctx"),
        P("ctx", None),
    )
    out_specs = (P("ctx", "heads", None), P("heads", None))
    return jax.shard_map(
        functools.partial(per_device, mesh.shape["heads"], mesh.shape["ctx"]),
        mesh=mesh,
        in_specs=in_specs,
        out_specs=out_specs,
        check_vma=False,
    )
```

```python
import functools

import jax
import jax.numpy as jnp
from jax import lax
from jax.experimental import pallas as pl
from jax.experimental.pallas import tpu as pltpu
from jax.sharding import PartitionSpec as P

HD = 64
BLK = 128
WIN = 5
RIM = 256
EPSILON = 1e-05
SCALE2 = HD ** (-0.5) * 1.4426950408889634
MESH = pl.DeviceIdType.MESH
BF = jnp.bfloat16
F32 = jnp.float32


def aligned(start, by):
    return pl.multiple_of(start, by)


def normalise(rows, gain):
    center = jnp.mean(rows, axis=-1, keepdims=True)
    spread = jnp.mean(jnp.square(rows - center), axis=-1, keepdims=True)
    return (rows - center) * lax.rsqrt(spread + EPSILON) * gain


def kernel(
    nh,
    nc,
    tok_hbm,
    lng_hbm,
    wqkv_hbm,
    wout_hbm,
    nb_hbm,
    cnt_hbm,
    lat_hbm,
    latg_hbm,
    wlq_hbm,
    wlo_hbm,
    mg_hbm,
    wup_hbm,
    wdn_hbm,
    tout_hbm,
    r5r,
    tout_ref,
    lng_ref,
    nb_ref,
    cnt_ref,
    latg_ref,
    mg_ref,
    tok,
    wqkv,
    wout,
    lat,
    wlq,
    wlo,
    wup,
    wdn,
    G,
    latn,
    Q,
    KV,
    kst,
    vst,
    fA,
    fB,
    f2,
    qlat,
    om,
    mm,
    hl,
    multr,
    biasr,
    r1s,
    r1t,
    r1r,
    r1u,
    r2s,
    r2r,
    r3s,
    r3r,
    r4s,
    r4r,
    r5s,
    A,
    R,
    in_sem,
    gs,
    gr,
    xs,
    xr,
    row_sem,
    go_sem,
):
    h = lax.axis_index("heads")
    c = lax.axis_index("ctx")
    x = h // 2
    k = h % 2
    nrow = tok.shape[0]
    nlat = lat.shape[0]
    dw = tok.shape[1]
    nk = dw // 128
    gtok = nh * nrow
    nblk = gtok // BLK
    per = nlat // nc

    ny = 4
    nz = nc // ny
    z = c // ny
    y = lax.rem(c, ny)
    way = 1 - 2 * k
    zs = [lax.rem(z + nz + way * d, nz) * ny for d in range(nz)]
    ys = [lax.rem(y + ny + way * d, ny) for d in range(ny)]
    own_y = pl.ds(aligned(y * 128, 128), 128)

    loads = [
        pltpu.make_async_copy(tok_hbm, tok, in_sem.at[0]),
        pltpu.make_async_copy(lat_hbm, lat, in_sem.at[1]),
        pltpu.make_async_copy(wlq_hbm, wlq, in_sem.at[2]),
        pltpu.make_async_copy(wqkv_hbm.at[0], wqkv.at[:, pl.ds(0, 128)], in_sem.at[3]),
        pltpu.make_async_copy(wqkv_hbm.at[1], wqkv.at[:, pl.ds(128, 128)], in_sem.at[4]),
        pltpu.make_async_copy(wqkv_hbm.at[2], wqkv.at[:, pl.ds(256, 128)], in_sem.at[5]),
        pltpu.make_async_copy(wlo_hbm, wlo, in_sem.at[6]),
        pltpu.make_async_copy(wup_hbm, wup.at[:, own_y], in_sem.at[7]),
        pltpu.make_async_copy(wdn_hbm, wdn.at[own_y, :], in_sem.at[8]),
        pltpu.make_async_copy(wout_hbm, wout, in_sem.at[9]),
    ]
    small = [
        pltpu.make_async_copy(lng_hbm, lng_ref, in_sem.at[10]),
        pltpu.make_async_copy(latg_hbm, latg_ref, in_sem.at[11]),
        pltpu.make_async_copy(nb_hbm, nb_ref, in_sem.at[12]),
        pltpu.make_async_copy(cnt_hbm, cnt_ref, in_sem.at[13]),
        pltpu.make_async_copy(mg_hbm, mg_ref, in_sem.at[14]),
    ]
    small[0].start()
    for load in loads[:3] + small[1:] + loads[3:]:
        load.start()

    barrier = pltpu.get_barrier_semaphore()

    def signal(sem, **to):
        pl.semaphore_signal(sem, inc=1, device_id=to, device_id_type=MESH)

    for d in range(1, nh):
        @pl.when(h != d)
        def _(d=d):
            signal(barrier, heads=d)

    loads[0].wait()
    small[0].wait()
    mine = aligned(h * nrow, 256)
    step = 32

    def norm_tokens(i, carry):
        at = pl.ds(aligned(i * step, step), step)
        G[pl.ds(aligned(mine + i * step, step), step), :] = normalise(
            tok[at, :].astype(F32), lng_ref[...]
        ).astype(BF)
        return carry

    lax.fori_loop(0, nrow // step, norm_tokens, 0)

    @pl.when(h != 0)
    def _():
        pl.semaphore_wait(barrier, nh - 1)

    @pl.when(h == 1)
    def _():
        signal(row_sem, heads=0)

    @pl.when(h == 0)
    def _():
        pl.semaphore_wait(row_sem, 1)


    sib = x * 2 + (1 - k)
    right = lax.rem(x + 1, nh // 2) * 2 + k
    left = lax.rem(x + nh // 2 - 1, nh // 2) * 2 + k
    far = lax.rem(x + 2, nh // 2) * 2 + k
    right_s = lax.rem(x + 1, nh // 2) * 2 + (1 - k)
    left_s = lax.rem(x + nh // 2 - 1, nh // 2) * 2 + (1 - k)
    far_s = lax.rem(x + 2, nh // 2) * 2 + (1 - k)

    quarter = nrow // 4

    def move(block, part, parts, sem, to):
        rows = pl.ds(aligned(block * nrow + part * quarter, quarter), parts * quarter)
        return pltpu.make_async_remote_copy(
            src_ref=G.at[rows, :],
            dst_ref=G.at[rows, :],
            send_sem=gs.at[sem],
            recv_sem=gr.at[sem],
            device_id={"heads": to},
            device_id_type=MESH,
        )

    pending = []
    sends = []
    for i in range(4):
        sends += [move(h, i, 1, 1 + i, right), move(h, 3 - i, 1, 8 - i, left)]
        if i == 1:
            sends += [move(h, 0, 4, 0, sib)]
    for send in sends:
        send.start()
    pending += [send.wait_send for send in sends]

    steps = sorted(
        ((dz, dy) for dz in range(nz) for dy in range(ny) if dz or dy),
        key=lambda d: -(min(d[0], nz - d[0]) + min(d[1], ny - d[1])),
    )
    others = [zs[dz] + ys[dy] for dz, dy in steps]
    z_peers = [zs[dz] + y for dz, dy in steps if dy == 0]
    y_steps = [dy for dz, dy in steps if dz == 0]

    @pl.when(h == 0)
    def _():
        for to in others:
            signal(barrier, ctx=to)


    loads[1].wait()
    for load in small[1:]:
        load.wait()

    def norm_latents(i, carry):
        at = pl.ds(aligned(i * step, step), step)
        latn[at, :] = normalise(lat[at, :].astype(F32), latg_ref[...]).astype(BF)
        return carry

    lax.fori_loop(0, nlat // step, norm_latents, 0)
    loads[2].wait()
    fA[...] = jnp.dot(latn[...], wlq[...], preferred_element_type=F32)
    share = nlat // nh
    two = share // nc
    for hh in range(nh):
        for i in range(two):
            fB[pl.ds(hh * two + i, nc, stride=per), :] = fA[
                pl.ds(hh * share + i, nc, stride=two), :
            ]
    lane = lax.broadcasted_iota(jnp.int32, (nlat, 128), 1)
    lq = fB[...]
    qlat[pl.ds(0, nlat), :] = jnp.where(lane < HD, lq, 0.0).astype(BF)
    qlat[pl.ds(nlat, nlat), :] = jnp.where(lane < HD, 0.0, lq).astype(BF)
    om[...] = jnp.zeros_like(om)
    mm[...] = jnp.full_like(mm, -jnp.inf)

    own64 = lat[pl.ds(aligned(h * share, share), share), :].astype(F32)
    for j in range(nk):
        fA[pl.ds(j, share, stride=nk), :] = own64[:, j * 128 : (j + 1) * 128]
    hl[...] = fA[pl.ds(aligned(c * two * nk, two * nk), two * nk), :]

    slot = lax.broadcasted_iota(jnp.int32, nb_ref.shape, 0)
    column = lax.broadcasted_iota(jnp.int32, nb_ref.shape, 1)
    live = slot < cnt_ref[...]
    eye = lax.broadcasted_iota(jnp.int32, (nblk, nblk), 0) == lax.broadcasted_iota(
        jnp.int32, (nblk, nblk), 1
    )
    for j in range(WIN):
        hits = jnp.where(live & (nb_ref[...] == column + j), 1.0, 0.0)
        times = jnp.sum(hits, axis=0, keepdims=True)
        times = jnp.sum(jnp.where(eye, times, 0.0), axis=1, keepdims=True)
        times = jnp.broadcast_to(times, (nblk, 128))
        multr[j] = times
        biasr[j] = jnp.where(times > 0.0, 0.0, -jnp.inf)

    def project(pieces):
        spans = [
            (aligned(block * nrow + part * quarter, quarter), parts * quarter)
            for block, part, parts in pieces
        ]
        rows = jnp.concatenate([G[pl.ds(s, size), :] for s, size in spans], axis=0)
        made = jnp.dot(rows, wqkv[...], preferred_element_type=F32)
        at = 0
        for s, size in spans:
            part = slice(at, at + size)
            at += size
            first = lax.broadcasted_iota(jnp.int32, (size, 128), 1) < HD
            q = made[part, 0:128]
            key = made[part, 128:256].astype(BF)
            v = made[part, 256:384]
            v0 = jnp.where(first, v, 1.0).astype(BF)
            v1 = jnp.where(first, 1.0, v).astype(BF)
            Q[0, pl.ds(s, size), :] = jnp.where(first, q, 0.0).astype(BF)
            Q[1, pl.ds(s, size), :] = jnp.where(first, 0.0, q).astype(BF)
            wide = pl.ds(aligned(s + RIM, quarter), size)
            KV[0, wide, :] = key
            KV[1, wide, :] = v0
            KV[2, wide, :] = v1
            kst[part, :] = key
            vst[0, part, :] = v0
            vst[1, part, :] = v1
        return at

    def cross(keys, t):
        at = pl.ds(t * nlat, nlat)
        s = lax.dot_general(
            qlat[at, :],
            kst[pl.ds(0, keys), :],
            (((1,), (1,)), ((), ())),
            preferred_element_type=F32,
        )
        before = mm[at, :]
        top = jnp.maximum(before, jnp.max(s, axis=1, keepdims=True))
        alpha = jnp.exp2((before - top) * SCALE2)
        p = jnp.concatenate(
            [
                jnp.exp2((s[:, j * 128 : (j + 1) * 128] - top) * SCALE2).astype(BF)
                for j in range(keys // 128)
            ],
            axis=1,
        )
        mm[at, :] = top
        om[at, :] = om[at, :] * alpha + jnp.dot(
            p, vst[t, pl.ds(0, keys), :], preferred_element_type=F32
        )

    def stage(pieces):
        keys = project(pieces)
        for t in range(2):
            cross(keys, t)

    def start(copies):
        for copy in copies:
            copy.start()
        pending.extend([copy.wait_send for copy in copies])

    move(left, 0, 1, 1, right).wait_recv()
    move(right, 3, 1, 8, left).wait_recv()
    start([move(left, 0, 1, 9, right), move(right, 3, 1, 12, left)])
    for i in (3, 4, 5):
        loads[i].wait()
    move(sib, 0, 4, 0, sib).wait_recv()
    stage([(h, 0, 4), (sib, 0, 4)])

    @pl.when(h == 0)
    def _():
        pl.semaphore_wait(barrier, nc - 1)
        for d in range(1, nh):
            signal(go_sem, heads=d)


    move(left, 1, 1, 2, right).wait_recv()
    move(right, 2, 1, 7, left).wait_recv()
    start([move(left, 1, 1, 10, right), move(right, 2, 1, 11, left)])
    start([move(left, 0, 2, 13, sib), move(right, 2, 2, 14, sib)])
    move(left_s, 0, 2, 13, sib).wait_recv()
    move(right_s, 2, 2, 14, sib).wait_recv()
    stage([(left, 0, 2), (right, 2, 2), (left_s, 0, 2), (right_s, 2, 2)])

    @pl.when(h != 0)
    def _():
        pl.semaphore_wait(go_sem, 1)

    loads[7].wait()
    loads[8].wait()

    def share_weight(ref, sem, **to):
        pltpu.make_async_remote_copy(
            src_ref=ref,
            dst_ref=ref,
            send_sem=xs.at[sem],
            recv_sem=xr.at[sem],
            device_id=to,
            device_id_type=MESH,
        ).start()

    @pl.when(k == 0)
    def _():
        for dy in y_steps:
            share_weight(wup.at[:, own_y], 9, ctx=zs[0] + ys[dy])

    @pl.when(k == 1)
    def _():
        for dy in y_steps:
            share_weight(wdn.at[own_y, :], 9, ctx=zs[0] + ys[dy])

    for i in (2, 3):
        move(left, i, 1, 1 + i, right).wait_recv()
        move(right, 3 - i, 1, 8 - i, left).wait_recv()
    start([move(left, 2, 2, 15, sib), move(right, 0, 2, 16, sib)])

    move(left_s, 2, 2, 15, sib).wait_recv()
    move(right_s, 0, 2, 16, sib).wait_recv()
    stage([(left, 2, 2), (right, 0, 2), (left_s, 2, 2), (right_s, 0, 2)])

    move(far, 0, 1, 9, right).wait_recv()
    move(far, 3, 1, 12, left).wait_recv()
    start([move(far, 0, 1, 17, sib), move(far, 3, 1, 18, sib)])
    move(far_s, 0, 1, 17, sib).wait_recv()
    move(far_s, 3, 1, 18, sib).wait_recv()
    stage([(far, 0, 1), (far, 3, 1), (far_s, 0, 1), (far_s, 3, 1)])

    move(far, 1, 1, 10, right).wait_recv()
    move(far, 2, 1, 11, left).wait_recv()
    start([move(far, 1, 2, 19, sib)])
    move(far_s, 1, 2, 19, sib).wait_recv()
    stage([(far, 1, 2), (far_s, 1, 2)])

    tile1 = 128
    lane1 = lax.broadcasted_iota(jnp.int32, (tile1, 128), 1)
    row1 = lax.broadcasted_iota(jnp.int32, (tile1, 128), 0)
    first1 = lane1 < HD
    pick1 = lax.rem(lane1, HD) == lax.rem(row1, per)
    for t in range(nlat // tile1):
        at0 = pl.ds(t * tile1, tile1)
        at1 = pl.ds(nlat + t * tile1, tile1)
        o0, o1 = om[at0, :], om[at1, :]
        total = pltpu.roll(jnp.where(first1, o1, o0), HD, 1)
        r1s[at0, :] = (jnp.where(first1, o0, o1) / total).astype(BF)
        lse = jnp.where(first1, mm[at0, :], mm[at1, :]) * SCALE2 + jnp.log2(total)
        lse = jnp.where(pick1, lse, 0.0)
        for g in range(tile1 // per):
            r1t[t * (tile1 // per) + g] = jnp.sum(
                lse[g * per : (g + 1) * per, :], axis=0, keepdims=True
            )

    own_c = pl.ds(aligned(c * per, 16), per)
    def to_ctx(src, dst, s, r, peers=others):
        for to in peers:
            pltpu.make_async_remote_copy(
                src_ref=src(to),
                dst_ref=dst,
                send_sem=xs.at[s],
                recv_sem=xr.at[r],
                device_id={"ctx": to},
                device_id_type=MESH,
            ).start()

    def spread(i, src, dst):
        to_ctx(lambda to: src.at[pl.ds(aligned(to * per, 16), per), :], dst.at[own_c, :], i, i)

    def await_bytes(ref, sem):
        pltpu.make_async_copy(ref, ref, sem).wait()

    rest = pl.ds(0, (nc - 1) * per)
    to_ctx(lambda to: r1t.at[to], r1u.at[c], 1, 1)
    spread(0, r1s, r1r)
    r1r[own_c, :] = r1s[own_c, :]
    r1u[c] = r1t[c]

    def rim(src, dst, sem, to):
        return pltpu.make_async_remote_copy(
            src_ref=KV.at[:, pl.ds(src, RIM), :],
            dst_ref=KV.at[:, pl.ds(dst, RIM), :],
            send_sem=xs.at[sem],
            recv_sem=xr.at[sem],
            device_id={"ctx": to},
            device_id_type=MESH,
        )

    rims = [
        rim(RIM, RIM + gtok, 2, lax.rem(c + nc - 1, nc)),
        rim(gtok, 0, 3, lax.rem(c + 1, nc)),
    ]
    for r in rims:
        r.start()
    pending += [r.wait_send for r in rims]
    pending += [lambda: await_bytes(r1r.at[rest, :], xs.at[0])]
    pending += [lambda: await_bytes(r1u.at[pl.ds(0, nc - 1)], xs.at[1])]

    firstb = lax.broadcasted_iota(jnp.int32, (BLK, 128), 1) < HD

    def attend(b):
        at = pl.ds(aligned(b * BLK, BLK), BLK)
        win = pl.ds(aligned(b * BLK, BLK), WIN * BLK)
        q = jnp.concatenate([Q[0, at, :], Q[1, at, :]], axis=0)
        s = lax.dot_general(
            q, KV[0, win, :], (((1,), (1,)), ((), ())), preferred_element_type=F32
        )
        parts = [
            s[:, j * BLK : (j + 1) * BLK] + biasr[j, pl.ds(b, 1), :] for j in range(WIN)
        ]
        top = parts[0]
        for part in parts[1:]:
            top = jnp.maximum(top, part)
        top = jnp.max(top, axis=1, keepdims=True)
        p = jnp.concatenate(
            [
                (jnp.exp2((part - top) * SCALE2) * multr[j, pl.ds(b, 1), :]).astype(BF)
                for j, part in enumerate(parts)
            ],
            axis=1,
        )
        o0 = jnp.dot(p[:BLK], KV[1, win, :], preferred_element_type=F32)
        o1 = jnp.dot(p[BLK:], KV[2, win, :], preferred_element_type=F32)
        total = pltpu.roll(jnp.where(firstb, o1, o0), HD, 1)
        A[at, :] = (jnp.where(firstb, o0, o1) / total).astype(BF)

    def attend_four(i, carry):
        for j in range(4):
            attend(2 + 4 * i + j)
        return carry

    lax.fori_loop(0, 2, attend_four, 0)

    await_bytes(r1r.at[rest, :], xr.at[0])
    await_bytes(r1u.at[pl.ds(0, nc - 1)], xr.at[1])
    lanes = lax.broadcasted_iota(jnp.int32, (per, 128), 1)
    pick = lax.rem(lanes, HD) == lax.broadcasted_iota(jnp.int32, (per, 128), 0)
    for i in range(nc):
        fA[pl.ds(i * per, per), :] = jnp.where(pick, r1u[i], 0.0)
    same = (
        lax.broadcasted_iota(jnp.int32, (128, 128), 0) // HD
        == lax.broadcasted_iota(jnp.int32, (128, 128), 1) // HD
    )
    fB[...] = jnp.dot(
        fA[...],
        jnp.where(same, 1.0, 0.0),
        preferred_element_type=F32,
        precision=lax.Precision.HIGHEST,
    )
    peak = fB[pl.ds(0, per), :]
    for i in range(1, nc):
        peak = jnp.maximum(peak, fB[pl.ds(i * per, per), :])
    weight = jnp.zeros((per, 128), F32)
    value = jnp.zeros((per, 128), F32)
    for i in range(nc):
        w = jnp.exp2(fB[pl.ds(i * per, per), :] - peak)
        weight += w
        value += w * r1r[pl.ds(i * per, per), :].astype(F32)
    lat_att = (value / weight).astype(BF)

    loads[6].wait()
    made = jnp.dot(lat_att, wlo[...], preferred_element_type=F32)
    for j in range(nk):
        r2s[pl.ds(j, per, stride=nk), :] = made[:, j * 128 : (j + 1) * 128]
    rest2 = pl.ds(0, (nh - 1) * two * nk)
    own_h = pl.ds(aligned(h * two * nk, 16), two * nk)

    def send2(d, carry):
        to = lax.rem(h + d, nh)
        pltpu.make_async_remote_copy(
            src_ref=r2s.at[pl.ds(aligned(to * two * nk, 16), two * nk), :],
            dst_ref=r2r.at[own_h, :],
            send_sem=xs.at[4],
            recv_sem=xr.at[4],
            device_id={"heads": to},
            device_id_type=MESH,
        ).start()
        return carry

    lax.fori_loop(1, nh, send2, 0)
    r2r[own_h, :] = r2s[own_h, :]
    pending += [lambda: await_bytes(r2r.at[rest2, :], xs.at[4])]

    foreign = (ny - 1) * 128

    @pl.when(k == 0)
    def _():
        await_bytes(wup.at[:, pl.ds(0, foreign)], xr.at[9])
        for dy in y_steps:
            share_weight(wup.at[:, pl.ds(aligned(ys[dy] * 128, 128), 128)], 10, heads=sib)

    @pl.when(k == 1)
    def _():
        await_bytes(wdn.at[pl.ds(0, foreign), :], xr.at[9])
        for dy in y_steps:
            share_weight(wdn.at[pl.ds(aligned(ys[dy] * 128, 128), 128), :], 10, heads=sib)

    pending += [lambda: await_bytes(wup.at[:, pl.ds(0, foreign)], xs.at[9])]
    pending += [lambda: await_bytes(wup.at[:, pl.ds(0, foreign)], xs.at[10])]

    lax.fori_loop(2, (nblk - 4) // 4, attend_four, 0)

    await_bytes(r2r.at[rest2, :], xr.at[4])
    hidden = hl[...]
    for i in range(nh):
        hidden += r2r[pl.ds(i * two * nk, two * nk), :]
    hl[...] = hidden
    for i in range(two):
        row = hidden[i * nk : (i + 1) * nk, :]
        center = jnp.sum(jnp.sum(row, axis=0, keepdims=True), axis=1, keepdims=True) / dw
        off = row - center
        spread2 = (
            jnp.sum(jnp.sum(jnp.square(off), axis=0, keepdims=True), axis=1, keepdims=True) / dw
        )
        f2[pl.ds(i * nk, nk), :] = off * lax.rsqrt(spread2 + EPSILON) * mg_ref[...]
    r3s[...] = f2[...].astype(BF)
    own_z = pl.ds(aligned(z * per, 16), per)
    restz = pl.ds(0, (nz - 1) * per)
    to_ctx(lambda to: r3s, r3r.at[own_z, :], 5, 5, z_peers)
    r3r[own_z, :] = r3s[...]
    pending += [lambda: await_bytes(r3r.at[restz, :], xs.at[5])]

    for r in rims:
        r.wait_recv()
    for b in (0, 1, nblk - 2, nblk - 1):
        attend(b)

    head_cols = pl.ds(aligned(h * 128, 128), 128)

    def send_back(d, carry):
        to = lax.rem(h + d, nh)
        pltpu.make_async_remote_copy(
            src_ref=A.at[pl.ds(aligned(to * nrow, 128), nrow), :],
            dst_ref=R.at[:, head_cols],
            send_sem=xs.at[6],
            recv_sem=xr.at[6],
            device_id={"heads": to},
            device_id_type=MESH,
        ).start()
        return carry

    lax.fori_loop(1, nh, send_back, 0)
    R[:, head_cols] = A[pl.ds(mine, nrow), :]
    pending += [lambda: await_bytes(A.at[pl.ds(0, (nh - 1) * nrow), :], xs.at[6])]

    await_bytes(r3r.at[restz, :], xr.at[5])
    await_bytes(wup.at[:, pl.ds(0, foreign)], xr.at[10])
    group = nz * two
    fA[pl.ds(0, nz * per), :] = r3r[...].astype(F32)
    rows = jnp.concatenate(
        [fA[pl.ds(j, group, stride=nk), :].astype(BF) for j in range(nk)], axis=1
    )
    inner = jax.nn.gelu(
        jnp.dot(rows, wup[...], preferred_element_type=F32), approximate=True
    ).astype(BF)
    made = jnp.dot(inner, wdn[...], preferred_element_type=F32)
    for j in range(nk):
        r4s[pl.ds(j, group, stride=nk), :] = made[:, j * 128 : (j + 1) * 128]
    to_ctx(
        lambda to: r4s.at[pl.ds(aligned(to // ny * per, 16), per), :],
        r4r.at[own_z, :],
        7,
        7,
        z_peers,
    )
    r4r[own_z, :] = r4s[own_z, :]
    pending += [lambda: await_bytes(r4r.at[restz, :], xs.at[7])]

    await_bytes(r4r.at[restz, :], xr.at[7])
    total = hl[...]
    for i in range(nz):
        total += r4r[pl.ds(i * per, per), :]
    r5s[...] = total.astype(BF)
    to_ctx(lambda to: r5s, r5r.at[own_c, :], 8, 8)
    own5 = pltpu.make_async_copy(r5s, r5r.at[own_c, :], in_sem.at[16])
    own5.start()
    pending += [own5.wait]
    pending += [lambda: await_bytes(r5r.at[rest, :], xs.at[8])]
    loads[9].wait()
    await_bytes(A.at[pl.ds(0, (nh - 1) * nrow), :], xr.at[6])

    def project_out(n, carry):
        cols = pl.ds(aligned(n * 256, 256), 256)
        tout_ref[:, cols] = (
            tok[:, cols].astype(F32)
            + jnp.dot(R[...], wout[:, cols], preferred_element_type=F32)
        ).astype(BF)
        return carry

    lax.fori_loop(0, dw // 256, project_out, 0)
    leave = pltpu.make_async_copy(tout_ref, tout_hbm, in_sem.at[15])
    leave.start()
    pending += [leave.wait]

    await_bytes(r5r.at[rest, :], xr.at[8])

    for done in pending:
        done()


def hand_over(a_ref, b_ref, a_out, b_out, a, b, f, r, came, left):
    rows = a.shape[0] // 4
    parts = [pl.ds(i * rows, rows) for i in range(4)]
    latents = pltpu.make_async_copy(b_ref, b, came.at[4])
    loads = [pltpu.make_async_copy(a_ref.at[p, :], a.at[p, :], came.at[i]) for i, p in enumerate(parts)]
    stores = [pltpu.make_async_copy(a.at[p, :], a_out.at[p, :], left.at[i]) for i, p in enumerate(parts)]
    stores += [pltpu.make_async_copy(r, b_out, left.at[4])]
    latents.start()
    for copy in loads:
        copy.start()
    latents.wait()
    f[...] = b[...].astype(F32)
    share, dw = r.shape
    nk = dw // 128
    for j in range(nk):
        r[:, j * 128 : (j + 1) * 128] = f[pl.ds(j, share, stride=nk), :].astype(BF)
    stores[4].start()
    for load, store in zip(loads, stores):
        load.wait()
        store.start()
    for copy in stores:
        copy.wait()


def per_device(
    nh,
    nc,
    tokens,
    ln_gain,
    w_qkv,
    w_out,
    neighbours,
    counts,
    latents,
    lat_gain,
    w_lat_q,
    w_lat_o,
    mlp_gain,
    w_up,
    w_down,
):
    nrow, dw = tokens.shape[1:]
    nlat = latents.shape[0]
    gtok = nrow * nh
    per = nlat // nc
    share = nlat // nh
    nblk = gtok // BLK
    two = share // nc * (dw // 128)
    hbm = pl.BlockSpec(memory_space=pltpu.HBM)
    vmem = pl.BlockSpec(memory_space=pltpu.VMEM)
    stage = gtok // 4
    scratch = [
        pltpu.VMEM((nrow, dw), BF),
        pltpu.VMEM((1, dw), F32),
        pltpu.VMEM((neighbours.shape[2], nblk), jnp.int32),
        pltpu.VMEM((1, nblk), jnp.int32),
        pltpu.VMEM((1, dw), F32),
        pltpu.VMEM((dw // 128, 128), F32),
        pltpu.VMEM((nrow, dw), BF),
        pltpu.VMEM((dw, 384), BF),
        pltpu.VMEM((dw, dw), BF),
        pltpu.VMEM((nlat, dw), BF),
        pltpu.VMEM((dw, 128), BF),
        pltpu.VMEM((128, dw), BF),
        pltpu.VMEM((dw, 4 * w_up.shape[1]), BF),
        pltpu.VMEM((4 * w_down.shape[0], dw), BF),
        pltpu.VMEM((gtok, dw), BF),
        pltpu.VMEM((nlat, dw), BF),
        pltpu.VMEM((2, gtok, 128), BF),
        pltpu.VMEM((3, gtok + 2 * RIM, 128), BF),
        pltpu.VMEM((stage, 128), BF),
        pltpu.VMEM((2, stage, 128), BF),
        pltpu.VMEM((nlat, 128), F32),
        pltpu.VMEM((nlat, 128), F32),
        pltpu.VMEM((two, 128), F32),
        pltpu.VMEM((2 * nlat, 128), BF),
        pltpu.VMEM((2 * nlat, 128), F32),
        pltpu.VMEM((2 * nlat, 128), F32),
        pltpu.VMEM((two, 128), F32),
        pltpu.VMEM((WIN, nblk, 128), F32),
        pltpu.VMEM((WIN, nblk, 128), F32),
        pltpu.VMEM((nlat, 128), BF),
        pltpu.VMEM((nc, 1, 128), F32),
        pltpu.VMEM((nlat, 128), BF),
        pltpu.VMEM((nc, 1, 128), F32),
        pltpu.VMEM((nh * two, 128), F32),
        pltpu.VMEM((nh * two, 128), F32),
        pltpu.VMEM((two, 128), BF),
        pltpu.VMEM((nlat // 4, 128), BF),
        pltpu.VMEM((nlat // 4, 128), F32),
        pltpu.VMEM((nlat // 4, 128), F32),
        pltpu.VMEM((two, 128), BF),
        pltpu.VMEM((gtok, 128), BF),
        pltpu.VMEM((nrow, dw), BF),
        pltpu.SemaphoreType.DMA((17,)),
        pltpu.SemaphoreType.DMA((20,)),
        pltpu.SemaphoreType.DMA((20,)),
        pltpu.SemaphoreType.DMA((11,)),
        pltpu.SemaphoreType.DMA((11,)),
        pltpu.SemaphoreType.REGULAR,
        pltpu.SemaphoreType.REGULAR,
    ]
    tokens_out, rows_out = pl.pallas_call(
        functools.partial(kernel, nh, nc),
        out_shape=(
            jax.ShapeDtypeStruct((nrow, dw), BF),
            jax.ShapeDtypeStruct((nlat, 128), BF),
        ),
        in_specs=[hbm] * 13,
        out_specs=(hbm, hbm),
        scratch_shapes=scratch,
        compiler_params=pltpu.CompilerParams(
            collective_id=0, has_side_effects=True, vmem_limit_bytes=60 * 1024 * 1024
        ),
        name="encoder_block",
    )(
        tokens[0],
        ln_gain.reshape(1, dw),
        jnp.transpose(w_qkv, (1, 0, 2)),
        w_out,
        neighbours[0].T,
        counts,
        latents,
        lat_gain.reshape(1, dw),
        w_lat_q,
        w_lat_o,
        mlp_gain.reshape(dw // 128, 128),
        w_up,
        w_down,
    )
    tokens_out, latents_out = pl.pallas_call(
        hand_over,
        out_shape=(
            jax.ShapeDtypeStruct((nrow, dw), BF),
            jax.ShapeDtypeStruct((share, dw), BF),
        ),
        in_specs=[hbm, hbm],
        out_specs=(hbm, hbm),
        scratch_shapes=[
            pltpu.VMEM((nrow, dw), BF),
            pltpu.VMEM((nlat, 128), BF),
            pltpu.VMEM((nlat, 128), F32),
            pltpu.VMEM((share, dw), BF),
            pltpu.SemaphoreType.DMA((5,)),
            pltpu.SemaphoreType.DMA((5,)),
        ],
        compiler_params=pltpu.CompilerParams(vmem_limit_bytes=60 * 1024 * 1024),
        name="hand_over",
    )(tokens_out, rows_out)
    return (tokens_out[None], latents_out)


def solution(mesh):
    in_specs = (
        P("ctx", "heads", None),
        P(),
        P(None, None, "heads"),
        P(),
        P("ctx", None, None),
        P("ctx", None),
        P(),
        P(),
        P(None, "heads"),
        P("heads", None),
        P(),
        P(None, "ctx"),
        P("ctx", None),
    )
    out_specs = (P("ctx", "heads", None), P("heads", None))
    return jax.shard_map(
        functools.partial(per_device, mesh.shape["heads"], mesh.shape["ctx"]),
        mesh=mesh,
        in_specs=in_specs,
        out_specs=out_specs,
        check_vma=False,
    )
```

```python
import functools

import jax
import jax.numpy as jnp
from jax import lax
from jax.experimental import pallas as pl
from jax.experimental.pallas import tpu as pltpu
from jax.sharding import PartitionSpec as P

HD = 64
BLK = 128
WIN = 5
RIM = 256
EPSILON = 1e-05
SCALE2 = HD ** (-0.5) * 1.4426950408889634
MESH = pl.DeviceIdType.MESH
BF = jnp.bfloat16
F32 = jnp.float32


def aligned(start, by):
    return pl.multiple_of(start, by)


def normalise(rows, gain):
    center = jnp.mean(rows, axis=-1, keepdims=True)
    spread = jnp.mean(jnp.square(rows - center), axis=-1, keepdims=True)
    return (rows - center) * lax.rsqrt(spread + EPSILON) * gain


def kernel(
    nh,
    nc,
    tok_hbm,
    lng_hbm,
    wqkv_hbm,
    wout_hbm,
    nb_hbm,
    cnt_hbm,
    lat_hbm,
    latg_hbm,
    wlq_hbm,
    wlo_hbm,
    mg_hbm,
    wup_hbm,
    wdn_hbm,
    tout_hbm,
    r5r,
    tout_ref,
    lng_ref,
    nb_ref,
    cnt_ref,
    latg_ref,
    mg_ref,
    tok,
    wqkv,
    wout,
    lat,
    wlq,
    wlo,
    wup,
    wdn,
    G,
    latn,
    Q,
    KV,
    kst,
    vst,
    fA,
    fB,
    f2,
    qlat,
    om,
    mm,
    hl,
    multr,
    biasr,
    r1s,
    r1t,
    r1r,
    r1u,
    r2s,
    r2r,
    r3s,
    r3r,
    r4s,
    r4r,
    r5s,
    A,
    R,
    in_sem,
    gs,
    gr,
    xs,
    xr,
    row_sem,
    go_sem,
):
    h = lax.axis_index("heads")
    c = lax.axis_index("ctx")
    x = h // 2
    k = h % 2
    nrow = tok.shape[0]
    nlat = lat.shape[0]
    dw = tok.shape[1]
    nk = dw // 128
    gtok = nh * nrow
    nblk = gtok // BLK
    per = nlat // nc

    ny = 4
    nz = nc // ny
    z = c // ny
    y = lax.rem(c, ny)
    way = 1 - 2 * k
    zs = [lax.rem(z + nz + way * d, nz) * ny for d in range(nz)]
    ys = [lax.rem(y + ny + way * d, ny) for d in range(ny)]
    own_y = pl.ds(aligned(y * 128, 128), 128)

    loads = [
        pltpu.make_async_copy(tok_hbm, tok, in_sem.at[0]),
        pltpu.make_async_copy(lat_hbm, lat, in_sem.at[1]),
        pltpu.make_async_copy(wlq_hbm, wlq, in_sem.at[2]),
        pltpu.make_async_copy(wqkv_hbm.at[0], wqkv.at[:, pl.ds(0, 128)], in_sem.at[3]),
        pltpu.make_async_copy(wqkv_hbm.at[1], wqkv.at[:, pl.ds(128, 128)], in_sem.at[4]),
        pltpu.make_async_copy(wqkv_hbm.at[2], wqkv.at[:, pl.ds(256, 128)], in_sem.at[5]),
        pltpu.make_async_copy(wlo_hbm, wlo, in_sem.at[6]),
        pltpu.make_async_copy(wup_hbm, wup.at[:, own_y], in_sem.at[7]),
        pltpu.make_async_copy(wdn_hbm, wdn.at[own_y, :], in_sem.at[8]),
        pltpu.make_async_copy(wout_hbm, wout, in_sem.at[9]),
    ]
    small = [
        pltpu.make_async_copy(lng_hbm, lng_ref, in_sem.at[10]),
        pltpu.make_async_copy(latg_hbm, latg_ref, in_sem.at[11]),
        pltpu.make_async_copy(nb_hbm, nb_ref, in_sem.at[12]),
        pltpu.make_async_copy(cnt_hbm, cnt_ref, in_sem.at[13]),
        pltpu.make_async_copy(mg_hbm, mg_ref, in_sem.at[14]),
    ]
    small[0].start()
    for load in loads[:3] + small[1:] + loads[3:]:
        load.start()

    barrier = pltpu.get_barrier_semaphore()

    def signal(sem, **to):
        pl.semaphore_signal(sem, inc=1, device_id=to, device_id_type=MESH)

    for d in range(1, nh):
        @pl.when(h != d)
        def _(d=d):
            signal(barrier, heads=d)

    loads[0].wait()
    small[0].wait()
    mine = aligned(h * nrow, 256)
    step = 32

    def norm_tokens(i, carry):
        at = pl.ds(aligned(i * step, step), step)
        G[pl.ds(aligned(mine + i * step, step), step), :] = normalise(
            tok[at, :].astype(F32), lng_ref[...]
        ).astype(BF)
        return carry

    lax.fori_loop(0, nrow // step, norm_tokens, 0)

    @pl.when(h != 0)
    def _():
        pl.semaphore_wait(barrier, nh - 1)

    @pl.when(h == 1)
    def _():
        signal(row_sem, heads=0)

    @pl.when(h == 0)
    def _():
        pl.semaphore_wait(row_sem, 1)


    sib = x * 2 + (1 - k)
    right = lax.rem(x + 1, nh // 2) * 2 + k
    left = lax.rem(x + nh // 2 - 1, nh // 2) * 2 + k
    far = lax.rem(x + 2, nh // 2) * 2 + k
    right_s = lax.rem(x + 1, nh // 2) * 2 + (1 - k)
    left_s = lax.rem(x + nh // 2 - 1, nh // 2) * 2 + (1 - k)
    far_s = lax.rem(x + 2, nh // 2) * 2 + (1 - k)

    quarter = nrow // 4

    def move(block, part, parts, sem, to):
        rows = pl.ds(aligned(block * nrow + part * quarter, quarter), parts * quarter)
        return pltpu.make_async_remote_copy(
            src_ref=G.at[rows, :],
            dst_ref=G.at[rows, :],
            send_sem=gs.at[sem],
            recv_sem=gr.at[sem],
            device_id={"heads": to},
            device_id_type=MESH,
        )

    pending = []
    sends = []
    for i in range(4):
        sends += [move(h, i, 1, 1 + i, right), move(h, 3 - i, 1, 8 - i, left)]
        if i == 1:
            sends += [move(h, 0, 4, 0, sib)]
    for send in sends:
        send.start()
    pending += [send.wait_send for send in sends]

    steps = sorted(
        ((dz, dy) for dz in range(nz) for dy in range(ny) if dz or dy),
        key=lambda d: -(min(d[0], nz - d[0]) + min(d[1], ny - d[1])),
    )
    others = [zs[dz] + ys[dy] for dz, dy in steps]
    z_peers = [zs[dz] + y for dz, dy in steps if dy == 0]
    y_steps = [dy for dz, dy in steps if dz == 0]

    @pl.when(h == 0)
    def _():
        for to in others:
            signal(barrier, ctx=to)


    loads[1].wait()
    for load in small[1:]:
        load.wait()

    def norm_latents(i, carry):
        at = pl.ds(aligned(i * step, step), step)
        latn[at, :] = normalise(lat[at, :].astype(F32), latg_ref[...]).astype(BF)
        return carry

    lax.fori_loop(0, nlat // step, norm_latents, 0)
    loads[2].wait()
    fA[...] = jnp.dot(latn[...], wlq[...], preferred_element_type=F32)
    share = nlat // nh
    two = share // nc
    for hh in range(nh):
        for i in range(two):
            fB[pl.ds(hh * two + i, nc, stride=per), :] = fA[
                pl.ds(hh * share + i, nc, stride=two), :
            ]
    lane = lax.broadcasted_iota(jnp.int32, (nlat, 128), 1)
    lq = fB[...]
    qlat[pl.ds(0, nlat), :] = jnp.where(lane < HD, lq, 0.0).astype(BF)
    qlat[pl.ds(nlat, nlat), :] = jnp.where(lane < HD, 0.0, lq).astype(BF)
    om[...] = jnp.zeros_like(om)
    mm[...] = jnp.full_like(mm, -jnp.inf)

    own64 = lat[pl.ds(aligned(h * share, share), share), :].astype(F32)
    for j in range(nk):
        fA[pl.ds(j, share, stride=nk), :] = own64[:, j * 128 : (j + 1) * 128]
    hl[...] = fA[pl.ds(aligned(c * two * nk, two * nk), two * nk), :]

    slot = lax.broadcasted_iota(jnp.int32, nb_ref.shape, 0)
    column = lax.broadcasted_iota(jnp.int32, nb_ref.shape, 1)
    live = slot < cnt_ref[...]
    eye = lax.broadcasted_iota(jnp.int32, (nblk, nblk), 0) == lax.broadcasted_iota(
        jnp.int32, (nblk, nblk), 1
    )
    for j in range(WIN):
        hits = jnp.where(live & (nb_ref[...] == column + j), 1.0, 0.0)
        times = jnp.sum(hits, axis=0, keepdims=True)
        times = jnp.sum(jnp.where(eye, times, 0.0), axis=1, keepdims=True)
        times = jnp.broadcast_to(times, (nblk, 128))
        multr[j] = times
        biasr[j] = jnp.where(times > 0.0, 0.0, -jnp.inf)

    def project(pieces, base=0):
        spans = [
            (aligned(block * nrow + part * quarter, quarter), parts * quarter)
            for block, part, parts in pieces
        ]
        rows = jnp.concatenate([G[pl.ds(s, size), :] for s, size in spans], axis=0)
        made = jnp.dot(rows, wqkv[...], preferred_element_type=F32)
        at = 0
        for s, size in spans:
            part = slice(at, at + size)
            slot = slice(base + at, base + at + size)
            at += size
            first = lax.broadcasted_iota(jnp.int32, (size, 128), 1) < HD
            q = made[part, 0:128]
            key = made[part, 128:256].astype(BF)
            v = made[part, 256:384]
            v0 = jnp.where(first, v, 1.0).astype(BF)
            v1 = jnp.where(first, 1.0, v).astype(BF)
            Q[0, pl.ds(s, size), :] = jnp.where(first, q, 0.0).astype(BF)
            Q[1, pl.ds(s, size), :] = jnp.where(first, 0.0, q).astype(BF)
            wide = pl.ds(aligned(s + RIM, quarter), size)
            KV[0, wide, :] = key
            KV[1, wide, :] = v0
            KV[2, wide, :] = v1
            kst[slot, :] = key
            vst[0, slot, :] = v0
            vst[1, slot, :] = v1
        return base + at

    def cross(keys, t):
        at = pl.ds(t * nlat, nlat)
        s = lax.dot_general(
            qlat[at, :],
            kst[pl.ds(0, keys), :],
            (((1,), (1,)), ((), ())),
            preferred_element_type=F32,
        )
        before = mm[at, :]
        top = jnp.maximum(before, jnp.max(s, axis=1, keepdims=True))
        alpha = jnp.exp2((before - top) * SCALE2)
        p = jnp.concatenate(
            [
                jnp.exp2((s[:, j * 128 : (j + 1) * 128] - top) * SCALE2).astype(BF)
                for j in range(keys // 128)
            ],
            axis=1,
        )
        mm[at, :] = top
        om[at, :] = om[at, :] * alpha + jnp.dot(
            p, vst[t, pl.ds(0, keys), :], preferred_element_type=F32
        )

    def stage(pieces):
        keys = project(pieces)
        for t in range(2):
            cross(keys, t)

    def start(copies):
        for copy in copies:
            copy.start()
        pending.extend([copy.wait_send for copy in copies])

    move(left, 0, 1, 1, right).wait_recv()
    move(right, 3, 1, 8, left).wait_recv()
    start([move(left, 0, 1, 9, right), move(right, 3, 1, 12, left)])
    for i in (3, 4, 5):
        loads[i].wait()
    move(sib, 0, 4, 0, sib).wait_recv()
    stage([(h, 0, 4), (sib, 0, 4)])

    @pl.when(h == 0)
    def _():
        pl.semaphore_wait(barrier, nc - 1)
        for d in range(1, nh):
            signal(go_sem, heads=d)


    move(left, 1, 1, 2, right).wait_recv()
    move(right, 2, 1, 7, left).wait_recv()
    start([move(left, 1, 1, 10, right), move(right, 2, 1, 11, left)])
    start([move(left, 0, 2, 13, sib), move(right, 2, 2, 14, sib)])
    move(left_s, 0, 2, 13, sib).wait_recv()
    move(right_s, 2, 2, 14, sib).wait_recv()
    stage([(left, 0, 2), (right, 2, 2), (left_s, 0, 2), (right_s, 2, 2)])

    @pl.when(h != 0)
    def _():
        pl.semaphore_wait(go_sem, 1)

    loads[7].wait()
    loads[8].wait()

    def share_weight(ref, sem, **to):
        pltpu.make_async_remote_copy(
            src_ref=ref,
            dst_ref=ref,
            send_sem=xs.at[sem],
            recv_sem=xr.at[sem],
            device_id=to,
            device_id_type=MESH,
        ).start()

    @pl.when(k == 0)
    def _():
        for dy in y_steps:
            share_weight(wup.at[:, own_y], 9, ctx=zs[0] + ys[dy])

    @pl.when(k == 1)
    def _():
        for dy in y_steps:
            share_weight(wdn.at[own_y, :], 9, ctx=zs[0] + ys[dy])

    for i in (2, 3):
        move(left, i, 1, 1 + i, right).wait_recv()
        move(right, 3 - i, 1, 8 - i, left).wait_recv()
    start([move(left, 2, 2, 15, sib), move(right, 0, 2, 16, sib)])

    move(left_s, 2, 2, 15, sib).wait_recv()
    move(right_s, 0, 2, 16, sib).wait_recv()
    stage([(left, 2, 2), (right, 0, 2), (left_s, 2, 2), (right_s, 0, 2)])

    move(far, 0, 1, 9, right).wait_recv()
    move(far, 3, 1, 12, left).wait_recv()
    start([move(far, 0, 1, 17, sib), move(far, 3, 1, 18, sib)])
    move(far_s, 0, 1, 17, sib).wait_recv()
    move(far_s, 3, 1, 18, sib).wait_recv()
    stage([(far, 0, 1), (far, 3, 1), (far_s, 0, 1), (far_s, 3, 1)])

    move(far, 1, 1, 10, right).wait_recv()
    move(far, 2, 1, 11, left).wait_recv()
    start([move(far, 1, 2, 19, sib)])
    keys = project([(far, 1, 2)])
    move(far_s, 1, 2, 19, sib).wait_recv()
    keys = project([(far_s, 1, 2)], keys)
    for t in range(2):
        cross(keys, t)

    tile1 = 128
    lane1 = lax.broadcasted_iota(jnp.int32, (tile1, 128), 1)
    row1 = lax.broadcasted_iota(jnp.int32, (tile1, 128), 0)
    first1 = lane1 < HD
    pick1 = lax.rem(lane1, HD) == lax.rem(row1, per)
    for t in range(nlat // tile1):
        at0 = pl.ds(t * tile1, tile1)
        at1 = pl.ds(nlat + t * tile1, tile1)
        o0, o1 = om[at0, :], om[at1, :]
        total = pltpu.roll(jnp.where(first1, o1, o0), HD, 1)
        r1s[at0, :] = (jnp.where(first1, o0, o1) / total).astype(BF)
        lse = jnp.where(first1, mm[at0, :], mm[at1, :]) * SCALE2 + jnp.log2(total)
        lse = jnp.where(pick1, lse, 0.0)
        for g in range(tile1 // per):
            r1t[t * (tile1 // per) + g] = jnp.sum(
                lse[g * per : (g + 1) * per, :], axis=0, keepdims=True
            )

    own_c = pl.ds(aligned(c * per, 16), per)
    def to_ctx(src, dst, s, r, peers=others):
        for to in peers:
            pltpu.make_async_remote_copy(
                src_ref=src(to),
                dst_ref=dst,
                send_sem=xs.at[s],
                recv_sem=xr.at[r],
                device_id={"ctx": to},
                device_id_type=MESH,
            ).start()

    def spread(i, src, dst):
        to_ctx(lambda to: src.at[pl.ds(aligned(to * per, 16), per), :], dst.at[own_c, :], i, i)

    def await_bytes(ref, sem):
        pltpu.make_async_copy(ref, ref, sem).wait()

    rest = pl.ds(0, (nc - 1) * per)
    to_ctx(lambda to: r1t.at[to], r1u.at[c], 1, 1)
    spread(0, r1s, r1r)
    r1r[own_c, :] = r1s[own_c, :]
    r1u[c] = r1t[c]

    def rim(src, dst, sem, to):
        return pltpu.make_async_remote_copy(
            src_ref=KV.at[:, pl.ds(src, RIM), :],
            dst_ref=KV.at[:, pl.ds(dst, RIM), :],
            send_sem=xs.at[sem],
            recv_sem=xr.at[sem],
            device_id={"ctx": to},
            device_id_type=MESH,
        )

    rims = [
        rim(RIM, RIM + gtok, 2, lax.rem(c + nc - 1, nc)),
        rim(gtok, 0, 3, lax.rem(c + 1, nc)),
    ]
    for r in rims:
        r.start()
    pending += [r.wait_send for r in rims]
    pending += [lambda: await_bytes(r1r.at[rest, :], xs.at[0])]
    pending += [lambda: await_bytes(r1u.at[pl.ds(0, nc - 1)], xs.at[1])]

    firstb = lax.broadcasted_iota(jnp.int32, (BLK, 128), 1) < HD

    def attend(b):
        at = pl.ds(aligned(b * BLK, BLK), BLK)
        win = pl.ds(aligned(b * BLK, BLK), WIN * BLK)
        q = jnp.concatenate([Q[0, at, :], Q[1, at, :]], axis=0)
        s = lax.dot_general(
            q, KV[0, win, :], (((1,), (1,)), ((), ())), preferred_element_type=F32
        )
        parts = [
            s[:, j * BLK : (j + 1) * BLK] + biasr[j, pl.ds(b, 1), :] for j in range(WIN)
        ]
        top = parts[0]
        for part in parts[1:]:
            top = jnp.maximum(top, part)
        top = jnp.max(top, axis=1, keepdims=True)
        p = jnp.concatenate(
            [
                (jnp.exp2((part - top) * SCALE2) * multr[j, pl.ds(b, 1), :]).astype(BF)
                for j, part in enumerate(parts)
            ],
            axis=1,
        )
        o0 = jnp.dot(p[:BLK], KV[1, win, :], preferred_element_type=F32)
        o1 = jnp.dot(p[BLK:], KV[2, win, :], preferred_element_type=F32)
        total = pltpu.roll(jnp.where(firstb, o1, o0), HD, 1)
        A[at, :] = (jnp.where(firstb, o0, o1) / total).astype(BF)

    def attend_four(i, carry):
        for j in range(4):
            attend(2 + 4 * i + j)
        return carry

    lax.fori_loop(0, 2, attend_four, 0)

    await_bytes(r1r.at[rest, :], xr.at[0])
    await_bytes(r1u.at[pl.ds(0, nc - 1)], xr.at[1])
    lanes = lax.broadcasted_iota(jnp.int32, (per, 128), 1)
    pick = lax.rem(lanes, HD) == lax.broadcasted_iota(jnp.int32, (per, 128), 0)
    for i in range(nc):
        fA[pl.ds(i * per, per), :] = jnp.where(pick, r1u[i], 0.0)
    same = (
        lax.broadcasted_iota(jnp.int32, (128, 128), 0) // HD
        == lax.broadcasted_iota(jnp.int32, (128, 128), 1) // HD
    )
    fB[...] = jnp.dot(
        fA[...],
        jnp.where(same, 1.0, 0.0),
        preferred_element_type=F32,
        precision=lax.Precision.HIGHEST,
    )
    peak = fB[pl.ds(0, per), :]
    for i in range(1, nc):
        peak = jnp.maximum(peak, fB[pl.ds(i * per, per), :])
    weight = jnp.zeros((per, 128), F32)
    value = jnp.zeros((per, 128), F32)
    for i in range(nc):
        w = jnp.exp2(fB[pl.ds(i * per, per), :] - peak)
        weight += w
        value += w * r1r[pl.ds(i * per, per), :].astype(F32)
    lat_att = (value / weight).astype(BF)

    loads[6].wait()
    made = jnp.dot(lat_att, wlo[...], preferred_element_type=F32)
    for j in range(nk):
        r2s[pl.ds(j, per, stride=nk), :] = made[:, j * 128 : (j + 1) * 128]
    rest2 = pl.ds(0, (nh - 1) * two * nk)
    own_h = pl.ds(aligned(h * two * nk, 16), two * nk)

    def send2(d, carry):
        to = lax.rem(h + d, nh)
        pltpu.make_async_remote_copy(
            src_ref=r2s.at[pl.ds(aligned(to * two * nk, 16), two * nk), :],
            dst_ref=r2r.at[own_h, :],
            send_sem=xs.at[4],
            recv_sem=xr.at[4],
            device_id={"heads": to},
            device_id_type=MESH,
        ).start()
        return carry

    lax.fori_loop(1, nh, send2, 0)
    r2r[own_h, :] = r2s[own_h, :]
    pending += [lambda: await_bytes(r2r.at[rest2, :], xs.at[4])]

    foreign = (ny - 1) * 128

    @pl.when(k == 0)
    def _():
        await_bytes(wup.at[:, pl.ds(0, foreign)], xr.at[9])
        for dy in y_steps:
            share_weight(wup.at[:, pl.ds(aligned(ys[dy] * 128, 128), 128)], 10, heads=sib)

    @pl.when(k == 1)
    def _():
        await_bytes(wdn.at[pl.ds(0, foreign), :], xr.at[9])
        for dy in y_steps:
            share_weight(wdn.at[pl.ds(aligned(ys[dy] * 128, 128), 128), :], 10, heads=sib)

    pending += [lambda: await_bytes(wup.at[:, pl.ds(0, foreign)], xs.at[9])]
    pending += [lambda: await_bytes(wup.at[:, pl.ds(0, foreign)], xs.at[10])]

    lax.fori_loop(2, (nblk - 4) // 4, attend_four, 0)

    await_bytes(r2r.at[rest2, :], xr.at[4])
    hidden = hl[...]
    for i in range(nh):
        hidden += r2r[pl.ds(i * two * nk, two * nk), :]
    hl[...] = hidden
    for i in range(two):
        row = hidden[i * nk : (i + 1) * nk, :]
        center = jnp.sum(jnp.sum(row, axis=0, keepdims=True), axis=1, keepdims=True) / dw
        off = row - center
        spread2 = (
            jnp.sum(jnp.sum(jnp.square(off), axis=0, keepdims=True), axis=1, keepdims=True) / dw
        )
        f2[pl.ds(i * nk, nk), :] = off * lax.rsqrt(spread2 + EPSILON) * mg_ref[...]
    r3s[...] = f2[...].astype(BF)
    own_z = pl.ds(aligned(z * per, 16), per)
    restz = pl.ds(0, (nz - 1) * per)
    to_ctx(lambda to: r3s, r3r.at[own_z, :], 5, 5, z_peers)
    r3r[own_z, :] = r3s[...]
    pending += [lambda: await_bytes(r3r.at[restz, :], xs.at[5])]

    for r in rims:
        r.wait_recv()
    for b in (0, 1, nblk - 2, nblk - 1):
        attend(b)

    head_cols = pl.ds(aligned(h * 128, 128), 128)

    def send_back(d, carry):
        to = lax.rem(h + d, nh)
        pltpu.make_async_remote_copy(
            src_ref=A.at[pl.ds(aligned(to * nrow, 128), nrow), :],
            dst_ref=R.at[:, head_cols],
            send_sem=xs.at[6],
            recv_sem=xr.at[6],
            device_id={"heads": to},
            device_id_type=MESH,
        ).start()
        return carry

    lax.fori_loop(1, nh, send_back, 0)
    R[:, head_cols] = A[pl.ds(mine, nrow), :]
    pending += [lambda: await_bytes(A.at[pl.ds(0, (nh - 1) * nrow), :], xs.at[6])]

    await_bytes(r3r.at[restz, :], xr.at[5])
    await_bytes(wup.at[:, pl.ds(0, foreign)], xr.at[10])
    group = nz * two
    fA[pl.ds(0, nz * per), :] = r3r[...].astype(F32)
    rows = jnp.concatenate(
        [fA[pl.ds(j, group, stride=nk), :].astype(BF) for j in range(nk)], axis=1
    )
    inner = jax.nn.gelu(
        jnp.dot(rows, wup[...], preferred_element_type=F32), approximate=True
    ).astype(BF)
    made = jnp.dot(inner, wdn[...], preferred_element_type=F32)
    for j in range(nk):
        r4s[pl.ds(j, group, stride=nk), :] = made[:, j * 128 : (j + 1) * 128]
    to_ctx(
        lambda to: r4s.at[pl.ds(aligned(to // ny * per, 16), per), :],
        r4r.at[own_z, :],
        7,
        7,
        z_peers,
    )
    r4r[own_z, :] = r4s[own_z, :]
    pending += [lambda: await_bytes(r4r.at[restz, :], xs.at[7])]

    await_bytes(r4r.at[restz, :], xr.at[7])
    total = hl[...]
    for i in range(nz):
        total += r4r[pl.ds(i * per, per), :]
    r5s[...] = total.astype(BF)
    to_ctx(lambda to: r5s, r5r.at[own_c, :], 8, 8)
    own5 = pltpu.make_async_copy(r5s, r5r.at[own_c, :], in_sem.at[16])
    own5.start()
    pending += [own5.wait]
    pending += [lambda: await_bytes(r5r.at[rest, :], xs.at[8])]
    loads[9].wait()
    await_bytes(A.at[pl.ds(0, (nh - 1) * nrow), :], xr.at[6])

    def project_out(n, carry):
        cols = pl.ds(aligned(n * 256, 256), 256)
        tout_ref[:, cols] = (
            tok[:, cols].astype(F32)
            + jnp.dot(R[...], wout[:, cols], preferred_element_type=F32)
        ).astype(BF)
        return carry

    lax.fori_loop(0, dw // 256, project_out, 0)
    leave = pltpu.make_async_copy(tout_ref, tout_hbm, in_sem.at[15])
    leave.start()
    pending += [leave.wait]

    await_bytes(r5r.at[rest, :], xr.at[8])

    for done in pending:
        done()


def hand_over(a_ref, b_ref, a_out, b_out, a, b, f, r, came, left):
    rows = a.shape[0] // 4
    parts = [pl.ds(i * rows, rows) for i in range(4)]
    latents = pltpu.make_async_copy(b_ref, b, came.at[4])
    loads = [pltpu.make_async_copy(a_ref.at[p, :], a.at[p, :], came.at[i]) for i, p in enumerate(parts)]
    stores = [pltpu.make_async_copy(a.at[p, :], a_out.at[p, :], left.at[i]) for i, p in enumerate(parts)]
    stores += [pltpu.make_async_copy(r, b_out, left.at[4])]
    latents.start()
    for copy in loads:
        copy.start()
    latents.wait()
    f[...] = b[...].astype(F32)
    share, dw = r.shape
    nk = dw // 128
    for j in range(nk):
        r[:, j * 128 : (j + 1) * 128] = f[pl.ds(j, share, stride=nk), :].astype(BF)
    stores[4].start()
    for load, store in zip(loads, stores):
        load.wait()
        store.start()
    for copy in stores:
        copy.wait()


def per_device(
    nh,
    nc,
    tokens,
    ln_gain,
    w_qkv,
    w_out,
    neighbours,
    counts,
    latents,
    lat_gain,
    w_lat_q,
    w_lat_o,
    mlp_gain,
    w_up,
    w_down,
):
    nrow, dw = tokens.shape[1:]
    nlat = latents.shape[0]
    gtok = nrow * nh
    per = nlat // nc
    share = nlat // nh
    nblk = gtok // BLK
    two = share // nc * (dw // 128)
    hbm = pl.BlockSpec(memory_space=pltpu.HBM)
    vmem = pl.BlockSpec(memory_space=pltpu.VMEM)
    stage = gtok // 4
    scratch = [
        pltpu.VMEM((nrow, dw), BF),
        pltpu.VMEM((1, dw), F32),
        pltpu.VMEM((neighbours.shape[2], nblk), jnp.int32),
        pltpu.VMEM((1, nblk), jnp.int32),
        pltpu.VMEM((1, dw), F32),
        pltpu.VMEM((dw // 128, 128), F32),
        pltpu.VMEM((nrow, dw), BF),
        pltpu.VMEM((dw, 384), BF),
        pltpu.VMEM((dw, dw), BF),
        pltpu.VMEM((nlat, dw), BF),
        pltpu.VMEM((dw, 128), BF),
        pltpu.VMEM((128, dw), BF),
        pltpu.VMEM((dw, 4 * w_up.shape[1]), BF),
        pltpu.VMEM((4 * w_down.shape[0], dw), BF),
        pltpu.VMEM((gtok, dw), BF),
        pltpu.VMEM((nlat, dw), BF),
        pltpu.VMEM((2, gtok, 128), BF),
        pltpu.VMEM((3, gtok + 2 * RIM, 128), BF),
        pltpu.VMEM((stage, 128), BF),
        pltpu.VMEM((2, stage, 128), BF),
        pltpu.VMEM((nlat, 128), F32),
        pltpu.VMEM((nlat, 128), F32),
        pltpu.VMEM((two, 128), F32),
        pltpu.VMEM((2 * nlat, 128), BF),
        pltpu.VMEM((2 * nlat, 128), F32),
        pltpu.VMEM((2 * nlat, 128), F32),
        pltpu.VMEM((two, 128), F32),
        pltpu.VMEM((WIN, nblk, 128), F32),
        pltpu.VMEM((WIN, nblk, 128), F32),
        pltpu.VMEM((nlat, 128), BF),
        pltpu.VMEM((nc, 1, 128), F32),
        pltpu.VMEM((nlat, 128), BF),
        pltpu.VMEM((nc, 1, 128), F32),
        pltpu.VMEM((nh * two, 128), F32),
        pltpu.VMEM((nh * two, 128), F32),
        pltpu.VMEM((two, 128), BF),
        pltpu.VMEM((nlat // 4, 128), BF),
        pltpu.VMEM((nlat // 4, 128), F32),
        pltpu.VMEM((nlat // 4, 128), F32),
        pltpu.VMEM((two, 128), BF),
        pltpu.VMEM((gtok, 128), BF),
        pltpu.VMEM((nrow, dw), BF),
        pltpu.SemaphoreType.DMA((17,)),
        pltpu.SemaphoreType.DMA((20,)),
        pltpu.SemaphoreType.DMA((20,)),
        pltpu.SemaphoreType.DMA((11,)),
        pltpu.SemaphoreType.DMA((11,)),
        pltpu.SemaphoreType.REGULAR,
        pltpu.SemaphoreType.REGULAR,
    ]
    tokens_out, rows_out = pl.pallas_call(
        functools.partial(kernel, nh, nc),
        out_shape=(
            jax.ShapeDtypeStruct((nrow, dw), BF),
            jax.ShapeDtypeStruct((nlat, 128), BF),
        ),
        in_specs=[hbm] * 13,
        out_specs=(hbm, hbm),
        scratch_shapes=scratch,
        compiler_params=pltpu.CompilerParams(
            collective_id=0, has_side_effects=True, vmem_limit_bytes=60 * 1024 * 1024
        ),
        name="encoder_block",
    )(
        tokens[0],
        ln_gain.reshape(1, dw),
        jnp.transpose(w_qkv, (1, 0, 2)),
        w_out,
        neighbours[0].T,
        counts,
        latents,
        lat_gain.reshape(1, dw),
        w_lat_q,
        w_lat_o,
        mlp_gain.reshape(dw // 128, 128),
        w_up,
        w_down,
    )
    tokens_out, latents_out = pl.pallas_call(
        hand_over,
        out_shape=(
            jax.ShapeDtypeStruct((nrow, dw), BF),
            jax.ShapeDtypeStruct((share, dw), BF),
        ),
        in_specs=[hbm, hbm],
        out_specs=(hbm, hbm),
        scratch_shapes=[
            pltpu.VMEM((nrow, dw), BF),
            pltpu.VMEM((nlat, 128), BF),
            pltpu.VMEM((nlat, 128), F32),
            pltpu.VMEM((share, dw), BF),
            pltpu.SemaphoreType.DMA((5,)),
            pltpu.SemaphoreType.DMA((5,)),
        ],
        compiler_params=pltpu.CompilerParams(vmem_limit_bytes=60 * 1024 * 1024),
        name="hand_over",
    )(tokens_out, rows_out)
    return (tokens_out[None], latents_out)


def solution(mesh):
    in_specs = (
        P("ctx", "heads", None),
        P(),
        P(None, None, "heads"),
        P(),
        P("ctx", None, None),
        P("ctx", None),
        P(),
        P(),
        P(None, "heads"),
        P("heads", None),
        P(),
        P(None, "ctx"),
        P("ctx", None),
    )
    out_specs = (P("ctx", "heads", None), P("heads", None))
    return jax.shard_map(
        functools.partial(per_device, mesh.shape["heads"], mesh.shape["ctx"]),
        mesh=mesh,
        in_specs=in_specs,
        out_specs=out_specs,
        check_vma=False,
    )
```
